32 devices in a mesh: wide: 8 (over y, x, core), group: 4 (over z).
Axes of the slice: x: 2, y: 2, z: 4, core: 2. Of those that a mesh axis runs over, the one named last changes fastest.
Arguments:
- inputs: bfloat16 [32, 128, 576], P(('wide', 'group')), may hold values from -6 to 6
- segments: int32 [32, 128], P(('wide', 'group')), may hold values from 0 to 5, never falling along the last dimension, each value on 1 to 64 neighbouring positions
- cotangent: bfloat16 [32, 128, 576], P(('wide', 'group')), may hold values from -6 to 6
- params: float32 [3540096], P('group')
- moment_one: float32 [3540096], P('group')
- moment_two: float32 [3540096], P('group')
Outputs:
- outputs: bfloat16 [32, 128, 576], P(('wide', 'group'))
- d_inputs: bfloat16 [32, 128, 576], P(('wide', 'group'))
- grads: float32 [3540096], P('group')
- new_params: float32 [3540096], P('group')
- new_moment_one: float32 [3540096], P('group')
- new_moment_two: float32 [3540096], P('group')
The draws below stay inside these ranges and needn't reach their ends.
All inputs are finite; a program needn't handle non-finite values.
Results may differ from the reference program's by a relative error of at most 0.023.
Values may be sent and summed in bfloat16 or wider, within the bound.
A program may use at most 128 MiB of HBM per device.

```python
import math
import jax
import jax.numpy as jnp
import numpy as np
from jax import lax

MODEL_WIDTH = 576
QUERY_HEADS = 9
KEY_VALUE_HEADS = 3
HEAD_SIZE = 64
FF = 1536
LEN = 128
SEGS = 6
SEG_MOST = 64
ROWS = 32
NPARAM = 3540096


def draw_params(key, part):
    query_key_value_width = (QUERY_HEADS + 2 * KEY_VALUE_HEADS) * HEAD_SIZE
    streams = jax.random.split(key, 6)
    query_key_value_weight = jax.random.normal(streams[0], (MODEL_WIDTH, query_key_value_width), jnp.float32) * MODEL_WIDTH ** (-0.5)
    output_weight = jax.random.normal(streams[1], (QUERY_HEADS * HEAD_SIZE, MODEL_WIDTH), jnp.float32) * (MODEL_WIDTH / 8.0) ** (-0.5)
    w_gateup = jax.random.normal(streams[2], (MODEL_WIDTH, 2 * FF), jnp.float32) * MODEL_WIDTH ** (-0.5)
    w_down = jax.random.normal(streams[3], (FF, MODEL_WIDTH), jnp.float32) * FF ** (-0.5)
    rising = jnp.exp(jnp.linspace(jnp.log(0.6), jnp.log(1.8), MODEL_WIDTH)).astype(jnp.float32)
    gain_attn = rising * jax.random.uniform(streams[4], (MODEL_WIDTH,), jnp.float32, 0.8, 1.2)
    gain_ffn = rising * jax.random.uniform(streams[5], (MODEL_WIDTH,), jnp.float32, 0.8, 1.2)
    return jnp.concatenate([query_key_value_weight.reshape(-1), output_weight.reshape(-1), w_gateup.reshape(-1), w_down.reshape(-1), gain_attn, gain_ffn]).astype(jnp.float32)


def draw_moment_one(key, part):
    value_rows = jax.random.normal(key, (NPARAM,), jnp.float32) * 0.3
    return (value_rows * NPARAM ** (-0.5)).astype(jnp.float32)


def draw_moment_two(key, part):
    value_rows = jnp.exp(jax.random.uniform(key, (NPARAM,), jnp.float32, jnp.log(0.01), jnp.log(0.1)))
    return (value_rows / NPARAM).astype(jnp.float32)


def levels(key, dims, cuts, least, top_value):
    def one(dim, parts):
        draws = jax.random.uniform(jax.random.fold_in(jax.random.fold_in(key, 6), dim), (parts,), jnp.float32, least / len(cuts), top_value / len(cuts))
        return jnp.repeat(jnp.exp(draws), dims[dim] // parts).reshape((-1,) + (1,) * (len(dims) - dim - 1))

    loudness = one(*cuts[0])
    for cut in cuts[1:]:
        loudness = loudness * one(*cut)
    return loudness


def length_profile(count, total, reach, lean):
    portions = [(1 << 20) // math.isqrt(rank ** lean) + 1 for rank in range(2, count + 1)]
    rest, counts = total - reach - (count - 1), [1] * (count - 1)
    while rest > 0:
        movable = [i for i in range(count - 1) if counts[i] < reach]
        mass, left = sum([portions[i] for i in movable]), rest
        for i in movable:
            addition = min(reach - counts[i], max(1, left * portions[i] // mass), rest)
            counts[i] = counts[i] + addition
            rest = rest - addition
    return np.array([reach] + counts)


def ragged(rng, amount, total, bound, skew):
    if amount == 2:
        one = jax.random.randint(rng, (), max(1, total - bound), min(bound, total - 1) + 1)
        return jnp.stack([one, total - one])
    tallies = jnp.asarray(length_profile(amount, total, bound, skew), jnp.int32)
    couples = (amount - 1) // 2
    source_of, sink = tallies[1:1 + 2 * couples:2], tallies[2:2 + 2 * couples:2]
    margin = jnp.minimum(source_of - 1, bound - sink)
    moved = jax.random.randint(jax.random.fold_in(rng, 1), (couples,), 0, 1 << 20) % (margin + 1)
    tallies = tallies.at[1:1 + 2 * couples:2].set(source_of - moved).at[2:2 + 2 * couples:2].set(sink + moved)
    return tallies[jax.random.permutation(jax.random.fold_in(rng, 2), amount)]


def normal_values(own_key, dims, deviation, most, shards=(), kind=jnp.bfloat16):
    level = levels(own_key, dims, shards, -0.22, 0.18) if shards else 1.0
    drawn = jax.random.normal(own_key, dims, jnp.float32) * deviation * level
    return jnp.minimum(jnp.maximum(drawn, -most), most).astype(kind)


def setup_inputs(seed: int = 0) -> dict:
    seeds = jax.random.split(jax.random.key(seed), 7)
    inputs = normal_values(seeds[0], (ROWS, LEN, MODEL_WIDTH), 1.0, 6.0, ((0, 32),))
    segments = jax.vmap(lambda own: jnp.searchsorted(jnp.cumsum(ragged(own, SEGS, LEN, SEG_MOST, 1)), jnp.arange(LEN), side="right"))(jax.random.split(seeds[1], ROWS)).reshape((ROWS, LEN)).astype(jnp.int32)
    cotangent = normal_values(seeds[2], (ROWS, LEN, MODEL_WIDTH), 1.0, 6.0, ((0, 32),))
    params = draw_params(jax.random.fold_in(seeds[6], 71), 0)
    moment_one = draw_moment_one(jax.random.fold_in(seeds[6], 71), 0)
    moment_two = draw_moment_two(jax.random.fold_in(seeds[6], 71), 0)
    return {"inputs": inputs, "segments": segments, "cotangent": cotangent, "params": params, "moment_one": moment_one, "moment_two": moment_two}


norm_eps = 1e-05
theta_base = 10000.0
masked_value = -1e+30
beta_one = 0.9
beta_two = 0.95
bias_one = 0.19
bias_two = 0.0975
learn_rate = 0.03
decay_rate = 0.1
adam_eps = 1e-08
max_norm = 1.0

def contract(pattern, left_op, right_op):
    return jnp.einsum(pattern, left_op.astype(jnp.float32), right_op.astype(jnp.float32))

def inner_rows(left_op, right_op):
    return lax.dot_general(left_op.astype(jnp.float32), right_op.astype(jnp.float32), (((0,), (0,)), ((), ())))

def outer_column_count(left_op, right_op):
    return lax.dot_general(left_op.astype(jnp.float32), right_op.astype(jnp.float32), (((1,), (1,)), ((), ())))

def unpack(flat):
    query_key_value_width = (QUERY_HEADS + 2 * KEY_VALUE_HEADS) * HEAD_SIZE
    shapes = [(MODEL_WIDTH, query_key_value_width), (QUERY_HEADS * HEAD_SIZE, MODEL_WIDTH), (MODEL_WIDTH, 2 * FF), (FF, MODEL_WIDTH), (MODEL_WIDTH,), (MODEL_WIDTH,)]
    pieces = []
    offset = 0
    for piece_shape in shapes:
        extent = math.prod(piece_shape)
        pieces.append(flat[offset:offset + extent].reshape(piece_shape))
        offset += extent
    return pieces

def positions_of(segment_row):
    index_row = jnp.arange(segment_row.shape[0], dtype=jnp.int32)
    previous = jnp.concatenate([segment_row[:1] - 1, segment_row[:-1]])
    starts = jnp.where(segment_row != previous, index_row, jnp.zeros_like(index_row))
    return index_row - lax.cummax(starts, axis=0)

def rope_tables(positions):
    half_size = HEAD_SIZE // 2
    freqs = theta_base ** (-2.0 * jnp.arange(half_size, dtype=jnp.float32) / HEAD_SIZE)
    angles = positions.astype(jnp.float32)[:, None] * freqs[None, :]
    return (jnp.cos(angles)[:, None, :], jnp.sin(angles)[:, None, :])

def apply_rotation(vectors, cosine_lookup, sine_lookup):
    half_size = HEAD_SIZE // 2
    first_half = vectors[..., :half_size]
    second_half = vectors[..., half_size:]
    return jnp.concatenate([first_half * cosine_lookup - second_half * sine_lookup, second_half * cosine_lookup + first_half * sine_lookup], axis=-1)

def unrotate(vectors, cosine_lookup, sine_lookup):
    half_size = HEAD_SIZE // 2
    first_half = vectors[..., :half_size]
    second_half = vectors[..., half_size:]
    return jnp.concatenate([first_half * cosine_lookup + second_half * sine_lookup, second_half * cosine_lookup - first_half * sine_lookup], axis=-1)

def norm_back(d_hidden, normed, inverse, gain):
    d_normed = d_hidden * gain
    return inverse * (d_normed - normed * lax.optimization_barrier(jnp.mean(d_normed * normed, axis=-1, keepdims=True)))

def layer_row(inputs, segment_row, cotangent, weights):
    query_key_value_weight, output_weight, w_gateup, w_down, gain_attn, gain_ffn = weights
    sequence_length = inputs.shape[0]
    repeat_count = QUERY_HEADS // KEY_VALUE_HEADS
    scale_factor = HEAD_SIZE ** (-0.5)
    gain_one = gain_attn.astype(jnp.float32)
    gain_two = gain_ffn.astype(jnp.float32)
    resid_in = inputs.astype(jnp.float32)
    inv_attn = lax.rsqrt(lax.optimization_barrier(jnp.mean(resid_in * resid_in, axis=-1, keepdims=True)) + norm_eps)
    normed_attn = resid_in * inv_attn
    hidden_attn = (normed_attn * gain_one).astype(jnp.bfloat16)
    projected_output = jnp.dot(hidden_attn, query_key_value_weight, preferred_element_type=jnp.float32)
    cosine_lookup, sine_lookup = rope_tables(positions_of(segment_row))
    query_rows = projected_output[:, :QUERY_HEADS * HEAD_SIZE].reshape(sequence_length, QUERY_HEADS, HEAD_SIZE)
    key_matrix = projected_output[:, QUERY_HEADS * HEAD_SIZE:(QUERY_HEADS + KEY_VALUE_HEADS) * HEAD_SIZE].reshape(sequence_length, KEY_VALUE_HEADS, HEAD_SIZE)
    query_rows_rotated = apply_rotation(query_rows, cosine_lookup, sine_lookup).astype(jnp.bfloat16).reshape(sequence_length, KEY_VALUE_HEADS, repeat_count, HEAD_SIZE)
    keys_rot = apply_rotation(key_matrix, cosine_lookup, sine_lookup).astype(jnp.bfloat16)
    value_rows = projected_output[:, (QUERY_HEADS + KEY_VALUE_HEADS) * HEAD_SIZE:].reshape(sequence_length, KEY_VALUE_HEADS, HEAD_SIZE).astype(jnp.bfloat16)
    index_row = jnp.arange(sequence_length)
    allowed = (segment_row[:, None] == segment_row[None, :]) & (index_row[:, None] >= index_row[None, :])
    scores = contract('qgrd,kgd->grqk', query_rows_rotated, keys_rot) * scale_factor
    scores = jnp.where(allowed, scores, masked_value)
    peak = lax.optimization_barrier(jnp.max(scores, axis=-1, keepdims=True))
    log_total = peak + jnp.log(lax.optimization_barrier(jnp.sum(jnp.exp(scores - peak), axis=-1, keepdims=True)))
    probs = jnp.exp(scores - log_total)
    probs_b = probs.astype(jnp.bfloat16)
    attended = contract('grqk,kgd->qgrd', probs_b, value_rows).astype(jnp.bfloat16).reshape(sequence_length, QUERY_HEADS * HEAD_SIZE)
    mid = resid_in + jnp.dot(attended, output_weight, preferred_element_type=jnp.float32)
    inv_ffn = lax.rsqrt(lax.optimization_barrier(jnp.mean(mid * mid, axis=-1, keepdims=True)) + norm_eps)
    normed_ffn = mid * inv_ffn
    hidden_ffn = (normed_ffn * gain_two).astype(jnp.bfloat16)
    gate_up = jnp.dot(hidden_ffn, w_gateup, preferred_element_type=jnp.float32)
    gate_pre = gate_up[:, :FF]
    upper = gate_up[:, FF:]
    sigmoid_gate = jax.nn.sigmoid(gate_pre)
    activation = (gate_pre * sigmoid_gate * upper).astype(jnp.bfloat16)
    outputs = (mid + jnp.dot(activation, w_down, preferred_element_type=jnp.float32)).astype(jnp.bfloat16)
    grad_down = inner_rows(activation, cotangent)
    d_act = outer_column_count(cotangent, w_down)
    d_gate = d_act * upper * sigmoid_gate * (1.0 + gate_pre * (1.0 - sigmoid_gate))
    d_upper = d_act * gate_pre * sigmoid_gate
    d_gate_up = jnp.concatenate([d_gate, d_upper], axis=-1).astype(jnp.bfloat16)
    grad_gateup = inner_rows(hidden_ffn, d_gate_up)
    d_hidden_ffn = outer_column_count(d_gate_up, w_gateup)
    grad_gain_ffn = lax.optimization_barrier(jnp.sum(d_hidden_ffn * normed_ffn, axis=0))
    d_mid = cotangent.astype(jnp.float32) + norm_back(d_hidden_ffn, normed_ffn, inv_ffn, gain_two)
    grad_middle_batch = d_mid.astype(jnp.bfloat16)
    grad_out = inner_rows(attended, grad_middle_batch)
    grad_attended_rows = outer_column_count(grad_middle_batch, output_weight).astype(jnp.bfloat16).reshape(sequence_length, KEY_VALUE_HEADS, repeat_count, HEAD_SIZE)
    d_probs = contract('qgrd,kgd->grqk', grad_attended_rows, value_rows)
    row_total = lax.optimization_barrier(jnp.sum(probs * d_probs, axis=-1, keepdims=True))
    d_scores = (probs * (d_probs - row_total) * scale_factor).astype(jnp.bfloat16)
    grad_query_rows = contract('grqk,kgd->qgrd', d_scores, keys_rot).reshape(sequence_length, QUERY_HEADS, HEAD_SIZE)
    grad_key_rows = contract('grqk,qgrd->kgd', d_scores, query_rows_rotated)
    grad_value_rows = contract('grqk,qgrd->kgd', probs_b, grad_attended_rows)
    grad_query_rows = unrotate(grad_query_rows, cosine_lookup, sine_lookup)
    grad_key_rows = unrotate(grad_key_rows, cosine_lookup, sine_lookup)
    grad_projected_rows = jnp.concatenate([grad_query_rows.reshape(sequence_length, QUERY_HEADS * HEAD_SIZE), grad_key_rows.reshape(sequence_length, KEY_VALUE_HEADS * HEAD_SIZE), grad_value_rows.reshape(sequence_length, KEY_VALUE_HEADS * HEAD_SIZE)], axis=-1).astype(jnp.bfloat16)
    grad_qkv = inner_rows(hidden_attn, grad_projected_rows)
    d_hidden_attn = outer_column_count(grad_projected_rows, query_key_value_weight)
    grad_gain_attn = lax.optimization_barrier(jnp.sum(d_hidden_attn * normed_attn, axis=0))
    d_inputs = (d_mid + norm_back(d_hidden_attn, normed_attn, inv_attn, gain_one)).astype(jnp.bfloat16)
    flat_grads = jnp.concatenate([grad_qkv.reshape(-1), grad_out.reshape(-1), grad_gateup.reshape(-1), grad_down.reshape(-1), grad_gain_attn, grad_gain_ffn])
    return (outputs, d_inputs, flat_grads)

def adam_update(grads, clip_factor, params, moment_one, moment_two, decay_mask):
    clipped = grads * clip_factor
    new_moment_one = beta_one * moment_one + (1.0 - beta_one) * clipped
    new_moment_two = beta_two * moment_two + (1.0 - beta_two) * clipped * clipped
    step_size = new_moment_one / bias_one / (jnp.sqrt(new_moment_two / bias_two) + adam_eps)
    decay_term = jnp.where(decay_mask, decay_rate * params, jnp.zeros_like(params))
    new_params = params - learn_rate * (step_size + decay_term)
    return (new_params, new_moment_one, new_moment_two)

def reference(inputs, segments, cotangent, params, moment_one, moment_two):
    weights = unpack(params.astype(jnp.bfloat16))
    block_rows = math.gcd(ROWS, max(1, 4096 // LEN))
    blocks = ROWS // block_rows
    inputs_blocked = inputs.reshape(blocks, block_rows, LEN, MODEL_WIDTH)
    segments_blocked = segments.reshape(blocks, block_rows, LEN)
    cotangent_blocked = cotangent.reshape(blocks, block_rows, LEN, MODEL_WIDTH)

    def row_block(running, blocked):
        outs_rows, dins_rows, grads_rows = jax.vmap(layer_row, in_axes=(0, 0, 0, None))(blocked[0], blocked[1], blocked[2], weights)
        rounded = lax.optimization_barrier(grads_rows.astype(jnp.bfloat16))
        return (running + lax.optimization_barrier(jnp.sum(rounded.astype(jnp.float32), axis=0)), (outs_rows, dins_rows))
    grads, stacked = lax.scan(row_block, jnp.zeros((NPARAM,), jnp.float32), (inputs_blocked, segments_blocked, cotangent_blocked))
    outputs = stacked[0].reshape(ROWS, LEN, MODEL_WIDTH)
    d_inputs = stacked[1].reshape(ROWS, LEN, MODEL_WIDTH)
    squares = jnp.sum(grads * grads)
    clip_factor = jnp.minimum(jnp.float32(1.0), max_norm * lax.rsqrt(squares))
    decay_mask = jnp.arange(NPARAM, dtype=jnp.int32) < NPARAM - 2 * MODEL_WIDTH
    new_params, new_moment_one, new_moment_two = adam_update(grads, clip_factor, params, moment_one, moment_two, decay_mask)
    return (outputs, d_inputs, grads, new_params, new_moment_one, new_moment_two)
```

```python
import functools
import math

import jax
import jax.numpy as jnp
from jax import lax
from jax.experimental import pallas as pl
from jax.experimental.pallas import tpu as pltpu
from jax.sharding import PartitionSpec as P

MESH = pl.DeviceIdType.MESH
LANES = 128

MODEL_WIDTH = 576
QUERY_HEADS = 9
KEY_VALUE_HEADS = 3
HEAD_SIZE = 64
FF = 1536


norm_eps = 1e-05
theta_base = 10000.0
masked_value = -1e30
beta_one = 0.9
beta_two = 0.95
bias_one = 0.19
bias_two = 0.0975
learn_rate = 0.03
decay_rate = 0.1
adam_eps = 1e-08
max_norm = 1.0


def contract(pattern, left_op, right_op):
    return jnp.einsum(pattern, left_op, right_op, preferred_element_type=jnp.float32)


def inner_rows(left_op, right_op):
    return lax.dot_general(
        left_op, right_op, (((0,), (0,)), ((), ())), preferred_element_type=jnp.float32
    )


def outer_column_count(left_op, right_op):
    return lax.dot_general(
        left_op, right_op, (((1,), (1,)), ((), ())), preferred_element_type=jnp.float32
    )


def unpack(main, gains):
    query_key_value_width = (QUERY_HEADS + 2 * KEY_VALUE_HEADS) * HEAD_SIZE
    shapes = [
        (MODEL_WIDTH, query_key_value_width),
        (QUERY_HEADS * HEAD_SIZE, MODEL_WIDTH),
        (MODEL_WIDTH, 2 * FF),
        (FF, MODEL_WIDTH),
    ]
    pieces = []
    offset = 0
    for piece_shape in shapes:
        extent = math.prod(piece_shape) // LANES
        pieces.append(main[offset : offset + extent].reshape(piece_shape))
        offset += extent
    return pieces + [gains[:MODEL_WIDTH], gains[MODEL_WIDTH:]]


def positions_of(segment_row):
    index_row = jnp.arange(segment_row.shape[0], dtype=jnp.int32)
    same = segment_row[:, None] == segment_row[None, :]
    before = index_row[:, None] > index_row[None, :]
    return jnp.sum((same & before).astype(jnp.int32), axis=1)


def rope_tables(positions):
    half_size = HEAD_SIZE // 2
    freqs = theta_base ** (-2.0 * jnp.arange(half_size, dtype=jnp.float32) / HEAD_SIZE)
    angles = positions.astype(jnp.float32)[:, None] * freqs[None, :]
    return (jnp.cos(angles)[:, None, :], jnp.sin(angles)[:, None, :])


def apply_rotation(vectors, cosine_lookup, sine_lookup):
    half_size = HEAD_SIZE // 2
    first_half = vectors[..., :half_size]
    second_half = vectors[..., half_size:]
    return jnp.concatenate(
        [
            first_half * cosine_lookup - second_half * sine_lookup,
            second_half * cosine_lookup + first_half * sine_lookup,
        ],
        axis=-1,
    )


def unrotate(vectors, cosine_lookup, sine_lookup):
    half_size = HEAD_SIZE // 2
    first_half = vectors[..., :half_size]
    second_half = vectors[..., half_size:]
    return jnp.concatenate(
        [
            first_half * cosine_lookup + second_half * sine_lookup,
            second_half * cosine_lookup - first_half * sine_lookup,
        ],
        axis=-1,
    )


def norm_back(d_hidden, normed, inverse, gain):
    d_normed = d_hidden * gain
    return inverse * (d_normed - normed * jnp.mean(d_normed * normed, axis=-1, keepdims=True))


def layer_row(inputs, segment_row, cotangent, weights):
    query_key_value_weight, output_weight, w_gateup, w_down, gain_attn, gain_ffn = weights
    sequence_length = inputs.shape[0]
    repeat_count = QUERY_HEADS // KEY_VALUE_HEADS
    scale_factor = HEAD_SIZE ** (-0.5)
    gain_one = gain_attn.astype(jnp.float32)
    gain_two = gain_ffn.astype(jnp.float32)
    resid_in = inputs.astype(jnp.float32)
    inv_attn = lax.rsqrt(jnp.mean(resid_in * resid_in, axis=-1, keepdims=True) + norm_eps)
    normed_attn = resid_in * inv_attn
    hidden_attn = (normed_attn * gain_one).astype(jnp.bfloat16)
    projected_output = jnp.dot(
        hidden_attn, query_key_value_weight, preferred_element_type=jnp.float32
    )
    cosine_lookup, sine_lookup = rope_tables(positions_of(segment_row))
    query_rows = projected_output[:, : QUERY_HEADS * HEAD_SIZE].reshape(
        sequence_length, QUERY_HEADS, HEAD_SIZE
    )
    key_matrix = projected_output[
        :, QUERY_HEADS * HEAD_SIZE : (QUERY_HEADS + KEY_VALUE_HEADS) * HEAD_SIZE
    ].reshape(sequence_length, KEY_VALUE_HEADS, HEAD_SIZE)
    query_rows_rotated = (
        apply_rotation(query_rows, cosine_lookup, sine_lookup)
        .astype(jnp.bfloat16)
        .reshape(sequence_length, KEY_VALUE_HEADS, repeat_count, HEAD_SIZE)
    )
    keys_rot = apply_rotation(key_matrix, cosine_lookup, sine_lookup).astype(jnp.bfloat16)
    value_rows = (
        projected_output[:, (QUERY_HEADS + KEY_VALUE_HEADS) * HEAD_SIZE :]
        .reshape(sequence_length, KEY_VALUE_HEADS, HEAD_SIZE)
        .astype(jnp.bfloat16)
    )
    index_row = jnp.arange(sequence_length)
    allowed = (segment_row[:, None] == segment_row[None, :]) & (
        index_row[:, None] >= index_row[None, :]
    )
    scores = contract("qgrd,kgd->grqk", query_rows_rotated, keys_rot) * scale_factor
    scores = jnp.where(allowed, scores, masked_value)
    peak = jnp.max(scores, axis=-1, keepdims=True)
    log_total = peak + jnp.log(jnp.sum(jnp.exp(scores - peak), axis=-1, keepdims=True))
    probs_b = jnp.exp(scores - log_total).astype(jnp.bfloat16)
    attended = (
        contract("grqk,kgd->qgrd", probs_b, value_rows)
        .astype(jnp.bfloat16)
        .reshape(sequence_length, QUERY_HEADS * HEAD_SIZE)
    )
    mid = resid_in + jnp.dot(attended, output_weight, preferred_element_type=jnp.float32)
    inv_ffn = lax.rsqrt(jnp.mean(mid * mid, axis=-1, keepdims=True) + norm_eps)
    normed_ffn = mid * inv_ffn
    hidden_ffn = (normed_ffn * gain_two).astype(jnp.bfloat16)
    gate_up = jnp.dot(hidden_ffn, w_gateup, preferred_element_type=jnp.float32)
    gate_pre = gate_up[:, :FF]
    upper = gate_up[:, FF:]
    sigmoid_gate = jax.nn.sigmoid(gate_pre)
    activation = (gate_pre * sigmoid_gate * upper).astype(jnp.bfloat16)
    outputs = (mid + jnp.dot(activation, w_down, preferred_element_type=jnp.float32)).astype(
        jnp.bfloat16
    )
    grad_down = inner_rows(activation, cotangent)
    d_act = outer_column_count(cotangent, w_down)
    d_gate = d_act * upper * sigmoid_gate * (1.0 + gate_pre * (1.0 - sigmoid_gate))
    d_upper = d_act * gate_pre * sigmoid_gate
    d_gate_up = jnp.concatenate([d_gate, d_upper], axis=-1).astype(jnp.bfloat16)
    grad_gateup = inner_rows(hidden_ffn, d_gate_up)
    d_hidden_ffn = outer_column_count(d_gate_up, w_gateup)
    grad_gain_ffn = jnp.sum(d_hidden_ffn * normed_ffn, axis=0)
    d_mid = cotangent.astype(jnp.float32) + norm_back(d_hidden_ffn, normed_ffn, inv_ffn, gain_two)
    grad_middle_batch = d_mid.astype(jnp.bfloat16)
    grad_out = inner_rows(attended, grad_middle_batch)
    grad_attended_rows = (
        outer_column_count(grad_middle_batch, output_weight)
        .astype(jnp.bfloat16)
        .reshape(sequence_length, KEY_VALUE_HEADS, repeat_count, HEAD_SIZE)
    )
    recomputed = contract("qgrd,kgd->grqk", query_rows_rotated, keys_rot) * scale_factor
    probs = jnp.exp(jnp.where(allowed, recomputed, masked_value) - log_total)
    d_probs = contract("qgrd,kgd->grqk", grad_attended_rows, value_rows)
    row_total = jnp.sum(probs * d_probs, axis=-1, keepdims=True)
    d_scores = (probs * (d_probs - row_total) * scale_factor).astype(jnp.bfloat16)
    grad_query_rows = contract("grqk,kgd->qgrd", d_scores, keys_rot).reshape(
        sequence_length, QUERY_HEADS, HEAD_SIZE
    )
    grad_key_rows = contract("grqk,qgrd->kgd", d_scores, query_rows_rotated)
    grad_value_rows = contract("grqk,qgrd->kgd", probs_b, grad_attended_rows)
    grad_query_rows = unrotate(grad_query_rows, cosine_lookup, sine_lookup)
    grad_key_rows = unrotate(grad_key_rows, cosine_lookup, sine_lookup)
    grad_projected_rows = jnp.concatenate(
        [
            grad_query_rows.reshape(sequence_length, QUERY_HEADS * HEAD_SIZE),
            grad_key_rows.reshape(sequence_length, KEY_VALUE_HEADS * HEAD_SIZE),
            grad_value_rows.reshape(sequence_length, KEY_VALUE_HEADS * HEAD_SIZE),
        ],
        axis=-1,
    ).astype(jnp.bfloat16)
    grad_qkv = inner_rows(hidden_attn, grad_projected_rows)
    d_hidden_attn = outer_column_count(grad_projected_rows, query_key_value_weight)
    grad_gain_attn = jnp.sum(d_hidden_attn * normed_attn, axis=0)
    d_inputs = (d_mid + norm_back(d_hidden_attn, normed_attn, inv_attn, gain_one)).astype(
        jnp.bfloat16
    )
    matrices = [grad_qkv, grad_out, grad_gateup, grad_down]
    main = jnp.concatenate([m.astype(jnp.bfloat16).reshape(-1, LANES) for m in matrices])
    gains = jnp.concatenate([grad_gain_attn, grad_gain_ffn])
    return (outputs, d_inputs, main, gains)


def adam_update(grads, clip_factor, params, moment_one, moment_two, decay_mask):
    clipped = grads * clip_factor
    new_moment_one = beta_one * moment_one + (1.0 - beta_one) * clipped
    new_moment_two = beta_two * moment_two + (1.0 - beta_two) * clipped * clipped
    step_size = new_moment_one / bias_one / (jnp.sqrt(new_moment_two / bias_two) + adam_eps)
    decay_term = jnp.where(decay_mask, decay_rate * params, jnp.zeros_like(params))
    new_params = params - learn_rate * (step_size + decay_term)
    return (new_params, new_moment_one, new_moment_two)


def my_bits(wide, count):
    return [(wide // 2**b) % 2 for b in range(count)]


def flipped(wide, bit, b):
    return wide + (1 - 2 * bit) * 2**b


def greet(wide, group, bits, groups):
    barrier = pltpu.get_barrier_semaphore()
    peers = [(flipped(wide, bit, b), group) for b, bit in enumerate(bits)]
    peers += [(wide, (group + d) % groups) for d in range(1, groups)]
    for peer in peers:
        pl.semaphore_signal(barrier, inc=1, device_id=peer, device_id_type=MESH)
    pl.semaphore_wait(barrier, len(peers))


def send(src, dst, send_sem, recv_sem, peer):
    copy = pltpu.make_async_remote_copy(
        src_ref=src,
        dst_ref=dst,
        send_sem=send_sem,
        recv_sem=recv_sem,
        device_id=peer,
        device_id_type=MESH,
    )
    copy.start()
    return copy


def bit_order(chunk, count):
    rest = list(range(1, count))
    return [0] + (rest if chunk % 2 == 0 else rest[::-1])


def tails_kernel(groups, bits_count, tail_ref, out_ref, send_sem, recv_sem):
    wide, group = lax.axis_index("wide"), lax.axis_index("group")
    greet(wide, group, [], groups)
    out_ref[pl.ds(group, 1)] = tail_ref[...][None]
    copies = []
    for d in range(1, groups):
        copies.append(
            send(
                tail_ref,
                out_ref.at[group],
                send_sem.at[d - 1],
                recv_sem.at[d - 1],
                (wide, (group + d) % groups),
            )
        )
    for copy in copies:
        copy.wait()


def gather_kernel(groups, count, chunks, block_ref, out_ref, own_sem, zs, zr, ws, wr):
    wide, group = lax.axis_index("wide"), lax.axis_index("group")
    bits = my_bits(wide, count)
    step = block_ref.shape[-2] // chunks
    greet(wide, group, bits, groups)

    def place(ref, lead, open_bits, chunk):
        index = [slice(None) if b in open_bits else bits[b] for b in reversed(range(count))]
        return ref.at[tuple(lead + index + [pl.ds(chunk * step, step)])]

    def copy(src, dst, send_sem, recv_sem, peer):
        return pltpu.make_async_remote_copy(
            src_ref=src,
            dst_ref=dst,
            send_sem=send_sem,
            recv_sem=recv_sem,
            device_id=peer,
            device_id_type=MESH,
        )

    def along(way, d, c):
        source = (group - way * (d - 1) + groups) % groups
        unit = (0 if way > 0 else groups - 1) + d - 1
        src = place(block_ref, [], [], c) if d == 1 else place(out_ref, [source], [], c)
        return copy(
            src,
            place(out_ref, [source], [], c),
            zs.at[unit, c],
            zr.at[unit, c],
            (wide, (group + way + groups) % groups),
        )

    def passes(way, d):
        ahead = group + way
        behind = group - way * (d - 1)
        return (ahead >= 0) & (ahead < groups) & (behind >= 0) & (behind < groups)

    def comes(way, d):
        behind = group - way * d
        return (behind >= 0) & (behind < groups)

    def across(way, d, c, stage):
        order = bit_order(c, count)[::-1]
        b = order[stage]
        source = (group - way * d + groups) % groups
        unit = (0 if way > 0 else groups - 1) + d - 1
        here = place(out_ref, [source], order[:stage], c)
        return copy(
            here,
            here,
            ws.at[unit, c, stage],
            wr.at[unit, c, stage],
            (flipped(wide, bits[b], b), group),
        )

    units = [(d, c) for d in range(1, groups) for c in range(chunks)]
    for c in range(chunks):
        for way in (1, -1):

            @pl.when(passes(way, 1))
            def _():
                along(way, 1, c).start()

    own = pltpu.make_async_copy(block_ref, out_ref.at[group], own_sem)
    own.start()
    for tick in range(len(units) // 2 + count + 1):
        for u, (d, c) in reversed(list(enumerate(units))):
            stage = tick - u // 2
            if not 0 <= stage <= count:
                continue
            for way in (1, -1):

                @pl.when(comes(way, d))
                def _():
                    if stage == 0:
                        along(way, d, c).wait_recv()
                    else:
                        across(way, d, c, stage - 1).wait_recv()
                    if stage < count:
                        across(way, d, c, stage).start()

                if stage == 0 and d + 1 < groups:

                    @pl.when(passes(way, d + 1))
                    def _():
                        along(way, d + 1, c).start()

    for way in (1, -1):
        for d, c in units:

            @pl.when(passes(way, d))
            def _():
                along(way, d, c).wait_send()

            @pl.when(comes(way, d))
            def _():
                for stage in range(count):
                    across(way, d, c, stage).wait_send()

    own.wait()


def sum_kernel(groups, count, chunks, x_ref, gain_ref, out_ref, head_ref, gsum_ref, sq_ref, *scratch):
    recvs, accs = scratch[:count], scratch[count : 2 * count]
    recv_z, gain_w, gain_z, sq_z, piece_head = scratch[2 * count : 2 * count + 5]
    ss, sr, zs, zr, gs, gr, xs, xr, gzs, gzr, qs, qr, hs, hr = scratch[2 * count + 5 :]
    wide, group = lax.axis_index("wide"), lax.axis_index("group")
    bits = my_bits(wide, count)
    step = x_ref.shape[-2] // chunks
    greet(wide, group, bits, groups)
    copies = {}
    f32 = jnp.float32

    def partner(b):
        return (flipped(wide, bits[b], b), group)

    def part(c, stage, value):
        order = bit_order(c, count)
        left = sorted(order[stage:], reverse=True)
        return [value if b == order[stage] else slice(None) for b in left]

    def held(c, stage):
        return x_ref if stage == 0 else accs[stage - 1].at[c]

    def view(c, stage, flip):
        b = bit_order(c, count)[stage]
        index = [slice(None)] + part(c, stage, 1 - bits[b] if flip else bits[b])
        if stage == 0:
            index += [slice(None)] * (count + 2 - len(index) - 1)
            return x_ref.at[tuple(index + [pl.ds(c * step, step)])]
        return accs[stage - 1].at[tuple([c] + index)]

    def start_scatter(c, stage):
        b = bit_order(c, count)[stage]
        copies["s", c, stage] = send(
            view(c, stage, True), recvs[stage].at[c], ss.at[c, stage], sr.at[c, stage], partner(b)
        )

    def add_scatter(c, stage):
        copies["s", c, stage].wait_recv()
        mine, other, total = view(c, stage, False), recvs[stage].at[c], accs[stage].at[c]

        def body(i, _):
            total[i] = (mine[i].astype(f32) + other[i].astype(f32)).astype(jnp.bfloat16)
            return 0

        lax.fori_loop(0, groups, body, 0)

    def start_groups(c):
        for d in range(1, groups):
            to = (group + d) % groups
            copies["z", c, d] = send(
                accs[-1].at[c, to],
                recv_z.at[c, d - 1],
                zs.at[c, d - 1],
                zr.at[c, d - 1],
                (wide, to),
            )

    def place(open_bits, c):
        index = [slice(None) if b in open_bits else bits[b] for b in reversed(range(count))]
        return out_ref.at[tuple(index + [pl.ds(c * step, step)])]

    def add_groups(c):
        total = accs[-1][c, group].astype(f32)
        for d in range(1, groups):
            copies["z", c, d].wait_recv()
            total = total + recv_z[c, d - 1].astype(f32)
        place([], c)[...] = total.astype(jnp.bfloat16)

    def start_gather(c, stage):
        order = bit_order(c, count)[::-1]
        here = place(order[:stage], c)
        copies["g", c, stage] = send(
            here, here, gs.at[c, stage], gr.at[c, stage], partner(order[stage])
        )

    for c in range(chunks):
        start_scatter(c, 0)
    gain_w[0] = gain_ref[...]
    copies["x", 0] = send(gain_w.at[0], gain_w.at[count + 1], xs.at[0], xr.at[0], partner(0))

    for tick in range(chunks // 2 + 2 * count + 1):
        for c in reversed(range(chunks)):
            s = tick - c // 2
            if 0 <= s < count:
                add_scatter(c, s)
                if s + 1 < count:
                    start_scatter(c, s + 1)
                else:
                    start_groups(c)
            elif s == count:
                add_groups(c)
                start_gather(c, 0)
            elif count < s <= 2 * count:
                copies["g", c, s - count - 1].wait_recv()
                if s < 2 * count:
                    start_gather(c, s - count)
        if tick < count:
            copies["x", tick].wait_recv()
            gain_w[tick + 1] = gain_w[tick] + gain_w[count + 1 + tick]
            if tick + 1 < count:
                copies["x", tick + 1] = send(
                    gain_w.at[tick + 1],
                    gain_w.at[count + 2 + tick],
                    xs.at[tick + 1],
                    xr.at[tick + 1],
                    partner(tick + 1),
                )
            else:
                gain_z[pl.ds(group, 1)] = gain_w[pl.ds(count, 1)]
                for d in range(1, groups):
                    copies["gz", d] = send(
                        gain_w.at[count],
                        gain_z.at[group],
                        gzs.at[d - 1],
                        gzr.at[d - 1],
                        (wide, (group + d) % groups),
                    )

    first = tuple([0] * count + [pl.ds(0, 16)])
    copies["h"] = send(out_ref.at[first], head_ref, hs, hr, (wide, (group + groups - 1) % groups))
    flat_lead = out_ref.shape[:-2]

    def squares(i, total):
        index = tuple((i // 2**b) % 2 for b in reversed(range(len(flat_lead))))
        value = out_ref[index].astype(f32)
        value = value * value
        return total + jnp.sum(value.reshape(-1, 8, LANES), axis=0)

    square = lax.fori_loop(0, math.prod(flat_lead), squares, jnp.zeros((8, LANES), f32))
    piece_head[...] = square
    sq_z[pl.ds(group, 1)] = square[None]
    for d in range(1, groups):
        copies["q", d] = send(
            piece_head, sq_z.at[group], qs.at[d - 1], qr.at[d - 1], (wide, (group + d) % groups)
        )
    for d in range(1, groups):
        copies["gz", d].wait_recv()
    gains = gain_z[0]
    for d in range(1, groups):
        gains = gains + gain_z[d]
    gains = gains.astype(jnp.bfloat16).astype(f32)
    gsum_ref[...] = gains
    for d in range(1, groups):
        copies["q", d].wait_recv()
    square = sq_z[0]
    for d in range(1, groups):
        square = square + sq_z[d]
    square = square + jnp.sum((gains * gains).reshape(-1, 8, LANES), axis=0)
    total = jnp.sum(jnp.sum(square, axis=-1, keepdims=True), axis=0, keepdims=True)
    clip = jnp.minimum(jnp.float32(1.0), max_norm * lax.rsqrt(total))
    sq_ref[...] = jnp.broadcast_to(clip, sq_ref.shape)
    copies["h"].wait_recv()
    for copy in copies.values():
        copy.wait_send()


def params_of(identity):
    return pltpu.CompilerParams(
        collective_id=identity, has_side_effects=True, vmem_limit_bytes=60 * 2**20
    )


def vmem_specs(n):
    return [pl.BlockSpec(memory_space=pltpu.VMEM)] * n


def gather_tails(tail, groups, identity):
    dma = pltpu.SemaphoreType.DMA
    return pl.pallas_call(
        functools.partial(tails_kernel, groups, 0),
        out_shape=jax.ShapeDtypeStruct((groups,) + tail.shape, tail.dtype),
        in_specs=vmem_specs(1),
        out_specs=vmem_specs(1)[0],
        scratch_shapes=[dma((groups - 1,)), dma((groups - 1,))],
        compiler_params=params_of(identity),
        name="tails",
    )(tail)


def gather_blocks(block, groups, count, chunks):
    dma = pltpu.SemaphoreType.DMA
    units = 2 * (groups - 1)
    return pl.pallas_call(
        functools.partial(gather_kernel, groups, count, chunks),
        out_shape=jax.ShapeDtypeStruct((groups,) + block.shape, block.dtype),
        in_specs=vmem_specs(1),
        out_specs=vmem_specs(1)[0],
        scratch_shapes=[
            dma,
            dma((units, chunks)),
            dma((units, chunks)),
            dma((units, chunks, count)),
            dma((units, chunks, count)),
        ],
        compiler_params=params_of(1),
        name="gather_weights",
    )(block)


def sum_blocks(main, gains, groups, count, chunks):
    dma = pltpu.SemaphoreType.DMA
    rows = main.shape[-2]
    step = rows // chunks
    bf16, f32 = jnp.bfloat16, jnp.float32
    stages = [
        pltpu.VMEM((chunks, groups) + (2,) * (count - 1 - k) + (step, LANES), bf16)
        for k in range(count)
    ]
    return pl.pallas_call(
        functools.partial(sum_kernel, groups, count, chunks),
        out_shape=(
            jax.ShapeDtypeStruct((2,) * count + (rows, LANES), bf16),
            jax.ShapeDtypeStruct((16, LANES), bf16),
            jax.ShapeDtypeStruct(gains.shape, f32),
            jax.ShapeDtypeStruct((8, LANES), f32),
        ),
        in_specs=vmem_specs(2),
        out_specs=tuple(vmem_specs(4)),
        scratch_shapes=stages
        + stages
        + [
            pltpu.VMEM((chunks, groups - 1, step, LANES), bf16),
            pltpu.VMEM((2 * count + 1,) + gains.shape, f32),
            pltpu.VMEM((groups,) + gains.shape, f32),
            pltpu.VMEM((groups, 8, LANES), f32),
            pltpu.VMEM((8, LANES), f32),
        ]
        + [dma((chunks, count))] * 2
        + [dma((chunks, groups - 1))] * 2
        + [dma((chunks, count))] * 2
        + [dma((count,))] * 2
        + [dma((groups - 1,))] * 4
        + [dma, dma],
        compiler_params=params_of(2),
        name="sum_grads",
    )(main, gains)


def dot(left_op, right_op, left_dim, right_dim):
    return lax.dot_general(
        left_op,
        right_op,
        (((left_dim,), (right_dim,)), ((), ())),
        preferred_element_type=jnp.float32,
    )


def cores_of(wide):
    core, x_bit, y_bit = wide % 2, (wide // 2) % 2, (wide // 4) % 2
    over_x, over_y = wide + (1 - 2 * x_bit) * 2, wide + (1 - 2 * y_bit) * 4
    one = over_x * (1 - core) + over_y * core
    two = over_y * (1 - core) + over_x * core
    far = over_x + over_y - wide
    twin = wide + 1 - 2 * core
    return core, over_x, over_y, far, one, two, twin


def greet_all(peers):
    barrier = pltpu.get_barrier_semaphore()
    for peer in peers:
        pl.semaphore_signal(barrier, inc=1, device_id=peer, device_id_type=MESH)
    pl.semaphore_wait(barrier, len(peers))


def remote(src, dst, send_sem, recv_sem, peer):
    return pltpu.make_async_remote_copy(
        src_ref=src,
        dst_ref=dst,
        send_sem=send_sem,
        recv_sem=recv_sem,
        device_id=peer,
        device_id_type=MESH,
    )


QKV = (QUERY_HEADS + 2 * KEY_VALUE_HEADS) * HEAD_SIZE
INNER = QUERY_HEADS * HEAD_SIZE
JOINT = QKV + INNER
HALF_JOINT = JOINT // 2
CHIPS = 4
CHIP_ROWS = MODEL_WIDTH // CHIPS
UNITS = FF // CHIPS
HALF_WIDTH = MODEL_WIDTH // 2
SPLIT = 3
SUB = CHIP_ROWS // SPLIT
BLOCK = MODEL_WIDTH * FF
BLOCK_ROWS = BLOCK // LANES
EXTRA = 2 * MODEL_WIDTH // 4
HEAD_ROWS = 8


def lanes_of(rows):
    return lax.broadcasted_iota(jnp.int32, (rows, LANES), 1)


def rows_at(ref, at, count, kept=0):
    if kept:
        value = ref[pl.ds(at * LANES, kept)]
        value = jnp.concatenate([value, jnp.zeros((count * LANES - kept,), value.dtype)])
    else:
        value = ref[pl.ds(pl.multiple_of(at * LANES, 1024), count * LANES)]
    return value.reshape(count, LANES)


def spread_kernel(
    groups, params_ref, joint_ref, gu_ref, down_ref, gain_ref,
    flat, lin, tail_s, gain_s, pan,
    load_sem, ts, tr, gs, gr, zs, zr, as_, ar, es, er,
):
    f32, bf16 = jnp.float32, jnp.bfloat16
    wide, group = lax.axis_index("wide"), lax.axis_index("group")
    core, over_x, over_y, far, one, two, twin = cores_of(wide)
    chip = wide // 2
    load = pltpu.make_async_copy(params_ref, lin, load_sem)
    load.start()
    peers = [(p, group) for p in (over_x, over_y, twin)]
    peers += [(wide, (group + d) % groups) for d in range(1, groups)]
    greet_all(peers)
    load.wait()
    flat[pl.ds(HEAD_ROWS + BLOCK_ROWS, 8), :] = rows_at(lin, BLOCK_ROWS, 8, EXTRA)
    copy_rows = 288

    def unroll(i, _):
        at = pl.multiple_of(i * copy_rows, 8)
        flat[pl.ds(HEAD_ROWS + at, copy_rows), :] = rows_at(lin, at, copy_rows)
        return 0

    lax.fori_loop(0, BLOCK_ROWS // copy_rows, unroll, 0)

    def joined(first, second, shift, cut):
        lane = lanes_of(first.shape[0])
        return jnp.where(lane < cut, pltpu.roll(first, shift, 1), pltpu.roll(second, shift, 1))

    tail = remote(tail_s, flat.at[pl.ds(0, HEAD_ROWS)], ts, tr, (wide, (group + 1) % groups))
    top = HEAD_ROWS + BLOCK_ROWS + 2

    @pl.when(group < groups - 1)
    def _():
        at = top - HEAD_ROWS
        tail_s[...] = joined(flat[at : at + 8, :], flat[at + 1 : at + 9, :], 96, 96)
        tail.start()

    def gain_copy(g):
        return remote(gain_s, gain_s, gs.at[g], gr, (wide, g))

    @pl.when(group == groups - 1)
    def _():
        at = top - 9
        gain_s[...] = joined(flat[at : at + 16, :], flat[at + 1 : at + 17, :], 96, 96)
        for g in range(groups - 1):
            gain_copy(g).start()

    @pl.when(group > 0)
    def _():
        tail.wait_recv()

    def take(start, count, stride):
        return flat[pl.ds(start, count, stride), :]

    pairs = CHIP_ROWS // 2

    def put_joint(p, even, odd):
        pan[pl.ds(p % 6 * CHIP_ROWS, pairs, 2), :] = even
        pan[pl.ds(p % 6 * CHIP_ROWS + 1, pairs, 2), :] = odd
        joint_ref[pl.ds(pl.multiple_of(CHIP_ROWS * chip, 16), CHIP_ROWS), p * LANES : (p + 1) * LANES] = pan[
            p % 6 * CHIP_ROWS : (p % 6 + 1) * CHIP_ROWS, :
        ].astype(bf16)

    qkv_at = HEAD_ROWS + 1080 * chip
    out_at = HEAD_ROWS + 4320 + 648 * chip

    def qkv(k):
        return take(qkv_at + k, pairs, 15)

    def out(k):
        return take(out_at + k, pairs, 9)

    @pl.when((group == 0) & (core == 0))
    def _():
        for p in range(6):
            put_joint(p, qkv(p), joined(qkv(7 + p), qkv(8 + p), 64, 64))

    @pl.when((group == 0) & (core == 1))
    def _():
        put_joint(6, qkv(6), joined(qkv(13), qkv(14), 64, 64))
        lane = lanes_of(pairs)
        put_joint(
            7,
            jnp.where(lane < 64, qkv(7), pltpu.roll(out(0), 64, 1)),
            jnp.where(lane < 64, pltpu.roll(qkv(14), 64, 1), out(4)),
        )
        for k in range(4):
            put_joint(8 + k, joined(out(k), out(k + 1), 64, 64), out(5 + k))

    for g, back, shift in ((1, 3, 32), (2, 5, 64)):

        @pl.when(group == g)
        def _():
            for j in range(3):
                at = HEAD_ROWS - back + 12 * core + 3 * chip + j
                value = joined(take(at, HALF_WIDTH, 24), take(at + 1, HALF_WIDTH, 24), shift, shift)
                gu_ref[core, (g - 1) * HALF_WIDTH : g * HALF_WIDTH, j * LANES : (j + 1) * LANES] = value.astype(bf16)

    half_units = UNITS // 2

    @pl.when(group == 3)
    def _():
        rows = pl.ds(pl.multiple_of(half_units * core, 16), half_units)
        count = half_units // 2
        for p in range(5):
            at = HEAD_ROWS + 864 * wide + p
            even = joined(take(at - 7, count, 9), take(at - 6, count, 9), 96, 96)
            odd = joined(take(at - 3, count, 9), take(at - 2, count, 9), 32, 32)
            pan[pl.ds(p * half_units, count, 2), :] = even
            pan[pl.ds(p * half_units + 1, count, 2), :] = odd
            value = pan[p * half_units : (p + 1) * half_units, :].astype(bf16)
            if p < 4:
                down_ref[rows, p * LANES : (p + 1) * LANES] = value
            else:
                down_ref[rows, p * LANES : MODEL_WIDTH] = value[:, : MODEL_WIDTH - p * LANES]

    def attn_at(q, c, k):
        return joint_ref.at[
            pl.ds(pl.multiple_of(CHIP_ROWS * q + SUB * k, 16), SUB),
            pl.ds(pl.multiple_of(HALF_JOINT * c, LANES), HALF_JOINT),
        ]

    def piece(s, k):
        if s == 0:
            return attn_at(chip, core, k)
        if s < 3:
            step = HALF_WIDTH // SPLIT
            return gu_ref.at[core, pl.ds((s - 1) * HALF_WIDTH + k * step, step)]
        step = half_units // SPLIT
        return down_ref.at[pl.ds(pl.multiple_of(half_units * core + k * step, 16), step)]

    def pass_on(s, k, way):
        to = (wide, (group + way + groups) % groups)
        return remote(piece(s, k), piece(s, k), zs.at[(way + 1) // 2, s, k], zr.at[s, k], to)

    def sends(s):
        right = (group >= s) & (group < groups - 1)
        left = (group <= s) & (group > 0)
        return right, left

    def forward(s, k):
        right, left = sends(s)

        @pl.when(right)
        def _():
            pass_on(s, k, 1).start()

        @pl.when(left)
        def _():
            pass_on(s, k, -1).start()

    def give(s, k):
        return remote(piece(s, k), piece(s, k), es.at[s, k], er.at[s, k], (twin, group))

    for s in range(groups):

        @pl.when(group == s)
        def _():
            for k in range(SPLIT):
                forward(s, k)
                if s:
                    give(s, k).start()

    q_one, q_two = one // 2, two // 2
    q_far = 3 - chip

    def stage(n, k, q):
        peer = (one, two, two, twin, twin, twin, twin)[n]
        return remote(attn_at(q, core, k), attn_at(q, core, k), as_.at[n, k], ar.at[n, k], (peer, group))

    for k in range(SPLIT):

        @pl.when(group > 0)
        def _():
            pass_on(0, k, 1).wait_recv()
            forward(0, k)

        stage(0, k, chip).start()
        stage(1, k, chip).start()
        stage(3, k, chip).start()

    def relay(distance):
        for s in range(1, groups):
            for side in (-distance, distance):

                @pl.when(group - s == side)
                def _():
                    for k in range(SPLIT):
                        pass_on(s, k, 1).wait_recv()
                        forward(s, k)
                        give(s, k).start()

    relay(1)
    for k in range(SPLIT):
        stage(0, k, q_one).wait_recv()
        stage(2, k, q_one).start()
        stage(4, k, q_one).start()
    relay(2)
    for k in range(SPLIT):
        stage(1, k, q_two).wait_recv()
        stage(5, k, q_two).start()
    for k in range(SPLIT):
        stage(2, k, q_far).wait_recv()
        stage(6, k, q_far).start()
    relay(3)

    @pl.when(group < groups - 1)
    def _():
        gain_copy(0).wait_recv()

    gains = gain_s[...].astype(bf16).astype(f32)
    for k in range(4):
        gain_ref[0:1, k * LANES : (k + 1) * LANES] = gains[k : k + 1]
    gain_ref[0:1, 4 * LANES : MODEL_WIDTH] = gains[4:5, : MODEL_WIDTH - 4 * LANES]
    turned = pltpu.roll(gains, 64, 1)
    lane = lanes_of(1)
    for k in range(4):
        gain_ref[1:2, k * LANES : (k + 1) * LANES] = jnp.where(lane < 64, turned[4 + k : 5 + k], turned[5 + k : 6 + k])
    gain_ref[1:2, 4 * LANES : MODEL_WIDTH] = turned[8:9, : MODEL_WIDTH - 4 * LANES]

    for k in range(SPLIT):
        for n in range(3, 7):
            stage(n, k, chip).wait_recv()
        for s in range(1, groups):
            give(s, k).wait_recv()
    for k in range(SPLIT):
        for s in range(1, groups):
            give(s, k).wait_send()
        for n in range(7):
            stage(n, k, chip).wait_send()
    for s in range(groups):
        right, left = sends(s)
        for k in range(SPLIT):

            @pl.when(right)
            def _():
                pass_on(s, k, 1).wait_send()

            @pl.when(left)
            def _():
                pass_on(s, k, -1).wait_send()

    @pl.when(group < groups - 1)
    def _():
        tail.wait_send()

    @pl.when(group == groups - 1)
    def _():
        for g in range(groups - 1):
            gain_copy(g).wait_send()


def spread(params, groups):
    dma = pltpu.SemaphoreType.DMA
    f32, bf16 = jnp.float32, jnp.bfloat16
    return pl.pallas_call(
        functools.partial(spread_kernel, groups),
        out_shape=(
            jax.ShapeDtypeStruct((MODEL_WIDTH, JOINT), bf16),
            jax.ShapeDtypeStruct((2, MODEL_WIDTH, UNITS), bf16),
            jax.ShapeDtypeStruct((UNITS, MODEL_WIDTH), bf16),
            jax.ShapeDtypeStruct((2, MODEL_WIDTH), f32),
        ),
        in_specs=[pl.BlockSpec(memory_space=pl.ANY)],
        out_specs=tuple(vmem_specs(4)),
        scratch_shapes=[
            pltpu.VMEM((HEAD_ROWS + BLOCK_ROWS + 24, LANES), f32),
            pltpu.VMEM(params.shape, f32),
            pltpu.VMEM((8, LANES), f32),
            pltpu.VMEM((16, LANES), f32),
            pltpu.VMEM((5 * UNITS // 2, LANES), f32),
            dma, dma, dma,
            dma((groups - 1,)), dma,
            dma((2, groups, SPLIT)), dma((groups, SPLIT)),
            dma((7, SPLIT)), dma((7, SPLIT)),
            dma((groups, SPLIT)), dma((groups, SPLIT)),
        ],
        compiler_params=params_of(4),
        name="spread",
    )(params)


def plane_kernel(
    x_ref, seg_ref, cot_ref, joint_ref, gu_ref, down_ref, gain_ref, freq_ref,
    out_ref, din_ref, gj_ref, ggu_ref, gdn_ref, gg_ref,
    proj_s, att_s, mid_s, dmid_s, dproj_s, cots, hids, act_s, gate_s, up_s,
    part_s, part_r, cs, cr, hs, hr, ps, pr,
):
    f32, bf16 = jnp.float32, jnp.bfloat16
    wide, group = lax.axis_index("wide"), lax.axis_index("group")
    core, over_x, over_y, far, one, two, twin = cores_of(wide)
    width, length, half = MODEL_WIDTH, x_ref.shape[1], HEAD_SIZE // 2
    heads, kv = QUERY_HEADS, KEY_VALUE_HEADS
    repeat = heads // kv
    scale = HEAD_SIZE**-0.5
    peers = [(p, group) for p in (over_x, over_y, far)]
    greet_all(peers)

    def block(ref, j):
        return ref.at[pl.ds(j * length, length)]

    cots[0:length, :] = cot_ref[...].astype(f32).T.astype(bf16)
    cot_copies = [
        remote(block(cots, 0), block(cots, j + 1), cs.at[j], cr.at[j], peers[j]) for j in range(3)
    ]
    for copy in cot_copies:
        copy.start()

    gain_one, gain_two = gain_ref[0:1, :], gain_ref[1:2, :]
    x = x_ref[...].astype(f32).T
    inv_attn = lax.rsqrt(jnp.mean(x * x, axis=-1, keepdims=True) + norm_eps)
    normed_attn = x * inv_attn
    hidden_attn = (normed_attn * gain_one).astype(bf16)

    seg_row = jnp.broadcast_to(seg_ref[...].astype(f32), (length, length))
    rows = lax.broadcasted_iota(jnp.int32, (length, length), 0)
    columns = lax.broadcasted_iota(jnp.int32, (length, length), 1)
    allowed = (seg_row == seg_row.T) & (rows >= columns)
    positions = jnp.sum(jnp.where(allowed, 1.0, 0.0), axis=-1, keepdims=True) - 1.0
    angles = positions * freq_ref[...]
    lane = lax.broadcasted_iota(jnp.int32, (length, LANES), 1)
    first = lane % HEAD_SIZE < half
    cosine, sine = jnp.cos(angles), jnp.sin(angles)
    sine = jnp.where(first, -sine, sine)

    def swap(u):
        return jnp.where(first, pltpu.roll(u, LANES - half, 1), pltpu.roll(u, half, 1))

    panels = 8
    turned_panels = (heads + kv) * HEAD_SIZE // LANES
    wide_qkv = panels * LANES
    for p in range(0, panels, 2):
        both = dot(hidden_attn, joint_ref[:, p * LANES : (p + 2) * LANES], 1, 0)
        for q in (p, p + 1):
            u = both[:, (q - p) * LANES : (q - p + 1) * LANES]
            if q < turned_panels:
                u = u * cosine + swap(u) * sine
            proj_s[:, q * LANES : (q + 1) * LANES] = u.astype(bf16)

    def slot(s):
        return proj_s[:, s * HEAD_SIZE : (s + 1) * HEAD_SIZE]

    mask = jnp.concatenate([allowed] * repeat, axis=0)
    saved = []
    for j in range(kv):
        queries = jnp.concatenate([slot(repeat * j + r) for r in range(repeat)], axis=0)
        keys, values = slot(heads + j), slot(heads + kv + j)
        scores = jnp.where(mask, dot(queries, keys, 1, 1) * scale, masked_value)
        peak = jnp.max(scores, axis=-1, keepdims=True)
        total = jnp.sum(jnp.exp(scores - peak), axis=-1, keepdims=True)
        probs = jnp.exp(scores - (peak + jnp.log(total)))
        probs_b = probs.astype(bf16)
        attended = dot(probs_b, values, 1, 0)
        for r in range(repeat):
            at = (repeat * j + r) * HEAD_SIZE
            att_s[:, at : at + HEAD_SIZE] = attended[r * length : (r + 1) * length].astype(bf16)
        saved.append((queries, keys, values, probs, probs_b))

    out_from = QKV // LANES * LANES
    shift = QKV - out_from
    w_out = joint_ref.at[:, out_from:JOINT]
    mid = x + dot(att_s[...], w_out[...], 1, 0)[:, shift:]
    inv_ffn = lax.rsqrt(jnp.mean(mid * mid, axis=-1, keepdims=True) + norm_eps)
    normed_ffn = mid * inv_ffn
    hids[0:length, :] = (normed_ffn * gain_two).astype(bf16)
    hid_copies = [
        remote(block(hids, 0), block(hids, j + 1), hs.at[j], hr.at[j], peers[j]) for j in range(3)
    ]
    for copy in hid_copies:
        copy.start()
    mid_s[...] = mid

    def feed(j):
        at = slice(j * length, (j + 1) * length)
        hidden, cotangent = hids[at, :], cots[at, :]
        gate, upper = dot(hidden, gu_ref[0], 1, 0), dot(hidden, gu_ref[1], 1, 0)
        d_act = dot(cotangent, down_ref[...], 1, 1)
        sigmoid = jax.nn.sigmoid(gate)
        activation = (gate * sigmoid * upper).astype(bf16)
        d_gate = (d_act * upper * sigmoid * (1.0 + gate * (1.0 - sigmoid))).astype(bf16)
        d_upper = (d_act * gate * sigmoid).astype(bf16)
        act_s[at, :], gate_s[at, :], up_s[at, :] = activation, d_gate, d_upper
        d_hidden = dot(d_gate, gu_ref[0], 1, 1) + dot(d_upper, gu_ref[1], 1, 1)
        return d_hidden, dot(activation, down_ref[...], 1, 0)

    def part_copy(n, j):
        return remote(part_s.at[n, j], part_r.at[n, j], ps.at[n, j], pr.at[n, j], peers[j])

    d_hidden, out_own = feed(0)
    for j in range(3):
        cot_copies[j].wait_recv()
        hid_copies[j].wait_recv()
        d_part, out_part = feed(j + 1)
        part_s[0, j] = d_part.astype(bf16)
        part_copy(0, j).start()
        part_s[1, j] = out_part.astype(bf16)
        part_copy(1, j).start()

    ggu_ref[0] = dot(hids[...], gate_s[...], 0, 0).astype(bf16)
    ggu_ref[1] = dot(hids[...], up_s[...], 0, 0).astype(bf16)
    gdn_ref[...] = dot(act_s[...], cots[...], 0, 0).astype(bf16)

    for j in range(3):
        part_copy(0, j).wait_recv()
        d_hidden = d_hidden + part_r[0, j].astype(f32)
    mid = mid_s[...]
    normed_ffn = mid * inv_ffn
    gain_ffn = jnp.sum(d_hidden * normed_ffn, axis=0, keepdims=True)
    d_mid = cots[0:length, :].astype(f32) + norm_back(d_hidden, normed_ffn, inv_ffn, gain_two)
    dmid_s[...] = jnp.zeros_like(dmid_s)
    dmid_s[:, shift:] = d_mid.astype(bf16)
    d_attended = dot(dmid_s[...], w_out[...], 1, 1)
    grad_out = dot(att_s[...], dmid_s[...], 0, 0)
    gj_ref[:, out_from + LANES : JOINT] = grad_out[:, LANES:].astype(bf16)
    edge = grad_out[:, :LANES]
    att_s[...] = d_attended.astype(bf16)

    dproj_s[...] = jnp.zeros_like(dproj_s)
    for j in range(kv):
        queries, keys, values, probs, probs_b = saved[j]
        d_att = jnp.concatenate(
            [
                att_s[:, (repeat * j + r) * HEAD_SIZE : (repeat * j + r + 1) * HEAD_SIZE]
                for r in range(repeat)
            ],
            axis=0,
        )
        d_probs = dot(d_att, values, 1, 1)
        row_total = jnp.sum(probs * d_probs, axis=-1, keepdims=True)
        d_scores = (probs * (d_probs - row_total) * scale).astype(bf16)
        d_queries = dot(d_scores, keys, 1, 0)
        for r in range(repeat):
            at = (repeat * j + r) * HEAD_SIZE
            dproj_s[:, at : at + HEAD_SIZE] = d_queries[r * length : (r + 1) * length]
        at = (heads + j) * HEAD_SIZE
        dproj_s[:, at : at + HEAD_SIZE] = dot(d_scores, queries, 0, 0)
        at = (heads + kv + j) * HEAD_SIZE
        dproj_s[:, at : at + HEAD_SIZE] = dot(probs_b, d_att, 0, 0)

    for p in range(panels):
        raw = dproj_s[:, p * LANES : (p + 1) * LANES]
        if p < turned_panels:
            raw = raw * cosine - swap(raw) * sine
        proj_s[:, p * LANES : (p + 1) * LANES] = raw.astype(bf16)
    d_hidden = dot(proj_s[...], joint_ref[:, :wide_qkv], 1, 1)
    grad_qkv = dot(hidden_attn, proj_s[...], 0, 0)
    gj_ref[:, :out_from] = grad_qkv[:, :out_from].astype(bf16)
    gj_ref[:, out_from:wide_qkv] = (grad_qkv[:, out_from:] + edge).astype(bf16)
    gain_attn = jnp.sum(d_hidden * normed_attn, axis=0, keepdims=True)
    din_ref[...] = (d_mid + norm_back(d_hidden, normed_attn, inv_attn, gain_one)).T.astype(bf16)
    both = jnp.concatenate([gain_attn, gain_ffn], axis=1)
    gg_ref[...] = jnp.zeros_like(gg_ref)
    for k in range(2 * width // LANES):
        gg_ref[k : k + 1, :] = both[:, k * LANES : (k + 1) * LANES].astype(bf16).astype(f32)

    outputs = mid + out_own
    for j in range(3):
        part_copy(1, j).wait_recv()
        outputs = outputs + part_r[1, j].astype(f32)
    out_ref[...] = outputs.T.astype(bf16)
    for j in range(3):
        cot_copies[j].wait_send()
        hid_copies[j].wait_send()
        part_copy(0, j).wait_send()
        part_copy(1, j).wait_send()


def plane_layer(inputs, segment_row, cotangent, joint, gu, down, gains):
    length = inputs.shape[0]
    half = HEAD_SIZE // 2
    f32, bf16 = jnp.float32, jnp.bfloat16
    dma = pltpu.SemaphoreType.DMA
    freqs = theta_base ** (-2.0 * jnp.arange(half, dtype=f32) / HEAD_SIZE)
    freqs = jnp.tile(freqs, LANES // half)[None]
    full = (length, MODEL_WIDTH)
    panel_lanes = 8 * LANES
    four = (CHIPS * length, MODEL_WIDTH)
    units = (CHIPS * length, UNITS)
    outputs, d_inputs, *grads = pl.pallas_call(
        plane_kernel,
        out_shape=(
            jax.ShapeDtypeStruct(full[::-1], bf16),
            jax.ShapeDtypeStruct(full[::-1], bf16),
            jax.ShapeDtypeStruct(joint.shape, bf16),
            jax.ShapeDtypeStruct(gu.shape, bf16),
            jax.ShapeDtypeStruct(down.shape, bf16),
            jax.ShapeDtypeStruct((16, LANES), f32),
        ),
        in_specs=vmem_specs(8),
        out_specs=tuple(vmem_specs(6)),
        scratch_shapes=[
            pltpu.VMEM((length, panel_lanes), bf16),
            pltpu.VMEM(full, bf16),
            pltpu.VMEM(full, f32),
            pltpu.VMEM((length, JOINT - QKV // LANES * LANES), bf16),
            pltpu.VMEM((length, panel_lanes), f32),
            pltpu.VMEM(four, bf16),
            pltpu.VMEM(four, bf16),
            pltpu.VMEM(units, bf16),
            pltpu.VMEM(units, bf16),
            pltpu.VMEM(units, bf16),
            pltpu.VMEM((2, 3) + full, bf16),
            pltpu.VMEM((2, 3) + full, bf16),
            dma((3,)), dma((3,)), dma((3,)), dma((3,)), dma((2, 3)), dma((2, 3)),
        ],
        compiler_params=params_of(5),
        name="plane_layer",
    )(inputs.T, segment_row[None], cotangent.T, joint, gu, down, gains, freqs)
    return (outputs, d_inputs, *grads)


ADAM_CHUNKS = 8
ADAM_ROWS = BLOCK_ROWS // ADAM_CHUNKS
ADAM_STEP = 96
PIECE_ROWS = BLOCK_ROWS // 8


def settle_kernel(
    groups, gj_ref, ggu_ref, gdn_ref, gain_ref, params_ref, one_ref, two_ref,
    flat, clip_ref, par_b, one_b, two_b,
    core_j, core_g, core_d, acc_j, acc_g, acc_d, rs_one, rs_two, z_j, z_g, z_d, ag,
    note, note_z, pan,
    load_sem, cs, cr, r1s, r1r, r2s, r2r, zs, zr, gs, gr, ns, nr, nzs, nzr, hs, hr,
):
    f32, bf16 = jnp.float32, jnp.bfloat16
    wide, group = lax.axis_index("wide"), lax.axis_index("group")
    core, over_x, over_y, far, one, two, twin = cores_of(wide)
    chip = wide // 2
    q_one, q_two, q_far = one // 2, two // 2, 3 - chip

    loads = [
        pltpu.make_async_copy(source, bank, load_sem.at[i])
        for i, (source, bank) in enumerate(
            ((params_ref, par_b), (one_ref, one_b), (two_ref, two_b))
        )
    ]
    peers = [(p, group) for p in (over_x, over_y, twin)]
    peers += [(wide, (group + d) % groups) for d in range(1, groups)]
    greet_all(peers)

    half_units = UNITS // 2
    other = 1 - core

    def half_cols(c):
        return pl.ds(pl.multiple_of(HALF_JOINT * c, LANES), HALF_JOINT)

    def half_rows(c):
        return pl.ds(pl.multiple_of(half_units * c, 16), half_units)

    def chip_rows(q):
        return pl.ds(pl.multiple_of(CHIP_ROWS * q, 16), CHIP_ROWS)

    swaps = [
        remote(ggu_ref.at[other], core_g, cs.at[0], cr.at[0], (twin, group)),
        remote(gdn_ref.at[half_rows(other)], core_d, cs.at[1], cr.at[1], (twin, group)),
        remote(gj_ref.at[:, half_cols(other)], core_j, cs.at[2], cr.at[2], (twin, group)),
    ]
    for swap in swaps:
        swap.start()
    for load in loads:
        load.start()

    def add_rows(count, step, total, mine, theirs):
        def body(i, _):
            at = pl.ds(pl.multiple_of(i * step, 16), step)
            total(at, mine(at).astype(f32) + theirs(at).astype(f32))
            return 0

        lax.fori_loop(0, count // step, body, 0)

    def into(ref):
        def put(at, value):
            ref[at, :] = value.astype(bf16)

        return put

    def z_source(g):
        if g == 0:
            return acc_j.at[chip_rows(chip)], z_j
        if g < 3:
            return acc_g.at[pl.ds((g - 1) * HALF_WIDTH, HALF_WIDTH)], z_g
        return acc_d, z_d

    def z_copy(g):
        source, target = z_source(g)
        place = (group - g + groups) % groups
        at = (place + groups - 1) % groups
        return remote(source, target.at[at], zs.at[g], zr.at[at], (wide, g))

    def z_send(g):
        @pl.when(group != g)
        def _():
            z_copy(g).start()

    swaps[0].wait_recv()
    add_rows(MODEL_WIDTH, 48, into(acc_g), lambda at: ggu_ref[core, at, :], lambda at: core_g[at, :])
    z_send(1)
    z_send(2)
    swaps[1].wait_recv()
    half_from = half_units * core

    def down_mine(at):
        return gdn_ref[pl.ds(pl.multiple_of(half_from + at.start, 16), at.size), :]

    add_rows(half_units, 48, into(acc_d), down_mine, lambda at: core_d[at, :])
    z_send(3)
    swaps[2].wait_recv()

    add_rows(MODEL_WIDTH, 16, into(acc_j), lambda at: gj_ref[at, half_cols(core)], lambda at: core_j[at, :])

    def rs_copy(i):
        q = (q_one, q_far)[i]
        return remote(acc_j.at[chip_rows(q)], rs_one.at[i], r1s.at[i], r1r.at[i], (one, group))

    rs_copy(1).start()
    rs_copy(0).start()

    def add_piece(q, theirs):
        def body(i, _):
            at = pl.ds(pl.multiple_of(CHIP_ROWS * q + i * 16, 16), 16)
            value = acc_j[at, :].astype(f32) + theirs[pl.ds(pl.multiple_of(i * 16, 16), 16), :].astype(f32)
            acc_j[at, :] = value.astype(bf16)
            return 0

        lax.fori_loop(0, CHIP_ROWS // 16, body, 0)

    rs_copy(1).wait_recv()
    add_piece(q_two, rs_one.at[1])
    rs_last = remote(acc_j.at[chip_rows(q_two)], rs_two, r2s, r2r, (two, group))
    rs_last.start()
    rs_copy(0).wait_recv()
    add_piece(chip, rs_one.at[0])
    rs_last.wait_recv()
    add_piece(chip, rs_two)
    z_send(0)

    def z_wait(i):
        source, target = z_source(0)
        return target, zr.at[i]

    note[0, 0:16, :] = gain_ref[...]

    def squares(value):
        return jnp.sum((value * value).reshape(-1, 8, LANES), axis=0)

    def z_total(g, rows, widths):
        source, target = z_source(g)
        for at in range(groups - 1):
            remote(source, target.at[at], zs.at[g], zr.at[at], (wide, g)).wait_recv()
        step = 16
        panels = -(-widths // LANES)

        def body(i, total):
            at = pl.ds(pl.multiple_of(i * step, 16), step)
            value = source[at, :].astype(f32)
            for d in range(groups - 1):
                value = value + target[d, at, :].astype(f32)
            value = value.astype(bf16)
            for p in range(widths // LANES):
                part = value[:, p * LANES : (p + 1) * LANES]
                ag[wide, pl.ds(pl.multiple_of(p * rows + i * step, 16), step), :] = part
                total = total + squares(part.astype(f32))
            if widths % LANES:
                part = value[:, widths // LANES * LANES :]
                half_s[pl.ds(pl.multiple_of(i * step, 16), step), 0 : LANES // 2] = part
                part = part.astype(f32)
                total = total + jnp.concatenate([squares_half(part), jnp.zeros((8, LANES // 2), f32)], axis=1)
            return total

        def squares_half(part):
            return (part * part)[:8] + (part * part)[8:]

        half_s = None
        if widths % LANES:
            half_s = pan_b
        note[0, 16:24, :] = lax.fori_loop(0, rows // step, body, jnp.zeros((8, LANES), f32))
        if widths % LANES:
            n = rows // 2
            low, high = half_s[0:n, 0 : LANES // 2], half_s[n:rows, 0 : LANES // 2]
            ag[wide, panels * rows - rows : panels * rows - n, :] = jnp.concatenate([low, high], axis=1)

    pan_b = core_d

    @pl.when(group == 0)
    def _():
        z_total(0, CHIP_ROWS, HALF_JOINT)

    @pl.when((group == 1))
    def _():
        z_total(1, HALF_WIDTH, UNITS)

    @pl.when((group == 2))
    def _():
        z_total(2, HALF_WIDTH, UNITS)

    @pl.when(group == 3)
    def _():
        z_total(3, half_units, MODEL_WIDTH)

    def note_copy(n):
        return remote(note.at[n], note.at[n + 4], ns.at[n], nr.at[n], ((one, two, twin)[n], group))

    def ag_copy(n):
        peer = (one, two, two, twin, twin, twin, twin)[n]
        q = (chip, chip, q_one, chip, q_one, q_two, q_far)[n]
        here = ag.at[2 * q + core]
        return remote(here, here, gs.at[n], gr.at[n], (peer, group))

    def note_step(n):
        note_copy(n).wait_recv()
        note[n + 1] = note[n] + note[n + 4]
        if n < 2:
            note_copy(n + 1).start()

    note_copy(0).start()
    for n in (0, 1, 3):
        ag_copy(n).start()
    note_step(0)
    ag_copy(0).wait_recv()
    ag_copy(2).start()
    ag_copy(4).start()
    note_step(1)
    ag_copy(1).wait_recv()
    ag_copy(5).start()
    note_step(2)
    note_z[pl.ds(group, 1)] = note[3:4]

    def note_far(d):
        return remote(
            note.at[3], note_z.at[group], nzs.at[d - 1], nzr.at[d - 1], (wide, (group + d) % groups)
        )

    for d in range(1, groups):
        note_far(d).start()

    pairs = CHIP_ROWS // 2
    lane_pairs = lanes_of(pairs)

    def halves(first, second):
        lane = lanes_of(first.shape[0])
        return jnp.where(lane < 64, pltpu.roll(first, 64, 1), pltpu.roll(second, 64, 1))

    def lay_joint(q):
        for p in range(12):
            at = p % 6 * CHIP_ROWS
            pan[p * CHIP_ROWS : (p + 1) * CHIP_ROWS, :] = ag[2 * q + p // 6, at : at + CHIP_ROWS, :].astype(f32)

        def even(p):
            return pan[pl.ds(p * CHIP_ROWS, pairs, 2), :]

        def odd(p):
            return pan[pl.ds(p * CHIP_ROWS + 1, pairs, 2), :]

        def put_qkv(k, value):
            flat[pl.ds(1080 * q + k, pairs, 15), :] = value

        def put_out(k, value):
            flat[pl.ds(4320 + 648 * q + k, pairs, 9), :] = value

        for p in range(7):
            put_qkv(p, even(p))
            put_qkv(8 + p, halves(odd(p), odd(p + 1)))
        put_qkv(7, jnp.where(lane_pairs < 64, even(7), pltpu.roll(odd(0), 64, 1)))
        for k in range(4):
            put_out(k, halves(even(7 + k), even(8 + k)))
            put_out(5 + k, odd(8 + k))
        put_out(4, jnp.where(lane_pairs < 64, pltpu.roll(even(11), 64, 1), odd(7)))

    def lay_gateup(q):
        for c in range(2):
            for j in range(3):
                value = ag[2 * q + c, j * HALF_WIDTH : (j + 1) * HALF_WIDTH, :].astype(f32)
                flat[pl.ds(12 * c + 3 * q + j, HALF_WIDTH, 24), :] = value

    def lay_down(q):
        n = half_units
        for c in range(2):
            w = 2 * q + c
            pan[0 : 4 * n, :] = ag[w, 0 : 4 * n, :].astype(f32)
            packed = ag[w, 4 * n : 4 * n + n // 2, :].astype(f32)
            pan[4 * n : 4 * n + n // 2, :] = packed
            pan[4 * n + n // 2 : 5 * n, :] = pltpu.roll(packed, 64, 1)

            def even(p):
                return pan[pl.ds(p * n, n // 2, 2), :]

            def odd(p):
                return pan[pl.ds(p * n + 1, n // 2, 2), :]

            def put(k, value):
                flat[pl.ds(864 * w + k, n // 2, 9), :] = value

            for p in range(4):
                put(p, even(p))
                put(5 + p, halves(odd(p), odd(p + 1)))
            put(4, jnp.where(lanes_of(n // 2) < 64, even(4), pltpu.roll(odd(0), 64, 1)))

    def lay(q):
        @pl.when(group == 0)
        def _():
            lay_joint(q)

        @pl.when((group == 1) | (group == 2))
        def _():
            lay_gateup(q)

        @pl.when(group == 3)
        def _():
            lay_down(q)

    ag_copy(3).wait_recv()
    lay(chip)
    ag_copy(2).wait_recv()
    ag_copy(6).start()
    ag_copy(4).wait_recv()
    lay(q_two)
    ag_copy(5).wait_recv()
    lay(q_one)
    ag_copy(6).wait_recv()
    lay(q_far)

    head = remote(
        flat.at[pl.ds(0, HEAD_ROWS)],
        flat.at[pl.ds(BLOCK_ROWS, HEAD_ROWS)],
        hs,
        hr,
        (wide, (group + groups - 1) % groups),
    )

    @pl.when(group > 0)
    def _():
        head.start()

    for d in range(1, groups):
        note_far(d).wait_recv()
    total = note_z[0]
    for d in range(1, groups):
        total = total + note_z[d]
    gains = total[:16]
    square = total[16:24] + squares(gains)
    square = jnp.sum(jnp.sum(square, axis=-1, keepdims=True), axis=0, keepdims=True)
    clip = jnp.minimum(jnp.float32(1.0), max_norm * lax.rsqrt(square))

    @pl.when(group == groups - 1)
    def _():
        flat[pl.ds(BLOCK_ROWS, 16), :] = gains

    clip_ref[...] = jnp.broadcast_to(clip, clip_ref.shape)

    @pl.when(group < groups - 1)
    def _():
        head.wait_recv()

    for load in loads:
        load.wait()
    for swap in swaps:
        swap.wait_send()
    for i in range(2):
        rs_copy(i).wait_send()
    rs_last.wait_send()
    for g in range(groups):

        @pl.when(group != g)
        def _():
            z_copy(g).wait_send()

    for n in range(7):
        ag_copy(n).wait_send()
    for n in range(3):
        note_copy(n).wait_send()
    for d in range(1, groups):
        note_far(d).wait_send()

    @pl.when(group > 0)
    def _():
        head.wait_send()


def adam_kernel(
    groups, flat, clip_ref, par_i, one_i, two_i, layer_out, layer_din,
    grads_out, params_out, one_out, two_out, out_ref, din_ref,
    grad_b, par_b, one_b, two_b, grad_t, par_t, one_t, two_t, out_sem, tout_sem, layer_sem,
):
    group = lax.axis_index("group")
    copies = [
        pltpu.make_async_copy(layer_out, out_ref, layer_sem.at[0]),
        pltpu.make_async_copy(layer_din, din_ref, layer_sem.at[1]),
    ]
    for copy in copies:
        copy.start()
    clip = clip_ref[0:1, 0:1]
    old = (par_i, one_i, two_i)

    def update(g, at, count, kept=0):
        lane = lanes_of(count)
        back, cut = 9 * g // 4, LANES - 32 * g
        grads = flat[pl.ds(at + back, count), :]
        if g:
            second = flat[pl.ds(at + back + 1, count), :]
            grads = jnp.where(lane < cut, pltpu.roll(grads, cut, 1), pltpu.roll(second, cut, 1))
        p, m1, m2 = [rows_at(ref, at, count, kept) for ref in old]
        clipped = grads * clip
        m1 = beta_one * m1 + (1.0 - beta_one) * clipped
        m2 = beta_two * m2 + (1.0 - beta_two) * clipped * clipped
        step_size = m1 * (1.0 / bias_one) / (jnp.sqrt(m2 * (1.0 / bias_two)) + adam_eps)
        if g == groups - 1:
            limit = BLOCK + EXTRA - 2 * MODEL_WIDTH
            place = (at + lax.broadcasted_iota(jnp.int32, (count, LANES), 0)) * LANES + lane
            decay = jnp.where(place < limit, decay_rate, 0.0)
        else:
            decay = decay_rate
        return grads, p - learn_rate * (step_size + decay * p), m1, m2

    outs = (grads_out, params_out, one_out, two_out)
    stores = (grad_b, par_b, one_b, two_b)
    ends = (grad_t, par_t, one_t, two_t)

    def out_copy(i, j):
        at = i * ADAM_ROWS
        return pltpu.make_async_copy(
            stores[j].at[pl.ds(at, ADAM_ROWS)].reshape(ADAM_ROWS * LANES),
            outs[j].at[pl.ds(at * LANES, ADAM_ROWS * LANES)],
            out_sem.at[i, j],
        )

    def tail_copy(j):
        return pltpu.make_async_copy(
            ends[j], outs[j].at[pl.ds(BLOCK, EXTRA)], tout_sem.at[j]
        )

    for i in range(ADAM_CHUNKS):
        for g in range(groups):

            @pl.when(group == g)
            def _():
                def body(k, _):
                    at = pl.multiple_of(i * ADAM_ROWS + k * ADAM_STEP, 8)
                    for store, value in zip(stores, update(g, at, ADAM_STEP)):
                        store[pl.ds(at, ADAM_STEP), :] = value
                    return 0

                lax.fori_loop(0, ADAM_ROWS // ADAM_STEP, body, 0)

        for j in range(4):
            out_copy(i, j).start()
    for g in range(groups):

        @pl.when(group == g)
        def _():
            for store, value in zip(ends, update(g, BLOCK_ROWS, 8, EXTRA)):
                store[...] = value.reshape(8 * LANES)[:EXTRA]

    for j in range(4):
        tail_copy(j).start()

    for i in range(ADAM_CHUNKS):
        for j in range(4):
            out_copy(i, j).wait()
    for j in range(4):
        tail_copy(j).wait()
    for copy in copies:
        copy.wait()


def settle(gj, ggu, gdn, gains, params, moment_one, moment_two, groups):
    dma = pltpu.SemaphoreType.DMA
    f32, bf16 = jnp.float32, jnp.bfloat16
    half_units = UNITS // 2
    z = groups - 1
    bank = jax.ShapeDtypeStruct(params.shape, f32)
    shapes = (
        jax.ShapeDtypeStruct((BLOCK_ROWS + 24, LANES), f32),
        jax.ShapeDtypeStruct((8, LANES), f32),
        bank, bank, bank,
    )
    return pl.pallas_call(
        functools.partial(settle_kernel, groups),
        out_shape=shapes,
        in_specs=vmem_specs(4) + [pl.BlockSpec(memory_space=pl.ANY)] * 3,
        out_specs=tuple(vmem_specs(5)),
        scratch_shapes=[
            pltpu.VMEM((MODEL_WIDTH, HALF_JOINT), bf16),
            pltpu.VMEM((MODEL_WIDTH, UNITS), bf16),
            pltpu.VMEM((half_units, MODEL_WIDTH), bf16),
            pltpu.VMEM((MODEL_WIDTH, HALF_JOINT), bf16),
            pltpu.VMEM((MODEL_WIDTH, UNITS), bf16),
            pltpu.VMEM((half_units, MODEL_WIDTH), bf16),
            pltpu.VMEM((2, CHIP_ROWS, HALF_JOINT), bf16),
            pltpu.VMEM((CHIP_ROWS, HALF_JOINT), bf16),
            pltpu.VMEM((z, CHIP_ROWS, HALF_JOINT), bf16),
            pltpu.VMEM((z, HALF_WIDTH, UNITS), bf16),
            pltpu.VMEM((z, half_units, MODEL_WIDTH), bf16),
            pltpu.VMEM((8, PIECE_ROWS, LANES), bf16),
            pltpu.VMEM((7, 24, LANES), f32),
            pltpu.VMEM((groups, 24, LANES), f32),
            pltpu.VMEM((12 * CHIP_ROWS, LANES), f32),

            dma((3,)), dma((3,)), dma((3,)), dma((2,)), dma((2,)), dma, dma,
            dma((groups,)), dma((z,)), dma((7,)), dma((7,)), dma((3,)), dma((3,)), dma((z,)), dma((z,)),
            dma, dma,
        ],
        compiler_params=params_of(6),
        name="settle",
    )(gj, ggu, gdn, gains, params, moment_one, moment_two)


def adam(settled, outputs, d_inputs, groups, share_len):
    dma = pltpu.SemaphoreType.DMA
    f32 = jnp.float32
    bank = pltpu.VMEM((BLOCK_ROWS, LANES), f32)
    end = pltpu.VMEM((EXTRA,), f32)
    return pl.pallas_call(
        functools.partial(adam_kernel, groups),
        out_shape=(jax.ShapeDtypeStruct((share_len,), f32),) * 4
        + tuple(jax.ShapeDtypeStruct(a.shape, a.dtype) for a in (outputs, d_inputs)),
        in_specs=vmem_specs(7),
        out_specs=tuple([pl.BlockSpec(memory_space=pl.ANY)] * 6),
        scratch_shapes=[bank] * 4 + [end] * 4 + [dma((ADAM_CHUNKS, 4)), dma((4,)), dma((2,))],
        compiler_params=pltpu.CompilerParams(vmem_limit_bytes=60 * 2**20),
        name="adam",
    )(*settled, outputs, d_inputs)


def on_device(inputs, segments, cotangent, params, moment_one, moment_two):
    groups = lax.axis_size("group")
    wides = lax.axis_size("wide")
    group = lax.axis_index("group")
    count = wides.bit_length() - 1
    share_len = params.shape[0]
    gain_len = 2 * MODEL_WIDTH
    extra = gain_len // groups
    block_len = share_len - extra
    if groups == 4 and wides == 2 * CHIPS and block_len == BLOCK and inputs.shape[0] == 1:
        joint, gu, down, gains = spread(params, groups)
        outputs, d_inputs, *grads = plane_layer(
            inputs[0], segments[0], cotangent[0], joint, gu, down, gains
        )
        settled = settle(*grads, params, moment_one, moment_two, groups)
        *updated, outputs, d_inputs = adam(settled, outputs, d_inputs, groups, share_len)
        return (outputs.T[None], d_inputs.T[None], *updated)
    block_rows = block_len // LANES
    piece_rows = -(-block_rows // wides)
    chunks = 6 if piece_rows % 96 == 0 else 2
    piece_rows = -(-piece_rows // (16 * chunks)) * 16 * chunks
    padding = piece_rows * wides - block_rows
    lead = (2,) * count

    def to_pieces(rows):
        rows = rows.reshape(-1, block_rows, LANES)
        if padding:
            rows = jnp.pad(rows, ((0, 0), (0, padding), (0, 0)))
        return rows.reshape((-1,) + lead + (piece_rows, LANES))

    def from_pieces(pieces):
        rows = pieces.reshape(-1, piece_rows * wides, LANES)[:, :block_rows]
        return rows.reshape(-1, LANES)

    rounded = params.astype(jnp.bfloat16)
    tail = jnp.pad(rounded[share_len - gain_len :], (0, 16 * LANES - gain_len)).reshape(16, LANES)
    tails = gather_tails(tail, groups, 0).reshape(groups, -1)[:, :gain_len]
    before = lax.dynamic_index_in_dim(tails, (group + groups - 1) % groups, keepdims=False)
    joined = jnp.concatenate([before, rounded])
    block = lax.dynamic_slice(joined, (gain_len - extra * group,), (block_len,))
    flat_gains = tails[groups - 1]
    gathered = gather_blocks(to_pieces(block)[0], groups, count, chunks)
    weights = unpack(from_pieces(gathered), flat_gains)
    outputs, d_inputs, main, gains = layer_row(inputs[0], segments[0], cotangent[0], weights)
    gains = gains.astype(jnp.bfloat16).astype(jnp.float32)
    gains = jnp.pad(gains, (0, 16 * LANES - gain_len)).reshape(16, LANES)
    summed_block, head, gains, square = sum_blocks(to_pieces(main), gains, groups, count, chunks)
    gains = gains.reshape(-1)[:gain_len].astype(jnp.bfloat16)
    flat_block = from_pieces(summed_block).reshape(-1)
    head = head.reshape(-1)[:gain_len]
    head = jnp.where(group == groups - 1, gains, head)
    joined = jnp.concatenate([flat_block, head])
    summed = lax.dynamic_slice(joined, (extra * group,), (share_len,)).astype(jnp.float32)
    clip_factor = square[0, 0]
    flat_index = group * share_len + jnp.arange(share_len, dtype=jnp.int32)
    decay_mask = flat_index < share_len * groups - gain_len
    new_params, new_moment_one, new_moment_two = adam_update(
        summed, clip_factor, params, moment_one, moment_two, decay_mask
    )
    return (outputs[None], d_inputs[None], summed, new_params, new_moment_one, new_moment_two)


def solution(mesh):
    return jax.shard_map(
        on_device,
        mesh=mesh,
        in_specs=(
            P(("wide", "group"), None, None),
            P(("wide", "group"), None),
            P(("wide", "group"), None, None),
            P("group"),
            P("group"),
            P("group"),
        ),
        out_specs=(
            P(("wide", "group"), None, None),
            P(("wide", "group"), None, None),
            P("group"),
            P("group"),
            P("group"),
            P("group"),
        ),
        check_vma=False,
    )
```

```python
import functools
import math

import jax
import jax.numpy as jnp
from jax import lax
from jax.experimental import pallas as pl
from jax.experimental.pallas import tpu as pltpu
from jax.sharding import PartitionSpec as P

MESH = pl.DeviceIdType.MESH
LANES = 128

MODEL_WIDTH = 576
QUERY_HEADS = 9
KEY_VALUE_HEADS = 3
HEAD_SIZE = 64
FF = 1536


norm_eps = 1e-05
theta_base = 10000.0
masked_value = -1e30
beta_one = 0.9
beta_two = 0.95
bias_one = 0.19
bias_two = 0.0975
learn_rate = 0.03
decay_rate = 0.1
adam_eps = 1e-08
max_norm = 1.0


def contract(pattern, left_op, right_op):
    return jnp.einsum(pattern, left_op, right_op, preferred_element_type=jnp.float32)


def inner_rows(left_op, right_op):
    return lax.dot_general(
        left_op, right_op, (((0,), (0,)), ((), ())), preferred_element_type=jnp.float32
    )


def outer_column_count(left_op, right_op):
    return lax.dot_general(
        left_op, right_op, (((1,), (1,)), ((), ())), preferred_element_type=jnp.float32
    )


def unpack(main, gains):
    query_key_value_width = (QUERY_HEADS + 2 * KEY_VALUE_HEADS) * HEAD_SIZE
    shapes = [
        (MODEL_WIDTH, query_key_value_width),
        (QUERY_HEADS * HEAD_SIZE, MODEL_WIDTH),
        (MODEL_WIDTH, 2 * FF),
        (FF, MODEL_WIDTH),
    ]
    pieces = []
    offset = 0
    for piece_shape in shapes:
        extent = math.prod(piece_shape) // LANES
        pieces.append(main[offset : offset + extent].reshape(piece_shape))
        offset += extent
    return pieces + [gains[:MODEL_WIDTH], gains[MODEL_WIDTH:]]


def positions_of(segment_row):
    index_row = jnp.arange(segment_row.shape[0], dtype=jnp.int32)
    same = segment_row[:, None] == segment_row[None, :]
    before = index_row[:, None] > index_row[None, :]
    return jnp.sum((same & before).astype(jnp.int32), axis=1)


def rope_tables(positions):
    half_size = HEAD_SIZE // 2
    freqs = theta_base ** (-2.0 * jnp.arange(half_size, dtype=jnp.float32) / HEAD_SIZE)
    angles = positions.astype(jnp.float32)[:, None] * freqs[None, :]
    return (jnp.cos(angles)[:, None, :], jnp.sin(angles)[:, None, :])


def apply_rotation(vectors, cosine_lookup, sine_lookup):
    half_size = HEAD_SIZE // 2
    first_half = vectors[..., :half_size]
    second_half = vectors[..., half_size:]
    return jnp.concatenate(
        [
            first_half * cosine_lookup - second_half * sine_lookup,
            second_half * cosine_lookup + first_half * sine_lookup,
        ],
        axis=-1,
    )


def unrotate(vectors, cosine_lookup, sine_lookup):
    half_size = HEAD_SIZE // 2
    first_half = vectors[..., :half_size]
    second_half = vectors[..., half_size:]
    return jnp.concatenate(
        [
            first_half * cosine_lookup + second_half * sine_lookup,
            second_half * cosine_lookup - first_half * sine_lookup,
        ],
        axis=-1,
    )


def norm_back(d_hidden, normed, inverse, gain):
    d_normed = d_hidden * gain
    return inverse * (d_normed - normed * jnp.mean(d_normed * normed, axis=-1, keepdims=True))


def layer_row(inputs, segment_row, cotangent, weights):
    query_key_value_weight, output_weight, w_gateup, w_down, gain_attn, gain_ffn = weights
    sequence_length = inputs.shape[0]
    repeat_count = QUERY_HEADS // KEY_VALUE_HEADS
    scale_factor = HEAD_SIZE ** (-0.5)
    gain_one = gain_attn.astype(jnp.float32)
    gain_two = gain_ffn.astype(jnp.float32)
    resid_in = inputs.astype(jnp.float32)
    inv_attn = lax.rsqrt(jnp.mean(resid_in * resid_in, axis=-1, keepdims=True) + norm_eps)
    normed_attn = resid_in * inv_attn
    hidden_attn = (normed_attn * gain_one).astype(jnp.bfloat16)
    projected_output = jnp.dot(
        hidden_attn, query_key_value_weight, preferred_element_type=jnp.float32
    )
    cosine_lookup, sine_lookup = rope_tables(positions_of(segment_row))
    query_rows = projected_output[:, : QUERY_HEADS * HEAD_SIZE].reshape(
        sequence_length, QUERY_HEADS, HEAD_SIZE
    )
    key_matrix = projected_output[
        :, QUERY_HEADS * HEAD_SIZE : (QUERY_HEADS + KEY_VALUE_HEADS) * HEAD_SIZE
    ].reshape(sequence_length, KEY_VALUE_HEADS, HEAD_SIZE)
    query_rows_rotated = (
        apply_rotation(query_rows, cosine_lookup, sine_lookup)
        .astype(jnp.bfloat16)
        .reshape(sequence_length, KEY_VALUE_HEADS, repeat_count, HEAD_SIZE)
    )
    keys_rot = apply_rotation(key_matrix, cosine_lookup, sine_lookup).astype(jnp.bfloat16)
    value_rows = (
        projected_output[:, (QUERY_HEADS + KEY_VALUE_HEADS) * HEAD_SIZE :]
        .reshape(sequence_length, KEY_VALUE_HEADS, HEAD_SIZE)
        .astype(jnp.bfloat16)
    )
    index_row = jnp.arange(sequence_length)
    allowed = (segment_row[:, None] == segment_row[None, :]) & (
        index_row[:, None] >= index_row[None, :]
    )
    scores = contract("qgrd,kgd->grqk", query_rows_rotated, keys_rot) * scale_factor
    scores = jnp.where(allowed, scores, masked_value)
    peak = jnp.max(scores, axis=-1, keepdims=True)
    log_total = peak + jnp.log(jnp.sum(jnp.exp(scores - peak), axis=-1, keepdims=True))
    probs_b = jnp.exp(scores - log_total).astype(jnp.bfloat16)
    attended = (
        contract("grqk,kgd->qgrd", probs_b, value_rows)
        .astype(jnp.bfloat16)
        .reshape(sequence_length, QUERY_HEADS * HEAD_SIZE)
    )
    mid = resid_in + jnp.dot(attended, output_weight, preferred_element_type=jnp.float32)
    inv_ffn = lax.rsqrt(jnp.mean(mid * mid, axis=-1, keepdims=True) + norm_eps)
    normed_ffn = mid * inv_ffn
    hidden_ffn = (normed_ffn * gain_two).astype(jnp.bfloat16)
    gate_up = jnp.dot(hidden_ffn, w_gateup, preferred_element_type=jnp.float32)
    gate_pre = gate_up[:, :FF]
    upper = gate_up[:, FF:]
    sigmoid_gate = jax.nn.sigmoid(gate_pre)
    activation = (gate_pre * sigmoid_gate * upper).astype(jnp.bfloat16)
    outputs = (mid + jnp.dot(activation, w_down, preferred_element_type=jnp.float32)).astype(
        jnp.bfloat16
    )
    grad_down = inner_rows(activation, cotangent)
    d_act = outer_column_count(cotangent, w_down)
    d_gate = d_act * upper * sigmoid_gate * (1.0 + gate_pre * (1.0 - sigmoid_gate))
    d_upper = d_act * gate_pre * sigmoid_gate
    d_gate_up = jnp.concatenate([d_gate, d_upper], axis=-1).astype(jnp.bfloat16)
    grad_gateup = inner_rows(hidden_ffn, d_gate_up)
    d_hidden_ffn = outer_column_count(d_gate_up, w_gateup)
    grad_gain_ffn = jnp.sum(d_hidden_ffn * normed_ffn, axis=0)
    d_mid = cotangent.astype(jnp.float32) + norm_back(d_hidden_ffn, normed_ffn, inv_ffn, gain_two)
    grad_middle_batch = d_mid.astype(jnp.bfloat16)
    grad_out = inner_rows(attended, grad_middle_batch)
    grad_attended_rows = (
        outer_column_count(grad_middle_batch, output_weight)
        .astype(jnp.bfloat16)
        .reshape(sequence_length, KEY_VALUE_HEADS, repeat_count, HEAD_SIZE)
    )
    recomputed = contract("qgrd,kgd->grqk", query_rows_rotated, keys_rot) * scale_factor
    probs = jnp.exp(jnp.where(allowed, recomputed, masked_value) - log_total)
    d_probs = contract("qgrd,kgd->grqk", grad_attended_rows, value_rows)
    row_total = jnp.sum(probs * d_probs, axis=-1, keepdims=True)
    d_scores = (probs * (d_probs - row_total) * scale_factor).astype(jnp.bfloat16)
    grad_query_rows = contract("grqk,kgd->qgrd", d_scores, keys_rot).reshape(
        sequence_length, QUERY_HEADS, HEAD_SIZE
    )
    grad_key_rows = contract("grqk,qgrd->kgd", d_scores, query_rows_rotated)
    grad_value_rows = contract("grqk,qgrd->kgd", probs_b, grad_attended_rows)
    grad_query_rows = unrotate(grad_query_rows, cosine_lookup, sine_lookup)
    grad_key_rows = unrotate(grad_key_rows, cosine_lookup, sine_lookup)
    grad_projected_rows = jnp.concatenate(
        [
            grad_query_rows.reshape(sequence_length, QUERY_HEADS * HEAD_SIZE),
            grad_key_rows.reshape(sequence_length, KEY_VALUE_HEADS * HEAD_SIZE),
            grad_value_rows.reshape(sequence_length, KEY_VALUE_HEADS * HEAD_SIZE),
        ],
        axis=-1,
    ).astype(jnp.bfloat16)
    grad_qkv = inner_rows(hidden_attn, grad_projected_rows)
    d_hidden_attn = outer_column_count(grad_projected_rows, query_key_value_weight)
    grad_gain_attn = jnp.sum(d_hidden_attn * normed_attn, axis=0)
    d_inputs = (d_mid + norm_back(d_hidden_attn, normed_attn, inv_attn, gain_one)).astype(
        jnp.bfloat16
    )
    matrices = [grad_qkv, grad_out, grad_gateup, grad_down]
    main = jnp.concatenate([m.astype(jnp.bfloat16).reshape(-1, LANES) for m in matrices])
    gains = jnp.concatenate([grad_gain_attn, grad_gain_ffn])
    return (outputs, d_inputs, main, gains)


def adam_update(grads, clip_factor, params, moment_one, moment_two, decay_mask):
    clipped = grads * clip_factor
    new_moment_one = beta_one * moment_one + (1.0 - beta_one) * clipped
    new_moment_two = beta_two * moment_two + (1.0 - beta_two) * clipped * clipped
    step_size = new_moment_one / bias_one / (jnp.sqrt(new_moment_two / bias_two) + adam_eps)
    decay_term = jnp.where(decay_mask, decay_rate * params, jnp.zeros_like(params))
    new_params = params - learn_rate * (step_size + decay_term)
    return (new_params, new_moment_one, new_moment_two)


def my_bits(wide, count):
    return [(wide // 2**b) % 2 for b in range(count)]


def flipped(wide, bit, b):
    return wide + (1 - 2 * bit) * 2**b


def greet(wide, group, bits, groups):
    barrier = pltpu.get_barrier_semaphore()
    peers = [(flipped(wide, bit, b), group) for b, bit in enumerate(bits)]
    peers += [(wide, (group + d) % groups) for d in range(1, groups)]
    for peer in peers:
        pl.semaphore_signal(barrier, inc=1, device_id=peer, device_id_type=MESH)
    pl.semaphore_wait(barrier, len(peers))


def send(src, dst, send_sem, recv_sem, peer):
    copy = pltpu.make_async_remote_copy(
        src_ref=src,
        dst_ref=dst,
        send_sem=send_sem,
        recv_sem=recv_sem,
        device_id=peer,
        device_id_type=MESH,
    )
    copy.start()
    return copy


def bit_order(chunk, count):
    rest = list(range(1, count))
    return [0] + (rest if chunk % 2 == 0 else rest[::-1])


def tails_kernel(groups, bits_count, tail_ref, out_ref, send_sem, recv_sem):
    wide, group = lax.axis_index("wide"), lax.axis_index("group")
    greet(wide, group, [], groups)
    out_ref[pl.ds(group, 1)] = tail_ref[...][None]
    copies = []
    for d in range(1, groups):
        copies.append(
            send(
                tail_ref,
                out_ref.at[group],
                send_sem.at[d - 1],
                recv_sem.at[d - 1],
                (wide, (group + d) % groups),
            )
        )
    for copy in copies:
        copy.wait()


def gather_kernel(groups, count, chunks, block_ref, out_ref, own_sem, zs, zr, ws, wr):
    wide, group = lax.axis_index("wide"), lax.axis_index("group")
    bits = my_bits(wide, count)
    step = block_ref.shape[-2] // chunks
    greet(wide, group, bits, groups)

    def place(ref, lead, open_bits, chunk):
        index = [slice(None) if b in open_bits else bits[b] for b in reversed(range(count))]
        return ref.at[tuple(lead + index + [pl.ds(chunk * step, step)])]

    def copy(src, dst, send_sem, recv_sem, peer):
        return pltpu.make_async_remote_copy(
            src_ref=src,
            dst_ref=dst,
            send_sem=send_sem,
            recv_sem=recv_sem,
            device_id=peer,
            device_id_type=MESH,
        )

    def along(way, d, c):
        source = (group - way * (d - 1) + groups) % groups
        unit = (0 if way > 0 else groups - 1) + d - 1
        src = place(block_ref, [], [], c) if d == 1 else place(out_ref, [source], [], c)
        return copy(
            src,
            place(out_ref, [source], [], c),
            zs.at[unit, c],
            zr.at[unit, c],
            (wide, (group + way + groups) % groups),
        )

    def passes(way, d):
        ahead = group + way
        behind = group - way * (d - 1)
        return (ahead >= 0) & (ahead < groups) & (behind >= 0) & (behind < groups)

    def comes(way, d):
        behind = group - way * d
        return (behind >= 0) & (behind < groups)

    def across(way, d, c, stage):
        order = bit_order(c, count)[::-1]
        b = order[stage]
        source = (group - way * d + groups) % groups
        unit = (0 if way > 0 else groups - 1) + d - 1
        here = place(out_ref, [source], order[:stage], c)
        return copy(
            here,
            here,
            ws.at[unit, c, stage],
            wr.at[unit, c, stage],
            (flipped(wide, bits[b], b), group),
        )

    units = [(d, c) for d in range(1, groups) for c in range(chunks)]
    for c in range(chunks):
        for way in (1, -1):

            @pl.when(passes(way, 1))
            def _():
                along(way, 1, c).start()

    own = pltpu.make_async_copy(block_ref, out_ref.at[group], own_sem)
    own.start()
    for tick in range(len(units) // 2 + count + 1):
        for u, (d, c) in reversed(list(enumerate(units))):
            stage = tick - u // 2
            if not 0 <= stage <= count:
                continue
            for way in (1, -1):

                @pl.when(comes(way, d))
                def _():
                    if stage == 0:
                        along(way, d, c).wait_recv()
                    else:
                        across(way, d, c, stage - 1).wait_recv()
                    if stage < count:
                        across(way, d, c, stage).start()

                if stage == 0 and d + 1 < groups:

                    @pl.when(passes(way, d + 1))
                    def _():
                        along(way, d + 1, c).start()

    for way in (1, -1):
        for d, c in units:

            @pl.when(passes(way, d))
            def _():
                along(way, d, c).wait_send()

            @pl.when(comes(way, d))
            def _():
                for stage in range(count):
                    across(way, d, c, stage).wait_send()

    own.wait()


def sum_kernel(groups, count, chunks, x_ref, gain_ref, out_ref, head_ref, gsum_ref, sq_ref, *scratch):
    recvs, accs = scratch[:count], scratch[count : 2 * count]
    recv_z, gain_w, gain_z, sq_z, piece_head = scratch[2 * count : 2 * count + 5]
    ss, sr, zs, zr, gs, gr, xs, xr, gzs, gzr, qs, qr, hs, hr = scratch[2 * count + 5 :]
    wide, group = lax.axis_index("wide"), lax.axis_index("group")
    bits = my_bits(wide, count)
    step = x_ref.shape[-2] // chunks
    greet(wide, group, bits, groups)
    copies = {}
    f32 = jnp.float32

    def partner(b):
        return (flipped(wide, bits[b], b), group)

    def part(c, stage, value):
        order = bit_order(c, count)
        left = sorted(order[stage:], reverse=True)
        return [value if b == order[stage] else slice(None) for b in left]

    def held(c, stage):
        return x_ref if stage == 0 else accs[stage - 1].at[c]

    def view(c, stage, flip):
        b = bit_order(c, count)[stage]
        index = [slice(None)] + part(c, stage, 1 - bits[b] if flip else bits[b])
        if stage == 0:
            index += [slice(None)] * (count + 2 - len(index) - 1)
            return x_ref.at[tuple(index + [pl.ds(c * step, step)])]
        return accs[stage - 1].at[tuple([c] + index)]

    def start_scatter(c, stage):
        b = bit_order(c, count)[stage]
        copies["s", c, stage] = send(
            view(c, stage, True), recvs[stage].at[c], ss.at[c, stage], sr.at[c, stage], partner(b)
        )

    def add_scatter(c, stage):
        copies["s", c, stage].wait_recv()
        mine, other, total = view(c, stage, False), recvs[stage].at[c], accs[stage].at[c]

        def body(i, _):
            total[i] = (mine[i].astype(f32) + other[i].astype(f32)).astype(jnp.bfloat16)
            return 0

        lax.fori_loop(0, groups, body, 0)

    def start_groups(c):
        for d in range(1, groups):
            to = (group + d) % groups
            copies["z", c, d] = send(
                accs[-1].at[c, to],
                recv_z.at[c, d - 1],
                zs.at[c, d - 1],
                zr.at[c, d - 1],
                (wide, to),
            )

    def place(open_bits, c):
        index = [slice(None) if b in open_bits else bits[b] for b in reversed(range(count))]
        return out_ref.at[tuple(index + [pl.ds(c * step, step)])]

    def add_groups(c):
        total = accs[-1][c, group].astype(f32)
        for d in range(1, groups):
            copies["z", c, d].wait_recv()
            total = total + recv_z[c, d - 1].astype(f32)
        place([], c)[...] = total.astype(jnp.bfloat16)

    def start_gather(c, stage):
        order = bit_order(c, count)[::-1]
        here = place(order[:stage], c)
        copies["g", c, stage] = send(
            here, here, gs.at[c, stage], gr.at[c, stage], partner(order[stage])
        )

    for c in range(chunks):
        start_scatter(c, 0)
    gain_w[0] = gain_ref[...]
    copies["x", 0] = send(gain_w.at[0], gain_w.at[count + 1], xs.at[0], xr.at[0], partner(0))

    for tick in range(chunks // 2 + 2 * count + 1):
        for c in reversed(range(chunks)):
            s = tick - c // 2
            if 0 <= s < count:
                add_scatter(c, s)
                if s + 1 < count:
                    start_scatter(c, s + 1)
                else:
                    start_groups(c)
            elif s == count:
                add_groups(c)
                start_gather(c, 0)
            elif count < s <= 2 * count:
                copies["g", c, s - count - 1].wait_recv()
                if s < 2 * count:
                    start_gather(c, s - count)
        if tick < count:
            copies["x", tick].wait_recv()
            gain_w[tick + 1] = gain_w[tick] + gain_w[count + 1 + tick]
            if tick + 1 < count:
                copies["x", tick + 1] = send(
                    gain_w.at[tick + 1],
                    gain_w.at[count + 2 + tick],
                    xs.at[tick + 1],
                    xr.at[tick + 1],
                    partner(tick + 1),
                )
            else:
                gain_z[pl.ds(group, 1)] = gain_w[pl.ds(count, 1)]
                for d in range(1, groups):
                    copies["gz", d] = send(
                        gain_w.at[count],
                        gain_z.at[group],
                        gzs.at[d - 1],
                        gzr.at[d - 1],
                        (wide, (group + d) % groups),
                    )

    first = tuple([0] * count + [pl.ds(0, 16)])
    copies["h"] = send(out_ref.at[first], head_ref, hs, hr, (wide, (group + groups - 1) % groups))
    flat_lead = out_ref.shape[:-2]

    def squares(i, total):
        index = tuple((i // 2**b) % 2 for b in reversed(range(len(flat_lead))))
        value = out_ref[index].astype(f32)
        value = value * value
        return total + jnp.sum(value.reshape(-1, 8, LANES), axis=0)

    square = lax.fori_loop(0, math.prod(flat_lead), squares, jnp.zeros((8, LANES), f32))
    piece_head[...] = square
    sq_z[pl.ds(group, 1)] = square[None]
    for d in range(1, groups):
        copies["q", d] = send(
            piece_head, sq_z.at[group], qs.at[d - 1], qr.at[d - 1], (wide, (group + d) % groups)
        )
    for d in range(1, groups):
        copies["gz", d].wait_recv()
    gains = gain_z[0]
    for d in range(1, groups):
        gains = gains + gain_z[d]
    gains = gains.astype(jnp.bfloat16).astype(f32)
    gsum_ref[...] = gains
    for d in range(1, groups):
        copies["q", d].wait_recv()
    square = sq_z[0]
    for d in range(1, groups):
        square = square + sq_z[d]
    square = square + jnp.sum((gains * gains).reshape(-1, 8, LANES), axis=0)
    total = jnp.sum(jnp.sum(square, axis=-1, keepdims=True), axis=0, keepdims=True)
    clip = jnp.minimum(jnp.float32(1.0), max_norm * lax.rsqrt(total))
    sq_ref[...] = jnp.broadcast_to(clip, sq_ref.shape)
    copies["h"].wait_recv()
    for copy in copies.values():
        copy.wait_send()


def params_of(identity):
    return pltpu.CompilerParams(
        collective_id=identity, has_side_effects=True, vmem_limit_bytes=60 * 2**20
    )


def vmem_specs(n):
    return [pl.BlockSpec(memory_space=pltpu.VMEM)] * n


def gather_tails(tail, groups, identity):
    dma = pltpu.SemaphoreType.DMA
    return pl.pallas_call(
        functools.partial(tails_kernel, groups, 0),
        out_shape=jax.ShapeDtypeStruct((groups,) + tail.shape, tail.dtype),
        in_specs=vmem_specs(1),
        out_specs=vmem_specs(1)[0],
        scratch_shapes=[dma((groups - 1,)), dma((groups - 1,))],
        compiler_params=params_of(identity),
        name="tails",
    )(tail)


def gather_blocks(block, groups, count, chunks):
    dma = pltpu.SemaphoreType.DMA
    units = 2 * (groups - 1)
    return pl.pallas_call(
        functools.partial(gather_kernel, groups, count, chunks),
        out_shape=jax.ShapeDtypeStruct((groups,) + block.shape, block.dtype),
        in_specs=vmem_specs(1),
        out_specs=vmem_specs(1)[0],
        scratch_shapes=[
            dma,
            dma((units, chunks)),
            dma((units, chunks)),
            dma((units, chunks, count)),
            dma((units, chunks, count)),
        ],
        compiler_params=params_of(1),
        name="gather_weights",
    )(block)


def sum_blocks(main, gains, groups, count, chunks):
    dma = pltpu.SemaphoreType.DMA
    rows = main.shape[-2]
    step = rows // chunks
    bf16, f32 = jnp.bfloat16, jnp.float32
    stages = [
        pltpu.VMEM((chunks, groups) + (2,) * (count - 1 - k) + (step, LANES), bf16)
        for k in range(count)
    ]
    return pl.pallas_call(
        functools.partial(sum_kernel, groups, count, chunks),
        out_shape=(
            jax.ShapeDtypeStruct((2,) * count + (rows, LANES), bf16),
            jax.ShapeDtypeStruct((16, LANES), bf16),
            jax.ShapeDtypeStruct(gains.shape, f32),
            jax.ShapeDtypeStruct((8, LANES), f32),
        ),
        in_specs=vmem_specs(2),
        out_specs=tuple(vmem_specs(4)),
        scratch_shapes=stages
        + stages
        + [
            pltpu.VMEM((chunks, groups - 1, step, LANES), bf16),
            pltpu.VMEM((2 * count + 1,) + gains.shape, f32),
            pltpu.VMEM((groups,) + gains.shape, f32),
            pltpu.VMEM((groups, 8, LANES), f32),
            pltpu.VMEM((8, LANES), f32),
        ]
        + [dma((chunks, count))] * 2
        + [dma((chunks, groups - 1))] * 2
        + [dma((chunks, count))] * 2
        + [dma((count,))] * 2
        + [dma((groups - 1,))] * 4
        + [dma, dma],
        compiler_params=params_of(2),
        name="sum_grads",
    )(main, gains)


def dot(left_op, right_op, left_dim, right_dim):
    return lax.dot_general(
        left_op,
        right_op,
        (((left_dim,), (right_dim,)), ((), ())),
        preferred_element_type=jnp.float32,
    )


def cores_of(wide):
    core, x_bit, y_bit = wide % 2, (wide // 2) % 2, (wide // 4) % 2
    over_x, over_y = wide + (1 - 2 * x_bit) * 2, wide + (1 - 2 * y_bit) * 4
    one = over_x * (1 - core) + over_y * core
    two = over_y * (1 - core) + over_x * core
    far = over_x + over_y - wide
    twin = wide + 1 - 2 * core
    return core, over_x, over_y, far, one, two, twin


def greet_all(peers):
    barrier = pltpu.get_barrier_semaphore()
    for peer in peers:
        pl.semaphore_signal(barrier, inc=1, device_id=peer, device_id_type=MESH)
    pl.semaphore_wait(barrier, len(peers))


def remote(src, dst, send_sem, recv_sem, peer):
    return pltpu.make_async_remote_copy(
        src_ref=src,
        dst_ref=dst,
        send_sem=send_sem,
        recv_sem=recv_sem,
        device_id=peer,
        device_id_type=MESH,
    )


QKV = (QUERY_HEADS + 2 * KEY_VALUE_HEADS) * HEAD_SIZE
INNER = QUERY_HEADS * HEAD_SIZE
JOINT = QKV + INNER
HALF_JOINT = JOINT // 2
CHIPS = 4
CHIP_ROWS = MODEL_WIDTH // CHIPS
UNITS = FF // CHIPS
HALF_WIDTH = MODEL_WIDTH // 2
SPLIT = 3
SUB = CHIP_ROWS // SPLIT
BLOCK = MODEL_WIDTH * FF
BLOCK_ROWS = BLOCK // LANES
EXTRA = 2 * MODEL_WIDTH // 4
HEAD_ROWS = 8


def lanes_of(rows):
    return lax.broadcasted_iota(jnp.int32, (rows, LANES), 1)


def rows_at(ref, at, count, kept=0):
    if kept:
        value = ref[pl.ds(at * LANES, kept)]
        value = jnp.concatenate([value, jnp.zeros((count * LANES - kept,), value.dtype)])
    else:
        value = ref[pl.ds(pl.multiple_of(at * LANES, 1024), count * LANES)]
    return value.reshape(count, LANES)


ADAM_CHUNKS = 8
ADAM_ROWS = BLOCK_ROWS // ADAM_CHUNKS
ADAM_STEP = 96
PIECE_ROWS = BLOCK_ROWS // 8


def row_kernel(
    groups, x_ref, seg_ref, cot_ref, params_ref, one_ref, two_ref,
    out_ref, din_ref, flat, clip_ref, par_b, one_b, two_b,
    joint_ref, gu_ref, down_ref, gain_w, raw, lin, lin_t, tail_s, gain_s, pan_w,
    proj_s, att_s, mid_s, dmid_s, dproj_s, cots, hids, act_s, gate_s, up_s, part_s, part_r,
    gj_ref, ggu_ref, gdn_ref, core_j, core_g, core_d, acc_j, acc_g, acc_d,
    rs_one, rs_two, z_j, z_g, z_d, ag, note, note_z, pan,
    raw_sem, ts, tr, gns, gnr, wzs, wzr, as_, ar, es, er,
    cs, cr, hs, hr, ps, pr,
    load_sem, sws, swr, r1s, r1r, r2s, r2r, zs, zr, ags, agr, ns, nr, nzs, nzr, hds, hdr,
):
    f32, bf16 = jnp.float32, jnp.bfloat16
    wide, group = lax.axis_index("wide"), lax.axis_index("group")
    core, over_x, over_y, far, one, two, twin = cores_of(wide)
    chip = wide // 2
    whole = pltpu.make_async_copy(params_ref, lin, raw_sem.at[0])

    def part_load(i, at, count):
        here = pl.ds(pl.multiple_of(at * LANES, 1024), count * LANES)
        return pltpu.make_async_copy(params_ref.at[here], lin.at[here], raw_sem.at[i])

    qkv_rows, out_rows = BLOCK_ROWS * QKV // JOINT // CHIPS, BLOCK_ROWS * INNER // JOINT // CHIPS
    qkv_from, out_from_row = qkv_rows * chip, CHIPS * qkv_rows + out_rows * chip
    load_qkv, load_out = part_load(1, qkv_from, qkv_rows), part_load(2, out_from_row, out_rows)

    load_end = pltpu.make_async_copy(
        params_ref.at[pl.ds(BLOCK - 8 * LANES, 8 * LANES + EXTRA)], lin_t, raw_sem.at[3]
    )

    @pl.when(group == 0)
    def _():
        load_qkv.start()
        load_out.start()
        load_end.start()

    @pl.when(group > 0)
    def _():
        whole.start()

    peers = [(p, group) for p in (over_x, over_y, far, twin)]
    peers += [(wide, (group + d) % groups) for d in range(1, groups)]
    near = peers[:3]
    greet_all(peers)
    width, length, half = MODEL_WIDTH, x_ref.shape[1], HEAD_SIZE // 2
    turn_rate = -2.0 * math.log(theta_base) / HEAD_SIZE
    heads, kv = QUERY_HEADS, KEY_VALUE_HEADS
    repeat = heads // kv
    scale = HEAD_SIZE**-0.5
    def block(ref, j):
        return ref.at[pl.ds(j * length, length)]

    cots[0:length, :] = cot_ref[...].astype(f32).T.astype(bf16)
    cot_copies = [
        remote(block(cots, 0), block(cots, j + 1), cs.at[j], cr.at[j], near[j]) for j in range(3)
    ]
    for copy in cot_copies:
        copy.start()


    copy_rows = 216

    def unroll(start, count):
        def step(i, _):
            at = start + i * copy_rows
            raw[pl.ds(pl.multiple_of(HEAD_ROWS + at, 8), copy_rows), :] = rows_at(lin, at, copy_rows)
            return 0

        lax.fori_loop(0, count // copy_rows, step, 0)

    @pl.when(group == 0)
    def _():
        load_qkv.wait()
        unroll(qkv_from, qkv_rows)
        load_out.wait()
        unroll(out_from_row, out_rows)
        load_end.wait()
        at = HEAD_ROWS + BLOCK_ROWS
        raw[at - 8 : at, :] = rows_at(lin_t, 0, 8)
        raw[at : at + 8, :] = rows_at(lin_t, 8, 8, EXTRA)

    @pl.when(group > 0)
    def _():
        whole.wait()
        unroll(0, BLOCK_ROWS)
        raw[pl.ds(HEAD_ROWS + BLOCK_ROWS, 8), :] = rows_at(lin, BLOCK_ROWS, 8, EXTRA)

    def joined(first, second, shift, cut):
        lane = lanes_of(first.shape[0])
        return jnp.where(lane < cut, pltpu.roll(first, shift, 1), pltpu.roll(second, shift, 1))

    tail = remote(tail_s, raw.at[pl.ds(0, HEAD_ROWS)], ts, tr, (wide, (group + 1) % groups))
    top = HEAD_ROWS + BLOCK_ROWS + 2

    @pl.when(group < groups - 1)
    def _():
        at = top - HEAD_ROWS
        tail_s[...] = joined(raw[at : at + 8, :], raw[at + 1 : at + 9, :], 96, 96)
        tail.start()

    def gain_copy(g):
        return remote(gain_s, gain_s, gns.at[g], gnr, (wide, g))

    @pl.when(group == groups - 1)
    def _():
        at = top - 9
        gain_s[...] = joined(raw[at : at + 16, :], raw[at + 1 : at + 17, :], 96, 96)
        for g in range(groups - 1):
            gain_copy(g).start()

    @pl.when(group > 0)
    def _():
        tail.wait_recv()

    def take(start, count, stride):
        return raw[pl.ds(start, count, stride), :]

    pairs = CHIP_ROWS // 2

    def put_joint(p, even, odd):
        pan_w[pl.ds(p % 6 * CHIP_ROWS, pairs, 2), :] = even
        pan_w[pl.ds(p % 6 * CHIP_ROWS + 1, pairs, 2), :] = odd
        joint_ref[pl.ds(pl.multiple_of(CHIP_ROWS * chip, 16), CHIP_ROWS), p * LANES : (p + 1) * LANES] = pan_w[
            p % 6 * CHIP_ROWS : (p % 6 + 1) * CHIP_ROWS, :
        ].astype(bf16)

    qkv_at = HEAD_ROWS + 1080 * chip
    out_at = HEAD_ROWS + 4320 + 648 * chip

    def qkv(k):
        return take(qkv_at + k, pairs, 15)

    def out(k):
        return take(out_at + k, pairs, 9)

    @pl.when((group == 0) & (core == 0))
    def _():
        for p in range(6):
            put_joint(p, qkv(p), joined(qkv(7 + p), qkv(8 + p), 64, 64))

    @pl.when((group == 0) & (core == 1))
    def _():
        put_joint(6, qkv(6), joined(qkv(13), qkv(14), 64, 64))
        lane = lanes_of(pairs)
        put_joint(
            7,
            jnp.where(lane < 64, qkv(7), pltpu.roll(out(0), 64, 1)),
            jnp.where(lane < 64, pltpu.roll(qkv(14), 64, 1), out(4)),
        )
        for k in range(4):
            put_joint(8 + k, joined(out(k), out(k + 1), 64, 64), out(5 + k))

    for g, back, shift in ((1, 3, 32), (2, 5, 64)):

        @pl.when(group == g)
        def _():
            for j in range(3):
                at = HEAD_ROWS - back + 12 * core + 3 * chip + j
                value = joined(take(at, HALF_WIDTH, 24), take(at + 1, HALF_WIDTH, 24), shift, shift)
                gu_ref[core, (g - 1) * HALF_WIDTH : g * HALF_WIDTH, j * LANES : (j + 1) * LANES] = value.astype(bf16)

    half_units = UNITS // 2

    @pl.when(group == 3)
    def _():
        rows = pl.ds(pl.multiple_of(half_units * core, 16), half_units)
        count = half_units // 2
        for p in range(5):
            at = HEAD_ROWS + 864 * wide + p
            even = joined(take(at - 7, count, 9), take(at - 6, count, 9), 96, 96)
            odd = joined(take(at - 3, count, 9), take(at - 2, count, 9), 32, 32)
            pan_w[pl.ds(p * half_units, count, 2), :] = even
            pan_w[pl.ds(p * half_units + 1, count, 2), :] = odd
            value = pan_w[p * half_units : (p + 1) * half_units, :].astype(bf16)
            if p < 4:
                down_ref[rows, p * LANES : (p + 1) * LANES] = value
            else:
                down_ref[rows, p * LANES : MODEL_WIDTH] = value[:, : MODEL_WIDTH - p * LANES]

    def attn_at(q, c, k):
        return joint_ref.at[
            pl.ds(pl.multiple_of(CHIP_ROWS * q + SUB * k, 16), SUB),
            pl.ds(pl.multiple_of(HALF_JOINT * c, LANES), HALF_JOINT),
        ]

    def piece(s, k):
        if s == 0:
            return attn_at(chip, core, k)
        if s < 3:
            step = HALF_WIDTH // SPLIT
            return gu_ref.at[core, pl.ds((s - 1) * HALF_WIDTH + k * step, step)]
        step = half_units // SPLIT
        return down_ref.at[pl.ds(pl.multiple_of(half_units * core + k * step, 16), step)]

    def pass_on(s, k, way):
        to = (wide, (group + way + groups) % groups)
        return remote(piece(s, k), piece(s, k), wzs.at[(way + 1) // 2, s, k], wzr.at[s, k], to)

    def sends(s):
        right = (group >= s) & (group < groups - 1)
        left = (group <= s) & (group > 0)
        return right, left

    def forward(s, k):
        right, left = sends(s)

        @pl.when(right)
        def _():
            pass_on(s, k, 1).start()

        @pl.when(left)
        def _():
            pass_on(s, k, -1).start()

    def give(s, k):
        return remote(piece(s, k), piece(s, k), es.at[s, k], er.at[s, k], (twin, group))

    for s in range(groups):

        @pl.when(group == s)
        def _():
            for k in range(SPLIT):
                if s == 0:
                    pass_on(s, k, 1).start()
                else:
                    pass_on(s, k, -1).start()
                    give(s, k).start()

    q_one, q_two = one // 2, two // 2
    q_far = 3 - chip

    def stage(n, k, q):
        peer = (one, two, two, twin, twin, twin, twin)[n]
        return remote(attn_at(q, core, k), attn_at(q, core, k), as_.at[n, k], ar.at[n, k], (peer, group))

    for k in range(SPLIT):

        @pl.when(group > 0)
        def _():
            pass_on(0, k, 1).wait_recv()
            forward(0, k)

        stage(0, k, chip).start()
        stage(1, k, chip).start()
        stage(3, k, chip).start()

    for s in range(1, groups - 1):

        @pl.when(group == s)
        def _():
            for k in range(SPLIT):
                pass_on(s, k, 1).start()

    def relay(s, g):
        @pl.when(group == g)
        def _():
            for k in range(SPLIT):
                pass_on(s, k, 1).wait_recv()
                forward(s, k)
                give(s, k).start()

    for s in (1, 2, 3):
        relay(s, s - 1)
    @pl.when(group < groups - 1)
    def _():
        gain_copy(0).wait_recv()

    gains = gain_s[...].astype(bf16).astype(f32)
    for k in range(4):
        gain_w[0:1, k * LANES : (k + 1) * LANES] = gains[k : k + 1]
    gain_w[0:1, 4 * LANES : MODEL_WIDTH] = gains[4:5, : MODEL_WIDTH - 4 * LANES]
    turned = pltpu.roll(gains, 64, 1)
    lane = lanes_of(1)
    for k in range(4):
        gain_w[1:2, k * LANES : (k + 1) * LANES] = jnp.where(lane < 64, turned[4 + k : 5 + k], turned[5 + k : 6 + k])
    gain_w[1:2, 4 * LANES : MODEL_WIDTH] = turned[8:9, : MODEL_WIDTH - 4 * LANES]

    gain_one, gain_two = gain_w[0:1, :], gain_w[1:2, :]
    x = x_ref[...].astype(f32).T
    inv_attn = lax.rsqrt(jnp.mean(x * x, axis=-1, keepdims=True) + norm_eps)
    normed_attn = x * inv_attn
    hidden_attn = (normed_attn * gain_one).astype(bf16)

    seg_row = jnp.broadcast_to(seg_ref[...].astype(f32), (length, length))
    rows = lax.broadcasted_iota(jnp.int32, (length, length), 0)
    columns = lax.broadcasted_iota(jnp.int32, (length, length), 1)
    allowed = (seg_row == seg_row.T) & (rows >= columns)
    positions = jnp.sum(jnp.where(allowed, 1.0, 0.0), axis=-1, keepdims=True) - 1.0
    angles = positions * jnp.exp(turn_rate * (lanes_of(1) % half).astype(f32))
    lane = lax.broadcasted_iota(jnp.int32, (length, LANES), 1)
    first = lane % HEAD_SIZE < half
    cosine, sine = jnp.cos(angles), jnp.sin(angles)
    sine = jnp.where(first, -sine, sine)

    def swap(u):
        return jnp.where(first, pltpu.roll(u, LANES - half, 1), pltpu.roll(u, half, 1))

    for k in range(SPLIT):
        stage(0, k, q_one).wait_recv()
        stage(2, k, q_one).start()
        stage(4, k, q_one).start()
    for k in range(SPLIT):
        stage(1, k, q_two).wait_recv()
        stage(5, k, q_two).start()
    for s in (2, 3):
        relay(s, s - 2)
    for k in range(SPLIT):
        stage(2, k, q_far).wait_recv()
        stage(6, k, q_far).start()
    for s in (1, 2):
        relay(s, s + 1)
    for k in range(SPLIT):
        for n in range(3, 7):
            stage(n, k, chip).wait_recv()

    panels = 8
    turned_panels = (heads + kv) * HEAD_SIZE // LANES
    wide_qkv = panels * LANES
    for p in range(0, panels, 2):
        both = dot(hidden_attn, joint_ref[:, p * LANES : (p + 2) * LANES], 1, 0)
        for q in (p, p + 1):
            u = both[:, (q - p) * LANES : (q - p + 1) * LANES]
            if q < turned_panels:
                u = u * cosine + swap(u) * sine
            proj_s[:, q * LANES : (q + 1) * LANES] = u.astype(bf16)

    def slot(s):
        return proj_s[:, s * HEAD_SIZE : (s + 1) * HEAD_SIZE]

    mask = jnp.concatenate([allowed] * repeat, axis=0)
    saved = []
    for j in range(kv):
        queries = jnp.concatenate([slot(repeat * j + r) for r in range(repeat)], axis=0)
        keys, values = slot(heads + j), slot(heads + kv + j)
        scores = jnp.where(mask, dot(queries, keys, 1, 1) * scale, masked_value)
        peak = jnp.max(scores, axis=-1, keepdims=True)
        total = jnp.sum(jnp.exp(scores - peak), axis=-1, keepdims=True)
        probs = jnp.exp(scores - (peak + jnp.log(total)))
        probs_b = probs.astype(bf16)
        attended = dot(probs_b, values, 1, 0)
        for r in range(repeat):
            at = (repeat * j + r) * HEAD_SIZE
            att_s[:, at : at + HEAD_SIZE] = attended[r * length : (r + 1) * length].astype(bf16)
        saved.append((queries, keys, values, probs, probs_b))

    out_from = QKV // LANES * LANES
    shift = QKV - out_from
    w_out = joint_ref.at[:, out_from:JOINT]
    mid = x + dot(att_s[...], w_out[...], 1, 0)[:, shift:]
    inv_ffn = lax.rsqrt(jnp.mean(mid * mid, axis=-1, keepdims=True) + norm_eps)
    normed_ffn = mid * inv_ffn
    hids[0:length, :] = (normed_ffn * gain_two).astype(bf16)
    hid_copies = [
        remote(block(hids, 0), block(hids, j + 1), hs.at[j], hr.at[j], near[j]) for j in range(3)
    ]
    for copy in hid_copies:
        copy.start()
    mid_s[...] = mid

    relay(3, 0)
    relay(1, 3)
    for k in range(SPLIT):
        for s in range(1, groups):
            give(s, k).wait_recv()

    def feed(j):
        at = slice(j * length, (j + 1) * length)
        hidden, cotangent = hids[at, :], cots[at, :]
        gate, upper = dot(hidden, gu_ref[0], 1, 0), dot(hidden, gu_ref[1], 1, 0)
        d_act = dot(cotangent, down_ref[...], 1, 1)
        sigmoid = jax.nn.sigmoid(gate)
        activation = (gate * sigmoid * upper).astype(bf16)
        d_gate = (d_act * upper * sigmoid * (1.0 + gate * (1.0 - sigmoid))).astype(bf16)
        d_upper = (d_act * gate * sigmoid).astype(bf16)
        act_s[at, :], gate_s[at, :], up_s[at, :] = activation, d_gate, d_upper
        d_hidden = dot(d_gate, gu_ref[0], 1, 1) + dot(d_upper, gu_ref[1], 1, 1)
        return d_hidden, dot(activation, down_ref[...], 1, 0)

    def part_copy(n, j):
        return remote(part_s.at[n, j], part_r.at[n, j], ps.at[n, j], pr.at[n, j], near[j])

    d_hidden, out_own = feed(0)
    for j in range(3):
        cot_copies[j].wait_recv()
        hid_copies[j].wait_recv()
        d_part, out_part = feed(j + 1)
        part_s[0, j] = d_part.astype(bf16)
        part_copy(0, j).start()
        part_s[1, j] = out_part.astype(bf16)

    ggu_ref[0] = dot(hids[...], gate_s[...], 0, 0).astype(bf16)
    ggu_ref[1] = dot(hids[...], up_s[...], 0, 0).astype(bf16)
    gdn_ref[...] = dot(act_s[...], cots[...], 0, 0).astype(bf16)

    half_units = UNITS // 2
    other = 1 - core

    def half_cols(c):
        return pl.ds(pl.multiple_of(HALF_JOINT * c, LANES), HALF_JOINT)

    def half_rows(c):
        return pl.ds(pl.multiple_of(half_units * c, 16), half_units)

    def chip_rows(q):
        return pl.ds(pl.multiple_of(CHIP_ROWS * q, 16), CHIP_ROWS)

    trades = [
        remote(ggu_ref.at[other], core_g, sws.at[0], swr.at[0], (twin, group)),
        remote(gdn_ref.at[half_rows(other)], core_d, sws.at[1], swr.at[1], (twin, group)),
        remote(gj_ref.at[:, half_cols(other)], core_j, sws.at[2], swr.at[2], (twin, group)),
    ]
    for trade in trades[:2]:
        trade.start()
    def add_rows(count, step, total, mine, theirs):
        def body(i, _):
            at = pl.ds(pl.multiple_of(i * step, 16), step)
            total(at, mine(at).astype(f32) + theirs(at).astype(f32))
            return 0

        lax.fori_loop(0, count // step, body, 0)

    def into(ref):
        def put(at, value):
            ref[at, :] = value.astype(bf16)

        return put

    def z_source(g):
        if g == 0:
            return acc_j.at[chip_rows(chip)], z_j
        if g < 3:
            return acc_g.at[pl.ds((g - 1) * HALF_WIDTH, HALF_WIDTH)], z_g
        return acc_d, z_d

    def z_copy(g):
        source, target = z_source(g)
        place = (group - g + groups) % groups
        at = (place + groups - 1) % groups
        return remote(source, target.at[at], zs.at[g], zr.at[at], (wide, g))

    def z_send(g):
        @pl.when(group != g)
        def _():
            z_copy(g).start()

    trades[0].wait_recv()
    add_rows(MODEL_WIDTH, 48, into(acc_g), lambda at: ggu_ref[core, at, :], lambda at: core_g[at, :])
    z_send(1)
    z_send(2)
    trades[1].wait_recv()
    half_from = half_units * core

    def down_mine(at):
        return gdn_ref[pl.ds(pl.multiple_of(half_from + at.start, 16), at.size), :]

    add_rows(half_units, 48, into(acc_d), down_mine, lambda at: core_d[at, :])
    z_send(3)
    for j in range(3):
        part_copy(0, j).wait_recv()
    for j in range(3):
        part_copy(1, j).start()
    for j in range(3):
        d_hidden = d_hidden + part_r[0, j].astype(f32)
    mid = mid_s[...]
    normed_ffn = mid * inv_ffn
    gain_ffn = jnp.sum(d_hidden * normed_ffn, axis=0, keepdims=True)
    d_mid = cots[0:length, :].astype(f32) + norm_back(d_hidden, normed_ffn, inv_ffn, gain_two)
    dmid_s[...] = jnp.zeros_like(dmid_s)
    dmid_s[:, shift:] = d_mid.astype(bf16)
    d_attended = dot(dmid_s[...], w_out[...], 1, 1)
    grad_out = dot(att_s[...], dmid_s[...], 0, 0)
    gj_ref[:, out_from + LANES : JOINT] = grad_out[:, LANES:].astype(bf16)
    edge = grad_out[:, :LANES]
    att_s[...] = d_attended.astype(bf16)

    dproj_s[...] = jnp.zeros_like(dproj_s)
    for j in range(kv):
        queries, keys, values, probs, probs_b = saved[j]
        d_att = jnp.concatenate(
            [
                att_s[:, (repeat * j + r) * HEAD_SIZE : (repeat * j + r + 1) * HEAD_SIZE]
                for r in range(repeat)
            ],
            axis=0,
        )
        d_probs = dot(d_att, values, 1, 1)
        row_total = jnp.sum(probs * d_probs, axis=-1, keepdims=True)
        d_scores = (probs * (d_probs - row_total) * scale).astype(bf16)
        d_queries = dot(d_scores, keys, 1, 0)
        for r in range(repeat):
            at = (repeat * j + r) * HEAD_SIZE
            dproj_s[:, at : at + HEAD_SIZE] = d_queries[r * length : (r + 1) * length]
        at = (heads + j) * HEAD_SIZE
        dproj_s[:, at : at + HEAD_SIZE] = dot(d_scores, queries, 0, 0)
        at = (heads + kv + j) * HEAD_SIZE
        dproj_s[:, at : at + HEAD_SIZE] = dot(probs_b, d_att, 0, 0)

    for p in range(panels):
        raw = dproj_s[:, p * LANES : (p + 1) * LANES]
        if p < turned_panels:
            raw = raw * cosine - swap(raw) * sine
        proj_s[:, p * LANES : (p + 1) * LANES] = raw.astype(bf16)
    d_hidden = dot(proj_s[...], joint_ref[:, :wide_qkv], 1, 1)
    grad_qkv = dot(hidden_attn, proj_s[...], 0, 0)
    gj_ref[:, :out_from] = grad_qkv[:, :out_from].astype(bf16)
    gj_ref[:, out_from:wide_qkv] = (grad_qkv[:, out_from:] + edge).astype(bf16)
    gain_attn = jnp.sum(d_hidden * normed_attn, axis=0, keepdims=True)
    din_ref[...] = (d_mid + norm_back(d_hidden, normed_attn, inv_attn, gain_one)).T.astype(bf16)
    both = jnp.concatenate([gain_attn, gain_ffn], axis=1)
    note[0, 0:16, :] = jnp.zeros((16, LANES), f32)
    for k in range(2 * width // LANES):
        note[0, k : k + 1, :] = both[:, k * LANES : (k + 1) * LANES].astype(bf16).astype(f32)

    trades[2].start()
    loads = [
        pltpu.make_async_copy(source, bank, load_sem.at[i])
        for i, (source, bank) in enumerate(
            ((params_ref, par_b), (one_ref, one_b), (two_ref, two_b))
        )
    ]
    for load in loads:
        load.start()
    trades[2].wait_recv()

    add_rows(MODEL_WIDTH, 16, into(acc_j), lambda at: gj_ref[at, half_cols(core)], lambda at: core_j[at, :])

    def rs_copy(i):
        q = (q_one, q_far)[i]
        return remote(acc_j.at[chip_rows(q)], rs_one.at[i], r1s.at[i], r1r.at[i], (one, group))

    rs_copy(1).start()
    rs_copy(0).start()
    outputs = mid + out_own
    for j in range(3):
        part_copy(1, j).wait_recv()
        outputs = outputs + part_r[1, j].astype(f32)
    out_ref[...] = outputs.T.astype(bf16)

    def add_piece(q, theirs):
        def body(i, _):
            at = pl.ds(pl.multiple_of(CHIP_ROWS * q + i * 16, 16), 16)
            value = acc_j[at, :].astype(f32) + theirs[pl.ds(pl.multiple_of(i * 16, 16), 16), :].astype(f32)
            acc_j[at, :] = value.astype(bf16)
            return 0

        lax.fori_loop(0, CHIP_ROWS // 16, body, 0)

    rs_copy(1).wait_recv()
    add_piece(q_two, rs_one.at[1])
    rs_last = remote(acc_j.at[chip_rows(q_two)], rs_two, r2s, r2r, (two, group))
    rs_last.start()
    rs_copy(0).wait_recv()
    add_piece(chip, rs_one.at[0])
    rs_last.wait_recv()
    add_piece(chip, rs_two)
    z_send(0)

    def squares(value):
        return jnp.sum((value * value).reshape(-1, 8, LANES), axis=0)

    def z_total(g, rows, widths):
        source, target = z_source(g)
        for at in range(groups - 1):
            remote(source, target.at[at], zs.at[g], zr.at[at], (wide, g)).wait_recv()
        step = 16
        panels = -(-widths // LANES)

        def body(i, total):
            at = pl.ds(pl.multiple_of(i * step, 16), step)
            value = source[at, :].astype(f32)
            for d in range(groups - 1):
                value = value + target[d, at, :].astype(f32)
            value = value.astype(bf16)
            for p in range(widths // LANES):
                part = value[:, p * LANES : (p + 1) * LANES]
                ag[wide, pl.ds(pl.multiple_of(p * rows + i * step, 16), step), :] = part
                total = total + squares(part.astype(f32))
            if widths % LANES:
                part = value[:, widths // LANES * LANES :]
                half_s[pl.ds(pl.multiple_of(i * step, 16), step), 0 : LANES // 2] = part
                part = part.astype(f32)
                total = total + jnp.concatenate([squares_half(part), jnp.zeros((8, LANES // 2), f32)], axis=1)
            return total

        def squares_half(part):
            return (part * part)[:8] + (part * part)[8:]

        half_s = None
        if widths % LANES:
            half_s = pan_b
        note[0, 16:24, :] = lax.fori_loop(0, rows // step, body, jnp.zeros((8, LANES), f32))
        if widths % LANES:
            n = rows // 2
            low, high = half_s[0:n, 0 : LANES // 2], half_s[n:rows, 0 : LANES // 2]
            ag[wide, panels * rows - rows : panels * rows - n, :] = jnp.concatenate([low, high], axis=1)

    pan_b = core_d

    @pl.when(group == 0)
    def _():
        z_total(0, CHIP_ROWS, HALF_JOINT)

    @pl.when((group == 1))
    def _():
        z_total(1, HALF_WIDTH, UNITS)

    @pl.when((group == 2))
    def _():
        z_total(2, HALF_WIDTH, UNITS)

    @pl.when(group == 3)
    def _():
        z_total(3, half_units, MODEL_WIDTH)

    def note_copy(n):
        return remote(note.at[n], note.at[n + 4], ns.at[n], nr.at[n], ((one, two, twin)[n], group))

    def ag_copy(n):
        peer = (one, two, two, twin, twin, twin, twin)[n]
        q = (chip, chip, q_one, chip, q_one, q_two, q_far)[n]
        here = ag.at[2 * q + core]
        return remote(here, here, ags.at[n], agr.at[n], (peer, group))

    def note_step(n):
        note_copy(n).wait_recv()
        note[n + 1] = note[n] + note[n + 4]
        if n < 2:
            note_copy(n + 1).start()

    note_copy(0).start()
    for n in (0, 1, 3):
        ag_copy(n).start()
    note_step(0)
    ag_copy(0).wait_recv()
    ag_copy(2).start()
    ag_copy(4).start()
    note_step(1)
    ag_copy(1).wait_recv()
    ag_copy(5).start()
    note_step(2)
    note_z[pl.ds(group, 1)] = note[3:4]

    def note_far(d):
        return remote(
            note.at[3], note_z.at[group], nzs.at[d - 1], nzr.at[d - 1], (wide, (group + d) % groups)
        )

    for d in range(1, groups):
        note_far(d).start()

    pairs = CHIP_ROWS // 2
    lane_pairs = lanes_of(pairs)

    def halves(first, second):
        lane = lanes_of(first.shape[0])
        return jnp.where(lane < 64, pltpu.roll(first, 64, 1), pltpu.roll(second, 64, 1))

    def lay_joint(q):
        for p in range(12):
            at = p % 6 * CHIP_ROWS
            pan[p * CHIP_ROWS : (p + 1) * CHIP_ROWS, :] = ag[2 * q + p // 6, at : at + CHIP_ROWS, :].astype(f32)

        def even(p):
            return pan[pl.ds(p * CHIP_ROWS, pairs, 2), :]

        def odd(p):
            return pan[pl.ds(p * CHIP_ROWS + 1, pairs, 2), :]

        def put_qkv(k, value):
            flat[pl.ds(1080 * q + k, pairs, 15), :] = value

        def put_out(k, value):
            flat[pl.ds(4320 + 648 * q + k, pairs, 9), :] = value

        for p in range(7):
            put_qkv(p, even(p))
            put_qkv(8 + p, halves(odd(p), odd(p + 1)))
        put_qkv(7, jnp.where(lane_pairs < 64, even(7), pltpu.roll(odd(0), 64, 1)))
        for k in range(4):
            put_out(k, halves(even(7 + k), even(8 + k)))
            put_out(5 + k, odd(8 + k))
        put_out(4, jnp.where(lane_pairs < 64, pltpu.roll(even(11), 64, 1), odd(7)))

    def lay_gateup(q):
        for c in range(2):
            for j in range(3):
                value = ag[2 * q + c, j * HALF_WIDTH : (j + 1) * HALF_WIDTH, :].astype(f32)
                flat[pl.ds(12 * c + 3 * q + j, HALF_WIDTH, 24), :] = value

    def lay_down(q):
        n = half_units
        for c in range(2):
            w = 2 * q + c
            pan[0 : 4 * n, :] = ag[w, 0 : 4 * n, :].astype(f32)
            packed = ag[w, 4 * n : 4 * n + n // 2, :].astype(f32)
            pan[4 * n : 4 * n + n // 2, :] = packed
            pan[4 * n + n // 2 : 5 * n, :] = pltpu.roll(packed, 64, 1)

            def even(p):
                return pan[pl.ds(p * n, n // 2, 2), :]

            def odd(p):
                return pan[pl.ds(p * n + 1, n // 2, 2), :]

            def put(k, value):
                flat[pl.ds(864 * w + k, n // 2, 9), :] = value

            for p in range(4):
                put(p, even(p))
                put(5 + p, halves(odd(p), odd(p + 1)))
            put(4, jnp.where(lanes_of(n // 2) < 64, even(4), pltpu.roll(odd(0), 64, 1)))

    def lay(q):
        @pl.when(group == 0)
        def _():
            lay_joint(q)

        @pl.when((group == 1) | (group == 2))
        def _():
            lay_gateup(q)

        @pl.when(group == 3)
        def _():
            lay_down(q)

    ag_copy(3).wait_recv()
    lay(chip)
    ag_copy(2).wait_recv()
    ag_copy(6).start()
    ag_copy(4).wait_recv()
    lay(q_two)
    ag_copy(5).wait_recv()
    lay(q_one)
    ag_copy(6).wait_recv()
    lay(q_far)

    head = remote(
        flat.at[pl.ds(0, HEAD_ROWS)],
        flat.at[pl.ds(BLOCK_ROWS, HEAD_ROWS)],
        hds,
        hdr,
        (wide, (group + groups - 1) % groups),
    )

    @pl.when(group > 0)
    def _():
        head.start()

    for d in range(1, groups):
        note_far(d).wait_recv()
    total = note_z[0]
    for d in range(1, groups):
        total = total + note_z[d]
    gains = total[:16]
    square = total[16:24] + squares(gains)
    square = jnp.sum(jnp.sum(square, axis=-1, keepdims=True), axis=0, keepdims=True)
    clip = jnp.minimum(jnp.float32(1.0), max_norm * lax.rsqrt(square))

    @pl.when(group == groups - 1)
    def _():
        flat[pl.ds(BLOCK_ROWS, 16), :] = gains

    clip_ref[...] = jnp.broadcast_to(clip, clip_ref.shape)

    @pl.when(group < groups - 1)
    def _():
        head.wait_recv()


    for load in loads:
        load.wait()
    for k in range(SPLIT):
        for s in range(1, groups):
            give(s, k).wait_send()
        for n in range(7):
            stage(n, k, chip).wait_send()
    for s in range(groups):
        right, left = sends(s)
        for k in range(SPLIT):

            @pl.when(right)
            def _():
                pass_on(s, k, 1).wait_send()

            @pl.when(left)
            def _():
                pass_on(s, k, -1).wait_send()

    @pl.when(group < groups - 1)
    def _():
        tail.wait_send()

    @pl.when(group == groups - 1)
    def _():
        for g in range(groups - 1):
            gain_copy(g).wait_send()

    for j in range(3):
        cot_copies[j].wait_send()
        hid_copies[j].wait_send()
        part_copy(0, j).wait_send()
        part_copy(1, j).wait_send()
    for trade in trades:
        trade.wait_send()
    for i in range(2):
        rs_copy(i).wait_send()
    rs_last.wait_send()
    for g in range(groups):

        @pl.when(group != g)
        def _():
            z_copy(g).wait_send()

    for n in range(7):
        ag_copy(n).wait_send()
    for n in range(3):
        note_copy(n).wait_send()
    for d in range(1, groups):
        note_far(d).wait_send()

    @pl.when(group > 0)
    def _():
        head.wait_send()


def row_step(inputs, segment_row, cotangent, params, moment_one, moment_two, groups):
    length = inputs.shape[0]
    dma = pltpu.SemaphoreType.DMA
    f32, bf16 = jnp.float32, jnp.bfloat16
    full = (length, MODEL_WIDTH)
    panel_lanes = 8 * LANES
    four = (CHIPS * length, MODEL_WIDTH)
    units = (CHIPS * length, UNITS)
    half_units = UNITS // 2
    z = groups - 1
    bank = jax.ShapeDtypeStruct(params.shape, f32)
    flipped_row = jax.ShapeDtypeStruct(full[::-1], bf16)
    joint = pltpu.VMEM((MODEL_WIDTH, JOINT), bf16)
    gateup = pltpu.VMEM((2, MODEL_WIDTH, UNITS), bf16)
    down = pltpu.VMEM((UNITS, MODEL_WIDTH), bf16)
    cut_joint = pltpu.VMEM((MODEL_WIDTH, HALF_JOINT), bf16)
    cut_gateup = pltpu.VMEM((MODEL_WIDTH, UNITS), bf16)
    cut_down = pltpu.VMEM((half_units, MODEL_WIDTH), bf16)
    return pl.pallas_call(
        functools.partial(row_kernel, groups),
        out_shape=(
            flipped_row,
            flipped_row,
            jax.ShapeDtypeStruct((BLOCK_ROWS + 24, LANES), f32),
            jax.ShapeDtypeStruct((8, LANES), f32),
            bank, bank, bank,
        ),
        in_specs=vmem_specs(3) + [pl.BlockSpec(memory_space=pl.ANY)] * 3,
        out_specs=tuple(vmem_specs(7)),
        scratch_shapes=[
            joint, gateup, down,
            pltpu.VMEM((2, MODEL_WIDTH), f32),
            pltpu.VMEM((HEAD_ROWS + BLOCK_ROWS + 24, LANES), f32),
            pltpu.VMEM(params.shape, f32),
            pltpu.VMEM((8 * LANES + EXTRA,), f32),
            pltpu.VMEM((8, LANES), f32),
            pltpu.VMEM((16, LANES), f32),
            pltpu.VMEM((5 * half_units, LANES), f32),
            pltpu.VMEM((length, panel_lanes), bf16),
            pltpu.VMEM(full, bf16),
            pltpu.VMEM(full, f32),
            pltpu.VMEM((length, JOINT - QKV // LANES * LANES), bf16),
            pltpu.VMEM((length, panel_lanes), f32),
            pltpu.VMEM(four, bf16),
            pltpu.VMEM(four, bf16),
            pltpu.VMEM(units, bf16),
            pltpu.VMEM(units, bf16),
            pltpu.VMEM(units, bf16),
            pltpu.VMEM((2, 3) + full, bf16),
            pltpu.VMEM((2, 3) + full, bf16),
            joint, gateup, down,
            cut_joint, cut_gateup, cut_down,
            cut_joint, cut_gateup, cut_down,
            pltpu.VMEM((2, CHIP_ROWS, HALF_JOINT), bf16),
            pltpu.VMEM((CHIP_ROWS, HALF_JOINT), bf16),
            pltpu.VMEM((z, CHIP_ROWS, HALF_JOINT), bf16),
            pltpu.VMEM((z, HALF_WIDTH, UNITS), bf16),
            pltpu.VMEM((z, half_units, MODEL_WIDTH), bf16),
            pltpu.VMEM((8, PIECE_ROWS, LANES), bf16),
            pltpu.VMEM((7, 24, LANES), f32),
            pltpu.VMEM((groups, 24, LANES), f32),
            pltpu.VMEM((12 * CHIP_ROWS, LANES), f32),
            dma((4,)), dma, dma, dma((z,)), dma,
            dma((2, groups, SPLIT)), dma((groups, SPLIT)),
            dma((7, SPLIT)), dma((7, SPLIT)),
            dma((groups, SPLIT)), dma((groups, SPLIT)),
            dma((3,)), dma((3,)), dma((3,)), dma((3,)), dma((2, 3)), dma((2, 3)),
            dma((3,)), dma((3,)), dma((3,)), dma((2,)), dma((2,)), dma, dma,
            dma((groups,)), dma((z,)), dma((7,)), dma((7,)), dma((3,)), dma((3,)), dma((z,)), dma((z,)),
            dma, dma,
        ],
        compiler_params=params_of(4),
        name="row_step",
    )(inputs.T, segment_row[None], cotangent.T, params, moment_one, moment_two)


def adam_kernel(
    groups, flat, clip_ref, par_i, one_i, two_i, layer_out, layer_din,
    grads_out, params_out, one_out, two_out, out_ref, din_ref,
    grad_b, par_b, one_b, two_b, grad_t, par_t, one_t, two_t, out_sem, tout_sem, layer_sem,
):
    group = lax.axis_index("group")
    copies = [
        pltpu.make_async_copy(layer_out, out_ref, layer_sem.at[0]),
        pltpu.make_async_copy(layer_din, din_ref, layer_sem.at[1]),
    ]
    for copy in copies:
        copy.start()
    old = (par_i, one_i, two_i)

    def update(g, at, count, kept=0):
        lane = lanes_of(count)
        back, cut = 9 * g // 4, LANES - 32 * g
        grads = flat[pl.ds(at + back, count), :]
        if g:
            second = flat[pl.ds(at + back + 1, count), :]
            grads = jnp.where(lane < cut, pltpu.roll(grads, cut, 1), pltpu.roll(second, cut, 1))
        p, m1, m2 = [rows_at(ref, at, count, kept) for ref in old]
        clipped = grads * clip_ref[0:1, :]
        m1 = beta_one * m1 + (1.0 - beta_one) * clipped
        m2 = beta_two * m2 + (1.0 - beta_two) * clipped * clipped
        step_size = m1 * (1.0 / bias_one) / (jnp.sqrt(m2 * (1.0 / bias_two)) + adam_eps)
        if g == groups - 1:
            limit = BLOCK + EXTRA - 2 * MODEL_WIDTH
            place = (at + lax.broadcasted_iota(jnp.int32, (count, LANES), 0)) * LANES + lane
            decay = jnp.where(place < limit, decay_rate, 0.0)
        else:
            decay = decay_rate
        return grads, p - learn_rate * (step_size + decay * p), m1, m2

    outs = (grads_out, params_out, one_out, two_out)
    stores = (grad_b, par_b, one_b, two_b)
    ends = (grad_t, par_t, one_t, two_t)

    def out_copy(i, j):
        at = i * ADAM_ROWS
        return pltpu.make_async_copy(
            stores[j].at[pl.ds(at, ADAM_ROWS)].reshape(ADAM_ROWS * LANES),
            outs[j].at[pl.ds(at * LANES, ADAM_ROWS * LANES)],
            out_sem.at[i, j],
        )

    def tail_copy(j):
        return pltpu.make_async_copy(
            ends[j], outs[j].at[pl.ds(BLOCK, EXTRA)], tout_sem.at[j]
        )

    for i in range(ADAM_CHUNKS):
        for g in range(groups):

            @pl.when(group == g)
            def _():
                def body(k, _):
                    at = pl.multiple_of(i * ADAM_ROWS + k * ADAM_STEP, 8)
                    for store, value in zip(stores, update(g, at, ADAM_STEP)):
                        store[pl.ds(at, ADAM_STEP), :] = value
                    return 0

                lax.fori_loop(0, ADAM_ROWS // ADAM_STEP, body, 0)

        for j in range(4):
            out_copy(i, j).start()
    for g in range(groups):

        @pl.when(group == g)
        def _():
            for store, value in zip(ends, update(g, BLOCK_ROWS, 8, EXTRA)):
                store[...] = value.reshape(8 * LANES)[:EXTRA]

    for j in range(4):
        tail_copy(j).start()

    for i in range(ADAM_CHUNKS):
        for j in range(4):
            out_copy(i, j).wait()
    for j in range(4):
        tail_copy(j).wait()
    for copy in copies:
        copy.wait()


def adam(settled, outputs, d_inputs, groups, share_len):
    dma = pltpu.SemaphoreType.DMA
    f32 = jnp.float32
    bank = pltpu.VMEM((BLOCK_ROWS, LANES), f32)
    end = pltpu.VMEM((EXTRA,), f32)
    return pl.pallas_call(
        functools.partial(adam_kernel, groups),
        out_shape=(jax.ShapeDtypeStruct((share_len,), f32),) * 4
        + tuple(jax.ShapeDtypeStruct(a.shape, a.dtype) for a in (outputs, d_inputs)),
        in_specs=vmem_specs(7),
        out_specs=tuple([pl.BlockSpec(memory_space=pl.ANY)] * 6),
        scratch_shapes=[bank] * 4 + [end] * 4 + [dma((ADAM_CHUNKS, 4)), dma((4,)), dma((2,))],
        compiler_params=pltpu.CompilerParams(vmem_limit_bytes=60 * 2**20),
        name="adam",
    )(*settled, outputs, d_inputs)


def on_device(inputs, segments, cotangent, params, moment_one, moment_two):
    groups = lax.axis_size("group")
    wides = lax.axis_size("wide")
    group = lax.axis_index("group")
    count = wides.bit_length() - 1
    share_len = params.shape[0]
    gain_len = 2 * MODEL_WIDTH
    extra = gain_len // groups
    block_len = share_len - extra
    if groups == 4 and wides == 2 * CHIPS and block_len == BLOCK and inputs.shape[0] == 1:
        outputs, d_inputs, *settled = row_step(
            inputs[0], segments[0], cotangent[0], params, moment_one, moment_two, groups
        )
        *updated, outputs, d_inputs = adam(settled, outputs, d_inputs, groups, share_len)
        return (outputs.T[None], d_inputs.T[None], *updated)
    block_rows = block_len // LANES
    piece_rows = -(-block_rows // wides)
    chunks = 6 if piece_rows % 96 == 0 else 2
    piece_rows = -(-piece_rows // (16 * chunks)) * 16 * chunks
    padding = piece_rows * wides - block_rows
    lead = (2,) * count

    def to_pieces(rows):
        rows = rows.reshape(-1, block_rows, LANES)
        if padding:
            rows = jnp.pad(rows, ((0, 0), (0, padding), (0, 0)))
        return rows.reshape((-1,) + lead + (piece_rows, LANES))

    def from_pieces(pieces):
        rows = pieces.reshape(-1, piece_rows * wides, LANES)[:, :block_rows]
        return rows.reshape(-1, LANES)

    rounded = params.astype(jnp.bfloat16)
    tail = jnp.pad(rounded[share_len - gain_len :], (0, 16 * LANES - gain_len)).reshape(16, LANES)
    tails = gather_tails(tail, groups, 0).reshape(groups, -1)[:, :gain_len]
    before = lax.dynamic_index_in_dim(tails, (group + groups - 1) % groups, keepdims=False)
    joined = jnp.concatenate([before, rounded])
    block = lax.dynamic_slice(joined, (gain_len - extra * group,), (block_len,))
    flat_gains = tails[groups - 1]
    gathered = gather_blocks(to_pieces(block)[0], groups, count, chunks)
    weights = unpack(from_pieces(gathered), flat_gains)
    outputs, d_inputs, main, gains = layer_row(inputs[0], segments[0], cotangent[0], weights)
    gains = gains.astype(jnp.bfloat16).astype(jnp.float32)
    gains = jnp.pad(gains, (0, 16 * LANES - gain_len)).reshape(16, LANES)
    summed_block, head, gains, square = sum_blocks(to_pieces(main), gains, groups, count, chunks)
    gains = gains.reshape(-1)[:gain_len].astype(jnp.bfloat16)
    flat_block = from_pieces(summed_block).reshape(-1)
    head = head.reshape(-1)[:gain_len]
    head = jnp.where(group == groups - 1, gains, head)
    joined = jnp.concatenate([flat_block, head])
    summed = lax.dynamic_slice(joined, (extra * group,), (share_len,)).astype(jnp.float32)
    clip_factor = square[0, 0]
    flat_index = group * share_len + jnp.arange(share_len, dtype=jnp.int32)
    decay_mask = flat_index < share_len * groups - gain_len
    new_params, new_moment_one, new_moment_two = adam_update(
        summed, clip_factor, params, moment_one, moment_two, decay_mask
    )
    return (outputs[None], d_inputs[None], summed, new_params, new_moment_one, new_moment_two)


def solution(mesh):
    return jax.shard_map(
        on_device,
        mesh=mesh,
        in_specs=(
            P(("wide", "group"), None, None),
            P(("wide", "group"), None),
            P(("wide", "group"), None, None),
            P("group"),
            P("group"),
            P("group"),
        ),
        out_specs=(
            P(("wide", "group"), None, None),
            P(("wide", "group"), None, None),
            P("group"),
            P("group"),
            P("group"),
            P("group"),
        ),
        check_vma=False,
    )
```

```python
import functools
import math

import jax
import jax.numpy as jnp
from jax import lax
from jax.experimental import pallas as pl
from jax.experimental.pallas import tpu as pltpu
from jax.sharding import PartitionSpec as P

MESH = pl.DeviceIdType.MESH
LANES = 128

MODEL_WIDTH = 576
QUERY_HEADS = 9
KEY_VALUE_HEADS = 3
HEAD_SIZE = 64
FF = 1536


norm_eps = 1e-05
theta_base = 10000.0
masked_value = -1e30
beta_one = 0.9
beta_two = 0.95
bias_one = 0.19
bias_two = 0.0975
learn_rate = 0.03
decay_rate = 0.1
adam_eps = 1e-08
max_norm = 1.0


def contract(pattern, left_op, right_op):
    return jnp.einsum(pattern, left_op, right_op, preferred_element_type=jnp.float32)


def inner_rows(left_op, right_op):
    return lax.dot_general(
        left_op, right_op, (((0,), (0,)), ((), ())), preferred_element_type=jnp.float32
    )


def outer_column_count(left_op, right_op):
    return lax.dot_general(
        left_op, right_op, (((1,), (1,)), ((), ())), preferred_element_type=jnp.float32
    )


def unpack(main, gains):
    query_key_value_width = (QUERY_HEADS + 2 * KEY_VALUE_HEADS) * HEAD_SIZE
    shapes = [
        (MODEL_WIDTH, query_key_value_width),
        (QUERY_HEADS * HEAD_SIZE, MODEL_WIDTH),
        (MODEL_WIDTH, 2 * FF),
        (FF, MODEL_WIDTH),
    ]
    pieces = []
    offset = 0
    for piece_shape in shapes:
        extent = math.prod(piece_shape) // LANES
        pieces.append(main[offset : offset + extent].reshape(piece_shape))
        offset += extent
    return pieces + [gains[:MODEL_WIDTH], gains[MODEL_WIDTH:]]


def positions_of(segment_row):
    index_row = jnp.arange(segment_row.shape[0], dtype=jnp.int32)
    same = segment_row[:, None] == segment_row[None, :]
    before = index_row[:, None] > index_row[None, :]
    return jnp.sum((same & before).astype(jnp.int32), axis=1)


def rope_tables(positions):
    half_size = HEAD_SIZE // 2
    freqs = theta_base ** (-2.0 * jnp.arange(half_size, dtype=jnp.float32) / HEAD_SIZE)
    angles = positions.astype(jnp.float32)[:, None] * freqs[None, :]
    return (jnp.cos(angles)[:, None, :], jnp.sin(angles)[:, None, :])


def apply_rotation(vectors, cosine_lookup, sine_lookup):
    half_size = HEAD_SIZE // 2
    first_half = vectors[..., :half_size]
    second_half = vectors[..., half_size:]
    return jnp.concatenate(
        [
            first_half * cosine_lookup - second_half * sine_lookup,
            second_half * cosine_lookup + first_half * sine_lookup,
        ],
        axis=-1,
    )


def unrotate(vectors, cosine_lookup, sine_lookup):
    half_size = HEAD_SIZE // 2
    first_half = vectors[..., :half_size]
    second_half = vectors[..., half_size:]
    return jnp.concatenate(
        [
            first_half * cosine_lookup + second_half * sine_lookup,
            second_half * cosine_lookup - first_half * sine_lookup,
        ],
        axis=-1,
    )


def norm_back(d_hidden, normed, inverse, gain):
    d_normed = d_hidden * gain
    return inverse * (d_normed - normed * jnp.mean(d_normed * normed, axis=-1, keepdims=True))


def layer_row(inputs, segment_row, cotangent, weights):
    query_key_value_weight, output_weight, w_gateup, w_down, gain_attn, gain_ffn = weights
    sequence_length = inputs.shape[0]
    repeat_count = QUERY_HEADS // KEY_VALUE_HEADS
    scale_factor = HEAD_SIZE ** (-0.5)
    gain_one = gain_attn.astype(jnp.float32)
    gain_two = gain_ffn.astype(jnp.float32)
    resid_in = inputs.astype(jnp.float32)
    inv_attn = lax.rsqrt(jnp.mean(resid_in * resid_in, axis=-1, keepdims=True) + norm_eps)
    normed_attn = resid_in * inv_attn
    hidden_attn = (normed_attn * gain_one).astype(jnp.bfloat16)
    projected_output = jnp.dot(
        hidden_attn, query_key_value_weight, preferred_element_type=jnp.float32
    )
    cosine_lookup, sine_lookup = rope_tables(positions_of(segment_row))
    query_rows = projected_output[:, : QUERY_HEADS * HEAD_SIZE].reshape(
        sequence_length, QUERY_HEADS, HEAD_SIZE
    )
    key_matrix = projected_output[
        :, QUERY_HEADS * HEAD_SIZE : (QUERY_HEADS + KEY_VALUE_HEADS) * HEAD_SIZE
    ].reshape(sequence_length, KEY_VALUE_HEADS, HEAD_SIZE)
    query_rows_rotated = (
        apply_rotation(query_rows, cosine_lookup, sine_lookup)
        .astype(jnp.bfloat16)
        .reshape(sequence_length, KEY_VALUE_HEADS, repeat_count, HEAD_SIZE)
    )
    keys_rot = apply_rotation(key_matrix, cosine_lookup, sine_lookup).astype(jnp.bfloat16)
    value_rows = (
        projected_output[:, (QUERY_HEADS + KEY_VALUE_HEADS) * HEAD_SIZE :]
        .reshape(sequence_length, KEY_VALUE_HEADS, HEAD_SIZE)
        .astype(jnp.bfloat16)
    )
    index_row = jnp.arange(sequence_length)
    allowed = (segment_row[:, None] == segment_row[None, :]) & (
        index_row[:, None] >= index_row[None, :]
    )
    scores = contract("qgrd,kgd->grqk", query_rows_rotated, keys_rot) * scale_factor
    scores = jnp.where(allowed, scores, masked_value)
    peak = jnp.max(scores, axis=-1, keepdims=True)
    log_total = peak + jnp.log(jnp.sum(jnp.exp(scores - peak), axis=-1, keepdims=True))
    probs_b = jnp.exp(scores - log_total).astype(jnp.bfloat16)
    attended = (
        contract("grqk,kgd->qgrd", probs_b, value_rows)
        .astype(jnp.bfloat16)
        .reshape(sequence_length, QUERY_HEADS * HEAD_SIZE)
    )
    mid = resid_in + jnp.dot(attended, output_weight, preferred_element_type=jnp.float32)
    inv_ffn = lax.rsqrt(jnp.mean(mid * mid, axis=-1, keepdims=True) + norm_eps)
    normed_ffn = mid * inv_ffn
    hidden_ffn = (normed_ffn * gain_two).astype(jnp.bfloat16)
    gate_up = jnp.dot(hidden_ffn, w_gateup, preferred_element_type=jnp.float32)
    gate_pre = gate_up[:, :FF]
    upper = gate_up[:, FF:]
    sigmoid_gate = jax.nn.sigmoid(gate_pre)
    activation = (gate_pre * sigmoid_gate * upper).astype(jnp.bfloat16)
    outputs = (mid + jnp.dot(activation, w_down, preferred_element_type=jnp.float32)).astype(
        jnp.bfloat16
    )
    grad_down = inner_rows(activation, cotangent)
    d_act = outer_column_count(cotangent, w_down)
    d_gate = d_act * upper * sigmoid_gate * (1.0 + gate_pre * (1.0 - sigmoid_gate))
    d_upper = d_act * gate_pre * sigmoid_gate
    d_gate_up = jnp.concatenate([d_gate, d_upper], axis=-1).astype(jnp.bfloat16)
    grad_gateup = inner_rows(hidden_ffn, d_gate_up)
    d_hidden_ffn = outer_column_count(d_gate_up, w_gateup)
    grad_gain_ffn = jnp.sum(d_hidden_ffn * normed_ffn, axis=0)
    d_mid = cotangent.astype(jnp.float32) + norm_back(d_hidden_ffn, normed_ffn, inv_ffn, gain_two)
    grad_middle_batch = d_mid.astype(jnp.bfloat16)
    grad_out = inner_rows(attended, grad_middle_batch)
    grad_attended_rows = (
        outer_column_count(grad_middle_batch, output_weight)
        .astype(jnp.bfloat16)
        .reshape(sequence_length, KEY_VALUE_HEADS, repeat_count, HEAD_SIZE)
    )
    recomputed = contract("qgrd,kgd->grqk", query_rows_rotated, keys_rot) * scale_factor
    probs = jnp.exp(jnp.where(allowed, recomputed, masked_value) - log_total)
    d_probs = contract("qgrd,kgd->grqk", grad_attended_rows, value_rows)
    row_total = jnp.sum(probs * d_probs, axis=-1, keepdims=True)
    d_scores = (probs * (d_probs - row_total) * scale_factor).astype(jnp.bfloat16)
    grad_query_rows = contract("grqk,kgd->qgrd", d_scores, keys_rot).reshape(
        sequence_length, QUERY_HEADS, HEAD_SIZE
    )
    grad_key_rows = contract("grqk,qgrd->kgd", d_scores, query_rows_rotated)
    grad_value_rows = contract("grqk,qgrd->kgd", probs_b, grad_attended_rows)
    grad_query_rows = unrotate(grad_query_rows, cosine_lookup, sine_lookup)
    grad_key_rows = unrotate(grad_key_rows, cosine_lookup, sine_lookup)
    grad_projected_rows = jnp.concatenate(
        [
            grad_query_rows.reshape(sequence_length, QUERY_HEADS * HEAD_SIZE),
            grad_key_rows.reshape(sequence_length, KEY_VALUE_HEADS * HEAD_SIZE),
            grad_value_rows.reshape(sequence_length, KEY_VALUE_HEADS * HEAD_SIZE),
        ],
        axis=-1,
    ).astype(jnp.bfloat16)
    grad_qkv = inner_rows(hidden_attn, grad_projected_rows)
    d_hidden_attn = outer_column_count(grad_projected_rows, query_key_value_weight)
    grad_gain_attn = jnp.sum(d_hidden_attn * normed_attn, axis=0)
    d_inputs = (d_mid + norm_back(d_hidden_attn, normed_attn, inv_attn, gain_one)).astype(
        jnp.bfloat16
    )
    matrices = [grad_qkv, grad_out, grad_gateup, grad_down]
    main = jnp.concatenate([m.astype(jnp.bfloat16).reshape(-1, LANES) for m in matrices])
    gains = jnp.concatenate([grad_gain_attn, grad_gain_ffn])
    return (outputs, d_inputs, main, gains)


def adam_update(grads, clip_factor, params, moment_one, moment_two, decay_mask):
    clipped = grads * clip_factor
    new_moment_one = beta_one * moment_one + (1.0 - beta_one) * clipped
    new_moment_two = beta_two * moment_two + (1.0 - beta_two) * clipped * clipped
    step_size = new_moment_one / bias_one / (jnp.sqrt(new_moment_two / bias_two) + adam_eps)
    decay_term = jnp.where(decay_mask, decay_rate * params, jnp.zeros_like(params))
    new_params = params - learn_rate * (step_size + decay_term)
    return (new_params, new_moment_one, new_moment_two)


def my_bits(wide, count):
    return [(wide // 2**b) % 2 for b in range(count)]


def flipped(wide, bit, b):
    return wide + (1 - 2 * bit) * 2**b


def greet(wide, group, bits, groups):
    barrier = pltpu.get_barrier_semaphore()
    peers = [(flipped(wide, bit, b), group) for b, bit in enumerate(bits)]
    peers += [(wide, (group + d) % groups) for d in range(1, groups)]
    for peer in peers:
        pl.semaphore_signal(barrier, inc=1, device_id=peer, device_id_type=MESH)
    pl.semaphore_wait(barrier, len(peers))


def send(src, dst, send_sem, recv_sem, peer):
    copy = pltpu.make_async_remote_copy(
        src_ref=src,
        dst_ref=dst,
        send_sem=send_sem,
        recv_sem=recv_sem,
        device_id=peer,
        device_id_type=MESH,
    )
    copy.start()
    return copy


def bit_order(chunk, count):
    rest = list(range(1, count))
    return [0] + (rest if chunk % 2 == 0 else rest[::-1])


def tails_kernel(groups, bits_count, tail_ref, out_ref, send_sem, recv_sem):
    wide, group = lax.axis_index("wide"), lax.axis_index("group")
    greet(wide, group, [], groups)
    out_ref[pl.ds(group, 1)] = tail_ref[...][None]
    copies = []
    for d in range(1, groups):
        copies.append(
            send(
                tail_ref,
                out_ref.at[group],
                send_sem.at[d - 1],
                recv_sem.at[d - 1],
                (wide, (group + d) % groups),
            )
        )
    for copy in copies[3:]:
        copy.wait()


def gather_kernel(groups, count, chunks, block_ref, out_ref, own_sem, zs, zr, ws, wr):
    wide, group = lax.axis_index("wide"), lax.axis_index("group")
    bits = my_bits(wide, count)
    step = block_ref.shape[-2] // chunks
    greet(wide, group, bits, groups)

    def place(ref, lead, open_bits, chunk):
        index = [slice(None) if b in open_bits else bits[b] for b in reversed(range(count))]
        return ref.at[tuple(lead + index + [pl.ds(chunk * step, step)])]

    def copy(src, dst, send_sem, recv_sem, peer):
        return pltpu.make_async_remote_copy(
            src_ref=src,
            dst_ref=dst,
            send_sem=send_sem,
            recv_sem=recv_sem,
            device_id=peer,
            device_id_type=MESH,
        )

    def along(way, d, c):
        source = (group - way * (d - 1) + groups) % groups
        unit = (0 if way > 0 else groups - 1) + d - 1
        src = place(block_ref, [], [], c) if d == 1 else place(out_ref, [source], [], c)
        return copy(
            src,
            place(out_ref, [source], [], c),
            zs.at[unit, c],
            zr.at[unit, c],
            (wide, (group + way + groups) % groups),
        )

    def passes(way, d):
        ahead = group + way
        behind = group - way * (d - 1)
        return (ahead >= 0) & (ahead < groups) & (behind >= 0) & (behind < groups)

    def comes(way, d):
        behind = group - way * d
        return (behind >= 0) & (behind < groups)

    def across(way, d, c, stage):
        order = bit_order(c, count)[::-1]
        b = order[stage]
        source = (group - way * d + groups) % groups
        unit = (0 if way > 0 else groups - 1) + d - 1
        here = place(out_ref, [source], order[:stage], c)
        return copy(
            here,
            here,
            ws.at[unit, c, stage],
            wr.at[unit, c, stage],
            (flipped(wide, bits[b], b), group),
        )

    units = [(d, c) for d in range(1, groups) for c in range(chunks)]
    for c in range(chunks):
        for way in (1, -1):

            @pl.when(passes(way, 1))
            def _():
                along(way, 1, c).start()

    own = pltpu.make_async_copy(block_ref, out_ref.at[group], own_sem)
    own.start()
    for tick in range(len(units) // 2 + count + 1):
        for u, (d, c) in reversed(list(enumerate(units))):
            stage = tick - u // 2
            if not 0 <= stage <= count:
                continue
            for way in (1, -1):

                @pl.when(comes(way, d))
                def _():
                    if stage == 0:
                        along(way, d, c).wait_recv()
                    else:
                        across(way, d, c, stage - 1).wait_recv()
                    if stage < count:
                        across(way, d, c, stage).start()

                if stage == 0 and d + 1 < groups:

                    @pl.when(passes(way, d + 1))
                    def _():
                        along(way, d + 1, c).start()

    for way in (1, -1):
        for d, c in units:

            @pl.when(passes(way, d))
            def _():
                along(way, d, c).wait_send()

            @pl.when(comes(way, d))
            def _():
                for stage in range(count):
                    across(way, d, c, stage).wait_send()

    own.wait()


def sum_kernel(groups, count, chunks, x_ref, gain_ref, out_ref, head_ref, gsum_ref, sq_ref, *scratch):
    recvs, accs = scratch[:count], scratch[count : 2 * count]
    recv_z, gain_w, gain_z, sq_z, piece_head = scratch[2 * count : 2 * count + 5]
    ss, sr, zs, zr, gs, gr, xs, xr, gzs, gzr, qs, qr, hs, hr = scratch[2 * count + 5 :]
    wide, group = lax.axis_index("wide"), lax.axis_index("group")
    bits = my_bits(wide, count)
    step = x_ref.shape[-2] // chunks
    greet(wide, group, bits, groups)
    copies = {}
    f32 = jnp.float32

    def partner(b):
        return (flipped(wide, bits[b], b), group)

    def part(c, stage, value):
        order = bit_order(c, count)
        left = sorted(order[stage:], reverse=True)
        return [value if b == order[stage] else slice(None) for b in left]

    def held(c, stage):
        return x_ref if stage == 0 else accs[stage - 1].at[c]

    def view(c, stage, flip):
        b = bit_order(c, count)[stage]
        index = [slice(None)] + part(c, stage, 1 - bits[b] if flip else bits[b])
        if stage == 0:
            index += [slice(None)] * (count + 2 - len(index) - 1)
            return x_ref.at[tuple(index + [pl.ds(c * step, step)])]
        return accs[stage - 1].at[tuple([c] + index)]

    def start_scatter(c, stage):
        b = bit_order(c, count)[stage]
        copies["s", c, stage] = send(
            view(c, stage, True), recvs[stage].at[c], ss.at[c, stage], sr.at[c, stage], partner(b)
        )

    def add_scatter(c, stage):
        copies["s", c, stage].wait_recv()
        mine, other, total = view(c, stage, False), recvs[stage].at[c], accs[stage].at[c]

        def body(i, _):
            total[i] = (mine[i].astype(f32) + other[i].astype(f32)).astype(jnp.bfloat16)
            return 0

        lax.fori_loop(0, groups, body, 0)

    def start_groups(c):
        for d in range(1, groups):
            to = (group + d) % groups
            copies["z", c, d] = send(
                accs[-1].at[c, to],
                recv_z.at[c, d - 1],
                zs.at[c, d - 1],
                zr.at[c, d - 1],
                (wide, to),
            )

    def place(open_bits, c):
        index = [slice(None) if b in open_bits else bits[b] for b in reversed(range(count))]
        return out_ref.at[tuple(index + [pl.ds(c * step, step)])]

    def add_groups(c):
        total = accs[-1][c, group].astype(f32)
        for d in range(1, groups):
            copies["z", c, d].wait_recv()
            total = total + recv_z[c, d - 1].astype(f32)
        place([], c)[...] = total.astype(jnp.bfloat16)

    def start_gather(c, stage):
        order = bit_order(c, count)[::-1]
        here = place(order[:stage], c)
        copies["g", c, stage] = send(
            here, here, gs.at[c, stage], gr.at[c, stage], partner(order[stage])
        )

    for c in range(chunks):
        start_scatter(c, 0)
    gain_w[0] = gain_ref[...]
    copies["x", 0] = send(gain_w.at[0], gain_w.at[count + 1], xs.at[0], xr.at[0], partner(0))

    for tick in range(chunks // 2 + 2 * count + 1):
        for c in reversed(range(chunks)):
            s = tick - c // 2
            if 0 <= s < count:
                add_scatter(c, s)
                if s + 1 < count:
                    start_scatter(c, s + 1)
                else:
                    start_groups(c)
            elif s == count:
                add_groups(c)
                start_gather(c, 0)
            elif count < s <= 2 * count:
                copies["g", c, s - count - 1].wait_recv()
                if s < 2 * count:
                    start_gather(c, s - count)
        if tick < count:
            copies["x", tick].wait_recv()
            gain_w[tick + 1] = gain_w[tick] + gain_w[count + 1 + tick]
            if tick + 1 < count:
                copies["x", tick + 1] = send(
                    gain_w.at[tick + 1],
                    gain_w.at[count + 2 + tick],
                    xs.at[tick + 1],
                    xr.at[tick + 1],
                    partner(tick + 1),
                )
            else:
                gain_z[pl.ds(group, 1)] = gain_w[pl.ds(count, 1)]
                for d in range(1, groups):
                    copies["gz", d] = send(
                        gain_w.at[count],
                        gain_z.at[group],
                        gzs.at[d - 1],
                        gzr.at[d - 1],
                        (wide, (group + d) % groups),
                    )

    first = tuple([0] * count + [pl.ds(0, 16)])
    copies["h"] = send(out_ref.at[first], head_ref, hs, hr, (wide, (group + groups - 1) % groups))
    flat_lead = out_ref.shape[:-2]

    def squares(i, total):
        index = tuple((i // 2**b) % 2 for b in reversed(range(len(flat_lead))))
        value = out_ref[index].astype(f32)
        value = value * value
        return total + jnp.sum(value.reshape(-1, 8, LANES), axis=0)

    square = lax.fori_loop(0, math.prod(flat_lead), squares, jnp.zeros((8, LANES), f32))
    piece_head[...] = square
    sq_z[pl.ds(group, 1)] = square[None]
    for d in range(1, groups):
        copies["q", d] = send(
            piece_head, sq_z.at[group], qs.at[d - 1], qr.at[d - 1], (wide, (group + d) % groups)
        )
    for d in range(1, groups):
        copies["gz", d].wait_recv()
    gains = gain_z[0]
    for d in range(1, groups):
        gains = gains + gain_z[d]
    gains = gains.astype(jnp.bfloat16).astype(f32)
    gsum_ref[...] = gains
    for d in range(1, groups):
        copies["q", d].wait_recv()
    square = sq_z[0]
    for d in range(1, groups):
        square = square + sq_z[d]
    square = square + jnp.sum((gains * gains).reshape(-1, 8, LANES), axis=0)
    total = jnp.sum(jnp.sum(square, axis=-1, keepdims=True), axis=0, keepdims=True)
    clip = jnp.minimum(jnp.float32(1.0), max_norm * lax.rsqrt(total))
    sq_ref[...] = jnp.broadcast_to(clip, sq_ref.shape)
    copies["h"].wait_recv()
    for copy in copies.values():
        copy.wait_send()


def params_of(identity):
    return pltpu.CompilerParams(
        collective_id=identity, has_side_effects=True, vmem_limit_bytes=60 * 2**20
    )


def vmem_specs(n):
    return [pl.BlockSpec(memory_space=pltpu.VMEM)] * n


def gather_tails(tail, groups, identity):
    dma = pltpu.SemaphoreType.DMA
    return pl.pallas_call(
        functools.partial(tails_kernel, groups, 0),
        out_shape=jax.ShapeDtypeStruct((groups,) + tail.shape, tail.dtype),
        in_specs=vmem_specs(1),
        out_specs=vmem_specs(1)[0],
        scratch_shapes=[dma((groups - 1,)), dma((groups - 1,))],
        compiler_params=params_of(identity),
        name="tails",
    )(tail)


def gather_blocks(block, groups, count, chunks):
    dma = pltpu.SemaphoreType.DMA
    units = 2 * (groups - 1)
    return pl.pallas_call(
        functools.partial(gather_kernel, groups, count, chunks),
        out_shape=jax.ShapeDtypeStruct((groups,) + block.shape, block.dtype),
        in_specs=vmem_specs(1),
        out_specs=vmem_specs(1)[0],
        scratch_shapes=[
            dma,
            dma((units, chunks)),
            dma((units, chunks)),
            dma((units, chunks, count)),
            dma((units, chunks, count)),
        ],
        compiler_params=params_of(1),
        name="gather_weights",
    )(block)


def sum_blocks(main, gains, groups, count, chunks):
    dma = pltpu.SemaphoreType.DMA
    rows = main.shape[-2]
    step = rows // chunks
    bf16, f32 = jnp.bfloat16, jnp.float32
    stages = [
        pltpu.VMEM((chunks, groups) + (2,) * (count - 1 - k) + (step, LANES), bf16)
        for k in range(count)
    ]
    return pl.pallas_call(
        functools.partial(sum_kernel, groups, count, chunks),
        out_shape=(
            jax.ShapeDtypeStruct((2,) * count + (rows, LANES), bf16),
            jax.ShapeDtypeStruct((16, LANES), bf16),
            jax.ShapeDtypeStruct(gains.shape, f32),
            jax.ShapeDtypeStruct((8, LANES), f32),
        ),
        in_specs=vmem_specs(2),
        out_specs=tuple(vmem_specs(4)),
        scratch_shapes=stages
        + stages
        + [
            pltpu.VMEM((chunks, groups - 1, step, LANES), bf16),
            pltpu.VMEM((2 * count + 1,) + gains.shape, f32),
            pltpu.VMEM((groups,) + gains.shape, f32),
            pltpu.VMEM((groups, 8, LANES), f32),
            pltpu.VMEM((8, LANES), f32),
        ]
        + [dma((chunks, count))] * 2
        + [dma((chunks, groups - 1))] * 2
        + [dma((chunks, count))] * 2
        + [dma((count,))] * 2
        + [dma((groups - 1,))] * 4
        + [dma, dma],
        compiler_params=params_of(2),
        name="sum_grads",
    )(main, gains)


def dot(left_op, right_op, left_dim, right_dim):
    return lax.dot_general(
        left_op,
        right_op,
        (((left_dim,), (right_dim,)), ((), ())),
        preferred_element_type=jnp.float32,
    )


def cores_of(wide):
    core, x_bit, y_bit = wide % 2, (wide // 2) % 2, (wide // 4) % 2
    over_x, over_y = wide + (1 - 2 * x_bit) * 2, wide + (1 - 2 * y_bit) * 4
    one = over_x * (1 - core) + over_y * core
    two = over_y * (1 - core) + over_x * core
    far = over_x + over_y - wide
    twin = wide + 1 - 2 * core
    return core, over_x, over_y, far, one, two, twin


def greet_all(peers):
    barrier = pltpu.get_barrier_semaphore()
    for peer in peers:
        pl.semaphore_signal(barrier, inc=1, device_id=peer, device_id_type=MESH)
    pl.semaphore_wait(barrier, len(peers))


def remote(src, dst, send_sem, recv_sem, peer):
    return pltpu.make_async_remote_copy(
        src_ref=src,
        dst_ref=dst,
        send_sem=send_sem,
        recv_sem=recv_sem,
        device_id=peer,
        device_id_type=MESH,
    )


QKV = (QUERY_HEADS + 2 * KEY_VALUE_HEADS) * HEAD_SIZE
INNER = QUERY_HEADS * HEAD_SIZE
JOINT = QKV + INNER
HALF_JOINT = JOINT // 2
CHIPS = 4
CHIP_ROWS = MODEL_WIDTH // CHIPS
UNITS = FF // CHIPS
HALF_WIDTH = MODEL_WIDTH // 2
SPLIT = 3
SUB = CHIP_ROWS // SPLIT
BLOCK = MODEL_WIDTH * FF
BLOCK_ROWS = BLOCK // LANES
EXTRA = 2 * MODEL_WIDTH // 4
HEAD_ROWS = 8


def lanes_of(rows):
    return lax.broadcasted_iota(jnp.int32, (rows, LANES), 1)


def rows_at(ref, at, count, kept=0):
    if kept:
        value = ref[pl.ds(at * LANES, kept)]
        value = jnp.concatenate([value, jnp.zeros((count * LANES - kept,), value.dtype)])
    else:
        value = ref[pl.ds(pl.multiple_of(at * LANES, 1024), count * LANES)]
    return value.reshape(count, LANES)


ADAM_CHUNKS = 8
ADAM_ROWS = BLOCK_ROWS // ADAM_CHUNKS
PIECE_ROWS = BLOCK_ROWS // 8
PART_ROWS = PIECE_ROWS // SPLIT
ROW_VMEM = 60 * 2**20
ADAM_VMEM = 60 * 2**20


def row_kernel(
    groups, x_ref, seg_ref, cot_ref, params_ref,
    out_ref, din_ref, flat, clip_ref,
    joint_ref, gu_ref, down_ref, gain_w, raw, lin, lin_t, tail_s, gain_s, pan_w,
    proj_s, att_s, mid_s, dmid_s, dproj_s, cots, hids, act_s, gate_s, up_s, part_s, part_r,
    gj_ref, ggu_ref, gdn_ref, core_j, core_g, core_d, acc_j, acc_g, acc_d,
    rs_one, rs_two, z_j, z_g, z_d, ag, note, note_z, pan,
    raw_sem, ts, tr, gns, gnr, wzs, wzr, as_, ar, es, er,
    cs, cr, hs, hr, ps, pr,
    sws, swr, r1s, r1r, r2s, r2r, zs, zr, zjs, zjr, ags, agr, ns, nr, nzs, nzr, hds, hdr,
):
    f32, bf16 = jnp.float32, jnp.bfloat16
    wide, group = lax.axis_index("wide"), lax.axis_index("group")
    core, over_x, over_y, far, one, two, twin = cores_of(wide)
    chip = wide // 2
    whole = pltpu.make_async_copy(params_ref, lin, raw_sem.at[0])

    def part_load(i, at, count):
        here = pl.ds(pl.multiple_of(at * LANES, 1024), count * LANES)
        return pltpu.make_async_copy(params_ref.at[here], lin.at[here], raw_sem.at[i])

    qkv_rows, out_rows = BLOCK_ROWS * QKV // JOINT // CHIPS, BLOCK_ROWS * INNER // JOINT // CHIPS
    qkv_from, out_from_row = qkv_rows * chip, CHIPS * qkv_rows + out_rows * chip
    load_qkv, load_out = part_load(1, qkv_from, qkv_rows), part_load(2, out_from_row, out_rows)

    load_end = pltpu.make_async_copy(
        params_ref.at[pl.ds(BLOCK - 8 * LANES, 8 * LANES + EXTRA)], lin_t, raw_sem.at[3]
    )

    @pl.when(group == 0)
    def _():
        load_qkv.start()
        load_out.start()
        load_end.start()

    @pl.when(group > 0)
    def _():
        whole.start()

    peers = [(p, group) for p in (over_x, over_y, far, twin)]
    peers += [(wide, (group + d) % groups) for d in range(1, groups)]
    near = peers[:3]
    greet_all(peers)
    width, length, half = MODEL_WIDTH, x_ref.shape[1], HEAD_SIZE // 2
    turn_rate = -2.0 * math.log(theta_base) / HEAD_SIZE
    heads, kv = QUERY_HEADS, KEY_VALUE_HEADS
    repeat = heads // kv
    scale = HEAD_SIZE**-0.5
    def block(ref, j):
        return ref.at[pl.ds(j * length, length)]

    cots[0:length, :] = cot_ref[...].astype(f32).T.astype(bf16)
    cot_copies = [
        remote(block(cots, 0), block(cots, j + 1), cs.at[j], cr.at[j], near[j]) for j in range(3)
    ]
    for copy in cot_copies:
        copy.start()


    copy_rows = 216

    def unroll(start, count):
        def step(i, _):
            at = start + i * copy_rows
            raw[pl.ds(pl.multiple_of(HEAD_ROWS + at, 8), copy_rows), :] = rows_at(lin, at, copy_rows)
            return 0

        lax.fori_loop(0, count // copy_rows, step, 0)

    @pl.when(group == 0)
    def _():
        load_qkv.wait()
        unroll(qkv_from, qkv_rows)
        load_out.wait()
        unroll(out_from_row, out_rows)
        load_end.wait()
        at = HEAD_ROWS + BLOCK_ROWS
        raw[at - 8 : at, :] = rows_at(lin_t, 0, 8)
        raw[at : at + 8, :] = rows_at(lin_t, 8, 8, EXTRA)

    @pl.when(group > 0)
    def _():
        whole.wait()
        unroll(0, BLOCK_ROWS)
        raw[pl.ds(HEAD_ROWS + BLOCK_ROWS, 8), :] = rows_at(lin, BLOCK_ROWS, 8, EXTRA)

    def joined(first, second, shift, cut):
        lane = lanes_of(first.shape[0])
        return jnp.where(lane < cut, pltpu.roll(first, shift, 1), pltpu.roll(second, shift, 1))

    tail = remote(tail_s, raw.at[pl.ds(0, HEAD_ROWS)], ts, tr, (wide, (group + 1) % groups))
    top = HEAD_ROWS + BLOCK_ROWS + 2

    @pl.when(group < groups - 1)
    def _():
        at = top - HEAD_ROWS
        tail_s[...] = joined(raw[at : at + 8, :], raw[at + 1 : at + 9, :], 96, 96)
        tail.start()

    def gain_copy(g):
        return remote(gain_s, gain_s, gns.at[g], gnr, (wide, g))

    @pl.when(group == groups - 1)
    def _():
        at = top - 9
        gain_s[...] = joined(raw[at : at + 16, :], raw[at + 1 : at + 17, :], 96, 96)
        for g in range(groups - 1):
            gain_copy(g).start()

    @pl.when(group > 0)
    def _():
        tail.wait_recv()

    def take(start, count, stride):
        return raw[pl.ds(start, count, stride), :]

    pairs = CHIP_ROWS // 2

    def put_joint(p, even, odd):
        pan_w[pl.ds(p % 6 * CHIP_ROWS, pairs, 2), :] = even
        pan_w[pl.ds(p % 6 * CHIP_ROWS + 1, pairs, 2), :] = odd
        joint_ref[pl.ds(pl.multiple_of(CHIP_ROWS * chip, 16), CHIP_ROWS), p * LANES : (p + 1) * LANES] = pan_w[
            p % 6 * CHIP_ROWS : (p % 6 + 1) * CHIP_ROWS, :
        ].astype(bf16)

    qkv_at = HEAD_ROWS + 1080 * chip
    out_at = HEAD_ROWS + 4320 + 648 * chip

    def qkv(k):
        return take(qkv_at + k, pairs, 15)

    def out(k):
        return take(out_at + k, pairs, 9)

    @pl.when((group == 0) & (core == 0))
    def _():
        for p in range(6):
            put_joint(p, qkv(p), joined(qkv(7 + p), qkv(8 + p), 64, 64))

    @pl.when((group == 0) & (core == 1))
    def _():
        put_joint(6, qkv(6), joined(qkv(13), qkv(14), 64, 64))
        lane = lanes_of(pairs)
        put_joint(
            7,
            jnp.where(lane < 64, qkv(7), pltpu.roll(out(0), 64, 1)),
            jnp.where(lane < 64, pltpu.roll(qkv(14), 64, 1), out(4)),
        )
        for k in range(4):
            put_joint(8 + k, joined(out(k), out(k + 1), 64, 64), out(5 + k))

    for g, back, shift in ((1, 3, 32), (2, 5, 64)):

        @pl.when(group == g)
        def _():
            for j in range(3):
                at = HEAD_ROWS - back + 12 * core + 3 * chip + j
                value = joined(take(at, HALF_WIDTH, 24), take(at + 1, HALF_WIDTH, 24), shift, shift)
                gu_ref[core, (g - 1) * HALF_WIDTH : g * HALF_WIDTH, j * LANES : (j + 1) * LANES] = value.astype(bf16)

    half_units = UNITS // 2

    @pl.when(group == 3)
    def _():
        rows = pl.ds(pl.multiple_of(half_units * core, 16), half_units)
        count = half_units // 2
        for p in range(5):
            at = HEAD_ROWS + 864 * wide + p
            even = joined(take(at - 7, count, 9), take(at - 6, count, 9), 96, 96)
            odd = joined(take(at - 3, count, 9), take(at - 2, count, 9), 32, 32)
            pan_w[pl.ds(p * half_units, count, 2), :] = even
            pan_w[pl.ds(p * half_units + 1, count, 2), :] = odd
            value = pan_w[p * half_units : (p + 1) * half_units, :].astype(bf16)
            if p < 4:
                down_ref[rows, p * LANES : (p + 1) * LANES] = value
            else:
                down_ref[rows, p * LANES : MODEL_WIDTH] = value[:, : MODEL_WIDTH - p * LANES]

    def attn_at(q, c, k):
        return joint_ref.at[
            pl.ds(pl.multiple_of(CHIP_ROWS * q + SUB * k, 16), SUB),
            pl.ds(pl.multiple_of(HALF_JOINT * c, LANES), HALF_JOINT),
        ]

    def piece(s, k):
        if s == 0:
            return attn_at(chip, core, k)
        if s < 3:
            step = HALF_WIDTH // SPLIT
            return gu_ref.at[core, pl.ds((s - 1) * HALF_WIDTH + k * step, step)]
        step = half_units // SPLIT
        return down_ref.at[pl.ds(pl.multiple_of(half_units * core + k * step, 16), step)]

    def pass_on(s, k, way):
        to = (wide, (group + way + groups) % groups)
        return remote(piece(s, k), piece(s, k), wzs.at[(way + 1) // 2, s, k], wzr.at[s, k], to)

    def sends(s):
        right = (group >= s) & (group < groups - 1)
        left = (group <= s) & (group > 0)
        return right, left

    def forward(s, k):
        right, left = sends(s)

        @pl.when(right)
        def _():
            pass_on(s, k, 1).start()

        @pl.when(left)
        def _():
            pass_on(s, k, -1).start()

    def give(s, k):
        return remote(piece(s, k), piece(s, k), es.at[s, k], er.at[s, k], (twin, group))

    for s in range(groups):

        @pl.when(group == s)
        def _():
            for k in range(SPLIT):
                if s == 0:
                    pass_on(s, k, 1).start()
                else:
                    pass_on(s, k, -1).start()
                    give(s, k).start()

    q_one, q_two = one // 2, two // 2
    q_far = 3 - chip

    def stage(n, k, q):
        peer = (one, two, two, twin, twin, twin, twin)[n]
        return remote(attn_at(q, core, k), attn_at(q, core, k), as_.at[n, k], ar.at[n, k], (peer, group))

    for k in range(SPLIT):

        @pl.when(group > 0)
        def _():
            pass_on(0, k, 1).wait_recv()
            forward(0, k)

        stage(0, k, chip).start()
        stage(1, k, chip).start()
        stage(3, k, chip).start()

    for s in range(1, groups - 1):

        @pl.when(group == s)
        def _():
            for k in range(SPLIT):
                pass_on(s, k, 1).start()

    def relay(s, g):
        @pl.when(group == g)
        def _():
            for k in range(SPLIT):
                pass_on(s, k, 1).wait_recv()
                forward(s, k)
                give(s, k).start()

    for s in (1, 2, 3):
        relay(s, s - 1)
    @pl.when(group < groups - 1)
    def _():
        gain_copy(0).wait_recv()

    gains = gain_s[...].astype(bf16).astype(f32)
    for k in range(4):
        gain_w[0:1, k * LANES : (k + 1) * LANES] = gains[k : k + 1]
    gain_w[0:1, 4 * LANES : MODEL_WIDTH] = gains[4:5, : MODEL_WIDTH - 4 * LANES]
    turned = pltpu.roll(gains, 64, 1)
    lane = lanes_of(1)
    for k in range(4):
        gain_w[1:2, k * LANES : (k + 1) * LANES] = jnp.where(lane < 64, turned[4 + k : 5 + k], turned[5 + k : 6 + k])
    gain_w[1:2, 4 * LANES : MODEL_WIDTH] = turned[8:9, : MODEL_WIDTH - 4 * LANES]

    gain_one, gain_two = gain_w[0:1, :], gain_w[1:2, :]
    x = x_ref[...].astype(f32).T
    inv_attn = lax.rsqrt(jnp.mean(x * x, axis=-1, keepdims=True) + norm_eps)
    normed_attn = x * inv_attn
    hidden_attn = (normed_attn * gain_one).astype(bf16)

    seg_row = jnp.broadcast_to(seg_ref[...].astype(f32), (length, length))
    rows = lax.broadcasted_iota(jnp.int32, (length, length), 0)
    columns = lax.broadcasted_iota(jnp.int32, (length, length), 1)
    allowed = (seg_row == seg_row.T) & (rows >= columns)
    positions = jnp.sum(jnp.where(allowed, 1.0, 0.0), axis=-1, keepdims=True) - 1.0
    angles = positions * jnp.exp(turn_rate * (lanes_of(1) % half).astype(f32))
    lane = lax.broadcasted_iota(jnp.int32, (length, LANES), 1)
    first = lane % HEAD_SIZE < half
    cosine, sine = jnp.cos(angles), jnp.sin(angles)
    sine = jnp.where(first, -sine, sine)

    def swap(u):
        return jnp.where(first, pltpu.roll(u, LANES - half, 1), pltpu.roll(u, half, 1))

    for k in range(SPLIT):
        stage(0, k, q_one).wait_recv()
        stage(2, k, q_one).start()
        stage(4, k, q_one).start()
    for k in range(SPLIT):
        stage(1, k, q_two).wait_recv()
        stage(5, k, q_two).start()
    for s in (2, 3):
        relay(s, s - 2)
    for k in range(SPLIT):
        stage(2, k, q_far).wait_recv()
        stage(6, k, q_far).start()
    for s in (1, 2):
        relay(s, s + 1)
    for k in range(SPLIT):
        for n in range(3, 7):
            stage(n, k, chip).wait_recv()

    panels = 8
    turned_panels = (heads + kv) * HEAD_SIZE // LANES
    wide_qkv = panels * LANES
    for p in range(0, panels, 2):
        both = dot(hidden_attn, joint_ref[:, p * LANES : (p + 2) * LANES], 1, 0)
        for q in (p, p + 1):
            u = both[:, (q - p) * LANES : (q - p + 1) * LANES]
            if q < turned_panels:
                u = u * cosine + swap(u) * sine
            proj_s[:, q * LANES : (q + 1) * LANES] = u.astype(bf16)

    def slot(s):
        return proj_s[:, s * HEAD_SIZE : (s + 1) * HEAD_SIZE]

    mask = jnp.concatenate([allowed] * repeat, axis=0)
    saved = []
    for j in range(kv):
        queries = jnp.concatenate([slot(repeat * j + r) for r in range(repeat)], axis=0)
        keys, values = slot(heads + j), slot(heads + kv + j)
        scores = jnp.where(mask, dot(queries, keys, 1, 1) * scale, masked_value)
        peak = jnp.max(scores, axis=-1, keepdims=True)
        raised = jnp.exp(scores - peak)
        probs = raised * (1.0 / jnp.sum(raised, axis=-1, keepdims=True))
        probs_b = probs.astype(bf16)
        attended = dot(probs_b, values, 1, 0)
        for r in range(repeat):
            at = (repeat * j + r) * HEAD_SIZE
            att_s[:, at : at + HEAD_SIZE] = attended[r * length : (r + 1) * length].astype(bf16)
        saved.append((queries, keys, values, probs, probs_b))

    out_from = QKV // LANES * LANES
    shift = QKV - out_from
    w_out = joint_ref.at[:, out_from:JOINT]
    mid = x + dot(att_s[...], w_out[...], 1, 0)[:, shift:]
    inv_ffn = lax.rsqrt(jnp.mean(mid * mid, axis=-1, keepdims=True) + norm_eps)
    normed_ffn = mid * inv_ffn
    hids[0:length, :] = (normed_ffn * gain_two).astype(bf16)
    hid_copies = [
        remote(block(hids, 0), block(hids, j + 1), hs.at[j], hr.at[j], near[j]) for j in range(3)
    ]
    for copy in hid_copies:
        copy.start()
    mid_s[...] = mid

    relay(3, 0)
    relay(1, 3)
    for k in range(SPLIT):
        for s in range(1, groups):
            give(s, k).wait_recv()

    def feed(j):
        at = slice(j * length, (j + 1) * length)
        hidden, cotangent = hids[at, :], cots[at, :]
        gate, upper = dot(hidden, gu_ref[0], 1, 0), dot(hidden, gu_ref[1], 1, 0)
        d_act = dot(cotangent, down_ref[...], 1, 1)
        sigmoid = jax.nn.sigmoid(gate)
        activation = (gate * sigmoid * upper).astype(bf16)
        d_gate = (d_act * upper * sigmoid * (1.0 + gate * (1.0 - sigmoid))).astype(bf16)
        d_upper = (d_act * gate * sigmoid).astype(bf16)
        act_s[at, :], gate_s[at, :], up_s[at, :] = activation, d_gate, d_upper
        d_hidden = dot(d_gate, gu_ref[0], 1, 1) + dot(d_upper, gu_ref[1], 1, 1)
        return d_hidden, dot(activation, down_ref[...], 1, 0)

    def part_copy(n, j):
        return remote(part_s.at[n, j], part_r.at[n, j], ps.at[n, j], pr.at[n, j], near[j])

    d_hidden, out_own = feed(0)
    for j in range(3):
        cot_copies[j].wait_recv()
        hid_copies[j].wait_recv()
        d_part, out_part = feed(j + 1)
        part_s[0, j] = d_part.astype(bf16)
        part_copy(0, j).start()
        part_s[1, j] = out_part.astype(bf16)

    ggu_ref[0] = dot(hids[...], gate_s[...], 0, 0).astype(bf16)
    ggu_ref[1] = dot(hids[...], up_s[...], 0, 0).astype(bf16)
    gdn_ref[...] = dot(act_s[...], cots[...], 0, 0).astype(bf16)

    half_units = UNITS // 2
    other = 1 - core

    def half_cols(c):
        return pl.ds(pl.multiple_of(HALF_JOINT * c, LANES), HALF_JOINT)

    def half_rows(c):
        return pl.ds(pl.multiple_of(half_units * c, 16), half_units)

    def chip_rows(q):
        return pl.ds(pl.multiple_of(CHIP_ROWS * q, 16), CHIP_ROWS)

    trades = [
        remote(ggu_ref.at[other], core_g, sws.at[0], swr.at[0], (twin, group)),
        remote(gdn_ref.at[half_rows(other)], core_d, sws.at[1], swr.at[1], (twin, group)),
        remote(gj_ref.at[:, half_cols(other)], core_j, sws.at[2], swr.at[2], (twin, group)),
    ]
    for trade in trades[:2]:
        trade.start()
    def add_rows(count, step, total, mine, theirs):
        def body(i, _):
            at = pl.ds(pl.multiple_of(i * step, 16), step)
            total(at, mine(at).astype(f32) + theirs(at).astype(f32))
            return 0

        lax.fori_loop(0, count // step, body, 0)

    def into(ref):
        def put(at, value):
            ref[at, :] = value.astype(bf16)

        return put

    def z_source(g):
        if g == 0:
            return acc_j.at[chip_rows(chip)], z_j
        if g < 3:
            return acc_g.at[pl.ds((g - 1) * HALF_WIDTH, HALF_WIDTH)], z_g
        return acc_d, z_d

    def z_copy(g):
        source, target = z_source(g)
        place = (group - g + groups) % groups
        at = (place + groups - 1) % groups
        return remote(source, target.at[at], zs.at[g], zr.at[at], (wide, g))

    def z_send(g):
        @pl.when(group != g)
        def _():
            z_copy(g).start()

    def sub_rows(q, k):
        return pl.ds(pl.multiple_of(CHIP_ROWS * q + SUB * k, 16), SUB)

    def z_part(k, at):
        return remote(
            acc_j.at[sub_rows(chip, k)],
            z_j.at[at, pl.ds(SUB * k, SUB)],
            zjs.at[k],
            zjr.at[at, k],
            (wide, 0),
        )

    trades[0].wait_recv()
    add_rows(MODEL_WIDTH, 192, into(acc_g), lambda at: ggu_ref[core, at, :], lambda at: core_g[at, :])
    z_send(1)
    z_send(2)
    trades[1].wait_recv()
    half_from = half_units * core

    def down_mine(at):
        return gdn_ref[pl.ds(pl.multiple_of(half_from + at.start, 16), at.size), :]

    add_rows(half_units, 96, into(acc_d), down_mine, lambda at: core_d[at, :])
    z_send(3)
    for j in range(3):
        part_copy(0, j).wait_recv()
    for j in range(3):
        part_copy(1, j).start()
    for j in range(3):
        d_hidden = d_hidden + part_r[0, j].astype(f32)
    mid = mid_s[...]
    normed_ffn = mid * inv_ffn
    gain_ffn = jnp.sum(d_hidden * normed_ffn, axis=0, keepdims=True)
    d_mid = cots[0:length, :].astype(f32) + norm_back(d_hidden, normed_ffn, inv_ffn, gain_two)
    dmid_s[...] = jnp.zeros_like(dmid_s)
    dmid_s[:, shift:] = d_mid.astype(bf16)
    d_attended = dot(dmid_s[...], w_out[...], 1, 1)
    grad_out = dot(att_s[...], dmid_s[...], 0, 0)
    gj_ref[:, out_from + LANES : JOINT] = grad_out[:, LANES:].astype(bf16)
    edge = grad_out[:, :LANES]
    att_s[...] = d_attended.astype(bf16)

    dproj_s[...] = jnp.zeros_like(dproj_s)
    for j in range(kv):
        queries, keys, values, probs, probs_b = saved[j]
        d_att = jnp.concatenate(
            [
                att_s[:, (repeat * j + r) * HEAD_SIZE : (repeat * j + r + 1) * HEAD_SIZE]
                for r in range(repeat)
            ],
            axis=0,
        )
        d_probs = dot(d_att, values, 1, 1)
        row_total = jnp.sum(probs * d_probs, axis=-1, keepdims=True)
        d_scores = (probs * (d_probs - row_total) * scale).astype(bf16)
        d_queries = dot(d_scores, keys, 1, 0)
        for r in range(repeat):
            at = (repeat * j + r) * HEAD_SIZE
            dproj_s[:, at : at + HEAD_SIZE] = d_queries[r * length : (r + 1) * length]
        at = (heads + j) * HEAD_SIZE
        dproj_s[:, at : at + HEAD_SIZE] = dot(d_scores, queries, 0, 0)
        at = (heads + kv + j) * HEAD_SIZE
        dproj_s[:, at : at + HEAD_SIZE] = dot(probs_b, d_att, 0, 0)

    for p in range(panels):
        raw = dproj_s[:, p * LANES : (p + 1) * LANES]
        if p < turned_panels:
            raw = raw * cosine - swap(raw) * sine
        proj_s[:, p * LANES : (p + 1) * LANES] = raw.astype(bf16)
    d_hidden = dot(proj_s[...], joint_ref[:, :wide_qkv], 1, 1)
    grad_qkv = dot(hidden_attn, proj_s[...], 0, 0)
    gj_ref[:, :out_from] = grad_qkv[:, :out_from].astype(bf16)
    gj_ref[:, out_from:wide_qkv] = (grad_qkv[:, out_from:] + edge).astype(bf16)
    gain_attn = jnp.sum(d_hidden * normed_attn, axis=0, keepdims=True)
    din_ref[...] = (d_mid + norm_back(d_hidden, normed_attn, inv_attn, gain_one)).T.astype(bf16)
    both = jnp.concatenate([gain_attn, gain_ffn], axis=1)
    note[0, 0:16, :] = jnp.zeros((16, LANES), f32)
    for k in range(2 * width // LANES):
        note[0, k : k + 1, :] = both[:, k * LANES : (k + 1) * LANES].astype(bf16).astype(f32)

    trades[2].start()
    trades[2].wait_recv()

    add_rows(MODEL_WIDTH, 96, into(acc_j), lambda at: gj_ref[at, half_cols(core)], lambda at: core_j[at, :])

    def rs_copy(i, k):
        q = (q_one, q_far)[i]
        return remote(
            acc_j.at[sub_rows(q, k)],
            rs_one.at[i, pl.ds(SUB * k, SUB)],
            r1s.at[i, k],
            r1r.at[i, k],
            (one, group),
        )

    def rs_last(k):
        return remote(
            acc_j.at[sub_rows(q_two, k)], rs_two.at[pl.ds(SUB * k, SUB)], r2s.at[k], r2r.at[k], (two, group)
        )

    for i in (1, 0):
        for k in range(SPLIT):
            rs_copy(i, k).start()
    outputs = mid + out_own
    for j in range(3):
        part_copy(1, j).wait_recv()
        outputs = outputs + part_r[1, j].astype(f32)
    out_ref[...] = outputs.T.astype(bf16)

    def add_piece(q, k, theirs):
        at = sub_rows(q, k)
        acc_j[at, :] = (acc_j[at, :].astype(f32) + theirs[SUB * k : SUB * (k + 1), :].astype(f32)).astype(bf16)

    for k in range(SPLIT):
        rs_copy(1, k).wait_recv()
        add_piece(q_two, k, rs_one.at[1])
        rs_last(k).start()
    for k in range(SPLIT):
        rs_copy(0, k).wait_recv()
        add_piece(chip, k, rs_one.at[0])
        rs_last(k).wait_recv()
        add_piece(chip, k, rs_two)

        @pl.when(group > 0)
        def _():
            z_part(k, group - 1).start()

    def squares(value):
        return jnp.sum((value * value).reshape(-1, 8, LANES), axis=0)

    def z_add(g, i, step, rows, widths):
        source, target = z_source(g)
        at = pl.ds(i * step, step)
        value = source[at, :].astype(f32)
        for d in range(groups - 1):
            value = value + target[d, at, :].astype(f32)
        value = value.astype(bf16)
        total = jnp.zeros((8, LANES), f32)
        for p in range(widths // LANES):
            part = value[:, p * LANES : (p + 1) * LANES]
            place = i * PART_ROWS + p * step if g == 0 else p * rows + i * step
            ag[wide, place : place + step, :] = part
            total = total + squares(part.astype(f32))
        if widths % LANES:
            part = value[:, widths // LANES * LANES :]
            core_d[at, 0 : LANES // 2] = part
            part = part.astype(f32)
            part = jnp.sum((part * part).reshape(-1, 8, LANES // 2), axis=0)
            total = total + jnp.concatenate([part, jnp.zeros_like(part)], axis=1)
        return total

    def z_total(g, rows, widths):
        source, target = z_source(g)
        for at in range(groups - 1):
            remote(source, target.at[at], zs.at[g], zr.at[at], (wide, g)).wait_recv()
        step = 48
        total = jnp.zeros((8, LANES), f32)
        for i in range(rows // step):
            total = total + z_add(g, i, step, rows, widths)
        note[0, 16:24, :] = total
        if widths % LANES:
            n, last = rows // 2, widths // LANES * rows
            both = [core_d[0:n, 0 : LANES // 2], core_d[n:rows, 0 : LANES // 2]]
            ag[wide, last : last + n, :] = jnp.concatenate(both, axis=1)

    def note_copy(n):
        return remote(note.at[n], note.at[n + 4], ns.at[n], nr.at[n], ((one, two, twin)[n], group))

    def ag_copy(n, k):
        peer = (one, two, two, twin, twin, twin, twin)[n]
        q = (chip, chip, q_one, chip, q_one, q_two, q_far)[n]
        here = ag.at[2 * q + core, pl.ds(PART_ROWS * k, PART_ROWS)]
        return remote(here, here, ags.at[n, k], agr.at[n, k], (peer, group))

    def note_step(n):
        note_copy(n).wait_recv()
        note[n + 1] = note[n] + note[n + 4]
        if n < 2:
            note_copy(n + 1).start()

    for tick in range(SPLIT + 2):
        k = tick
        if k < SPLIT:

            @pl.when(group == 0)
            def _():
                for at in range(groups - 1):
                    z_part(k, at).wait_recv()
                total = z_add(0, k, SUB, CHIP_ROWS, HALF_JOINT)
                note[0, 16:24, :] = total if k == 0 else note[0, 16:24, :] + total

            if k == 0:
                for g, rows, widths in ((1, HALF_WIDTH, UNITS), (2, HALF_WIDTH, UNITS), (3, half_units, MODEL_WIDTH)):

                    @pl.when(group == g)
                    def _():
                        z_total(g, rows, widths)

            for n in (0, 1, 3):
                ag_copy(n, k).start()
            if k == SPLIT - 1:
                note_copy(0).start()
        k = tick - 1
        if 0 <= k < SPLIT:
            ag_copy(0, k).wait_recv()
            ag_copy(2, k).start()
            ag_copy(4, k).start()
            ag_copy(1, k).wait_recv()
            ag_copy(5, k).start()
        k = tick - 2
        if 0 <= k < SPLIT:
            if k == SPLIT - 2:
                note_step(0)
            if k == SPLIT - 1:
                note_step(1)
            ag_copy(2, k).wait_recv()
            ag_copy(6, k).start()
    note_step(2)
    note_z[pl.ds(group, 1)] = note[3:4]

    def note_far(d):
        return remote(
            note.at[3], note_z.at[group], nzs.at[d - 1], nzr.at[d - 1], (wide, (group + d) % groups)
        )

    for d in range(1, groups):
        note_far(d).start()

    pairs = CHIP_ROWS // 2
    lane_pairs = lanes_of(pairs)

    def halves(first, second):
        lane = lanes_of(first.shape[0])
        return jnp.where(lane < 64, pltpu.roll(first, 64, 1), pltpu.roll(second, 64, 1))

    def lay_joint(q):
        for p in range(12):
            for k in range(SPLIT):
                at, to = k * PART_ROWS + p % 6 * SUB, p * CHIP_ROWS + k * SUB
                pan[to : to + SUB, :] = ag[2 * q + p // 6, at : at + SUB, :].astype(f32)

        def even(p):
            return pan[pl.ds(p * CHIP_ROWS, pairs, 2), :]

        def odd(p):
            return pan[pl.ds(p * CHIP_ROWS + 1, pairs, 2), :]

        def put_qkv(k, value):
            flat[pl.ds(1080 * q + k, pairs, 15), :] = value

        def put_out(k, value):
            flat[pl.ds(4320 + 648 * q + k, pairs, 9), :] = value

        for p in range(7):
            put_qkv(p, even(p))
            put_qkv(8 + p, halves(odd(p), odd(p + 1)))
        put_qkv(7, jnp.where(lane_pairs < 64, even(7), pltpu.roll(odd(0), 64, 1)))
        for k in range(4):
            put_out(k, halves(even(7 + k), even(8 + k)))
            put_out(5 + k, odd(8 + k))
        put_out(4, jnp.where(lane_pairs < 64, pltpu.roll(even(11), 64, 1), odd(7)))

    def lay_gateup(q):
        for c in range(2):
            for j in range(3):
                value = ag[2 * q + c, j * HALF_WIDTH : (j + 1) * HALF_WIDTH, :].astype(f32)
                flat[pl.ds(12 * c + 3 * q + j, HALF_WIDTH, 24), :] = value

    def lay_down(q):
        n = half_units
        for c in range(2):
            w = 2 * q + c
            pan[0 : 4 * n, :] = ag[w, 0 : 4 * n, :].astype(f32)
            packed = ag[w, 4 * n : 4 * n + n // 2, :].astype(f32)
            pan[4 * n : 4 * n + n // 2, :] = packed
            pan[4 * n + n // 2 : 5 * n, :] = pltpu.roll(packed, 64, 1)

            def even(p):
                return pan[pl.ds(p * n, n // 2, 2), :]

            def odd(p):
                return pan[pl.ds(p * n + 1, n // 2, 2), :]

            def put(k, value):
                flat[pl.ds(864 * w + k, n // 2, 9), :] = value

            for p in range(4):
                put(p, even(p))
                put(5 + p, halves(odd(p), odd(p + 1)))
            put(4, jnp.where(lanes_of(n // 2) < 64, even(4), pltpu.roll(odd(0), 64, 1)))

    def lay(q):
        @pl.when(group == 0)
        def _():
            lay_joint(q)

        @pl.when((group == 1) | (group == 2))
        def _():
            lay_gateup(q)

        @pl.when(group == 3)
        def _():
            lay_down(q)

    for q, ends in ((chip, (3,)), (q_two, (4,)), (q_one, (5,)), (q_far, (6,))):
        for n in ends:
            for k in range(SPLIT):
                ag_copy(n, k).wait_recv()
        lay(q)

    head = remote(
        flat.at[pl.ds(0, HEAD_ROWS)],
        flat.at[pl.ds(BLOCK_ROWS, HEAD_ROWS)],
        hds,
        hdr,
        (wide, (group + groups - 1) % groups),
    )

    @pl.when(group > 0)
    def _():
        head.start()

    for d in range(1, groups):
        note_far(d).wait_recv()
    total = note_z[0]
    for d in range(1, groups):
        total = total + note_z[d]
    gains = total[:16]
    square = total[16:24] + squares(gains)
    square = jnp.sum(jnp.sum(square, axis=-1, keepdims=True), axis=0, keepdims=True)
    clip = jnp.minimum(jnp.float32(1.0), max_norm * lax.rsqrt(square))

    @pl.when(group == groups - 1)
    def _():
        flat[pl.ds(BLOCK_ROWS, 16), :] = gains

    clip_ref[...] = jnp.broadcast_to(clip, clip_ref.shape)

    @pl.when(group < groups - 1)
    def _():
        head.wait_recv()

    for k in range(SPLIT):
        for s in range(1, groups):
            give(s, k).wait_send()
        for n in range(7):
            stage(n, k, chip).wait_send()
    for s in range(groups):
        right, left = sends(s)
        for k in range(SPLIT):

            @pl.when(right)
            def _():
                pass_on(s, k, 1).wait_send()

            @pl.when(left)
            def _():
                pass_on(s, k, -1).wait_send()

    @pl.when(group < groups - 1)
    def _():
        tail.wait_send()

    @pl.when(group == groups - 1)
    def _():
        for g in range(groups - 1):
            gain_copy(g).wait_send()

    for j in range(3):
        cot_copies[j].wait_send()
        hid_copies[j].wait_send()
        part_copy(0, j).wait_send()
        part_copy(1, j).wait_send()
    for trade in trades:
        trade.wait_send()
    for k in range(SPLIT):
        for i in range(2):
            rs_copy(i, k).wait_send()
        rs_last(k).wait_send()
        for n in range(7):
            ag_copy(n, k).wait_send()

        @pl.when(group > 0)
        def _():
            z_part(k, group - 1).wait_send()

    for g in range(1, groups):

        @pl.when(group != g)
        def _():
            z_copy(g).wait_send()

    for n in range(3):
        note_copy(n).wait_send()
    for d in range(1, groups):
        note_far(d).wait_send()

    @pl.when(group > 0)
    def _():
        head.wait_send()


def row_step(inputs, segment_row, cotangent, params, groups):
    length = inputs.shape[0]
    dma = pltpu.SemaphoreType.DMA
    f32, bf16 = jnp.float32, jnp.bfloat16
    full = (length, MODEL_WIDTH)
    panel_lanes = 8 * LANES
    four = (CHIPS * length, MODEL_WIDTH)
    units = (CHIPS * length, UNITS)
    half_units = UNITS // 2
    z = groups - 1
    flipped_row = jax.ShapeDtypeStruct(full[::-1], bf16)
    joint = pltpu.VMEM((MODEL_WIDTH, JOINT), bf16)
    gateup = pltpu.VMEM((2, MODEL_WIDTH, UNITS), bf16)
    down = pltpu.VMEM((UNITS, MODEL_WIDTH), bf16)
    cut_joint = pltpu.VMEM((MODEL_WIDTH, HALF_JOINT), bf16)
    cut_gateup = pltpu.VMEM((MODEL_WIDTH, UNITS), bf16)
    cut_down = pltpu.VMEM((half_units, MODEL_WIDTH), bf16)
    return pl.pallas_call(
        functools.partial(row_kernel, groups),
        out_shape=(
            flipped_row,
            flipped_row,
            jax.ShapeDtypeStruct((BLOCK_ROWS + 24, LANES), f32),
            jax.ShapeDtypeStruct((8, LANES), f32),
        ),
        in_specs=vmem_specs(3) + [pl.BlockSpec(memory_space=pl.ANY)],
        out_specs=tuple(vmem_specs(4)),
        scratch_shapes=[
            joint, gateup, down,
            pltpu.VMEM((2, MODEL_WIDTH), f32),
            pltpu.VMEM((HEAD_ROWS + BLOCK_ROWS + 24, LANES), f32),
            pltpu.VMEM(params.shape, f32),
            pltpu.VMEM((8 * LANES + EXTRA,), f32),
            pltpu.VMEM((8, LANES), f32),
            pltpu.VMEM((16, LANES), f32),
            pltpu.VMEM((5 * half_units, LANES), f32),
            pltpu.VMEM((length, panel_lanes), bf16),
            pltpu.VMEM(full, bf16),
            pltpu.VMEM(full, f32),
            pltpu.VMEM((length, JOINT - QKV // LANES * LANES), bf16),
            pltpu.VMEM((length, panel_lanes), f32),
            pltpu.VMEM(four, bf16),
            pltpu.VMEM(four, bf16),
            pltpu.VMEM(units, bf16),
            pltpu.VMEM(units, bf16),
            pltpu.VMEM(units, bf16),
            pltpu.VMEM((2, 3) + full, bf16),
            pltpu.VMEM((2, 3) + full, bf16),
            joint, gateup, down,
            cut_joint, cut_gateup, cut_down,
            cut_joint, cut_gateup, cut_down,
            pltpu.VMEM((2, CHIP_ROWS, HALF_JOINT), bf16),
            pltpu.VMEM((CHIP_ROWS, HALF_JOINT), bf16),
            pltpu.VMEM((z, CHIP_ROWS, HALF_JOINT), bf16),
            pltpu.VMEM((z, HALF_WIDTH, UNITS), bf16),
            pltpu.VMEM((z, half_units, MODEL_WIDTH), bf16),
            pltpu.VMEM((8, PIECE_ROWS, LANES), bf16),
            pltpu.VMEM((7, 24, LANES), f32),
            pltpu.VMEM((groups, 24, LANES), f32),
            pltpu.VMEM((12 * CHIP_ROWS, LANES), f32),
            dma((4,)), dma, dma, dma((z,)), dma,
            dma((2, groups, SPLIT)), dma((groups, SPLIT)),
            dma((7, SPLIT)), dma((7, SPLIT)),
            dma((groups, SPLIT)), dma((groups, SPLIT)),
            dma((3,)), dma((3,)), dma((3,)), dma((3,)), dma((2, 3)), dma((2, 3)),
            dma((3,)), dma((3,)), dma((2, SPLIT)), dma((2, SPLIT)), dma((SPLIT,)), dma((SPLIT,)),
            dma((groups,)), dma((z,)), dma((SPLIT,)), dma((z, SPLIT)), dma((7, SPLIT)), dma((7, SPLIT)), dma((3,)), dma((3,)), dma((z,)), dma((z,)),
            dma, dma,
        ],
        compiler_params=pltpu.CompilerParams(
            collective_id=4, has_side_effects=True, vmem_limit_bytes=ROW_VMEM
        ),
        name="row_step",
    )(inputs.T, segment_row[None], cotangent.T, params)


def adam_kernel(
    groups, flat_in, clip_ref, par_in, one_in, two_in, layer_out, layer_din,
    grads_out, params_out, one_out, two_out, out_ref, din_ref,
    flat, grad_b, par_b, one_b, two_b, grad_t, par_t, one_t, two_t,
    flat_sem, load_sem, end_sem, out_sem, tout_sem, layer_sem,
):
    group = lax.axis_index("group")
    sources = (par_in, one_in, two_in)
    banks = (par_b, one_b, two_b)
    ahead = 24

    def flat_load(i):
        rows = pl.ds(pl.multiple_of(i * ADAM_ROWS + ahead, 8), ADAM_ROWS)
        return pltpu.make_async_copy(flat_in.at[rows], flat.at[rows], flat_sem.at[i])

    def bank_load(i, j):
        at = pl.multiple_of(i * ADAM_ROWS, 8)
        return pltpu.make_async_copy(
            sources[j].at[pl.ds(pl.multiple_of(at * LANES, 1024), ADAM_ROWS * LANES)],
            banks[j].at[pl.ds(at, ADAM_ROWS)].reshape(ADAM_ROWS * LANES),
            load_sem.at[i, j],
        )

    first = pltpu.make_async_copy(
        flat_in.at[pl.ds(0, ahead)], flat.at[pl.ds(0, ahead)], flat_sem.at[ADAM_CHUNKS]
    )
    first.start()
    for i in range(ADAM_CHUNKS):
        flat_load(i).start()
        for j in range(3):
            bank_load(i, j).start()
    end_loads = [
        pltpu.make_async_copy(source.at[pl.ds(BLOCK, EXTRA)], end, end_sem.at[j])
        for j, (source, end) in enumerate(zip(sources, (par_t, one_t, two_t)))
    ]
    copies = end_loads + [
        pltpu.make_async_copy(layer_out, out_ref, layer_sem.at[0]),
        pltpu.make_async_copy(layer_din, din_ref, layer_sem.at[1]),
    ]
    for copy in copies:
        copy.start()

    def update(g, at, count, kept=0):
        lane = lanes_of(count)
        back, cut = 9 * g // 4, LANES - 32 * g
        grads = flat[pl.ds(at + back, count), :]
        if g:
            second = flat[pl.ds(at + back + 1, count), :]
            grads = jnp.where(lane < cut, pltpu.roll(grads, cut, 1), pltpu.roll(second, cut, 1))
        if kept:
            p, m1, m2 = [rows_at(ref, 0, count, kept) for ref in (par_t, one_t, two_t)]
        else:
            p, m1, m2 = [ref[pl.ds(at, count), :] for ref in banks]
        clipped = grads * clip_ref[0:1, :]
        m1 = beta_one * m1 + (1.0 - beta_one) * clipped
        m2 = beta_two * m2 + (1.0 - beta_two) * clipped * clipped
        step_size = m1 * (1.0 / bias_one) / (jnp.sqrt(m2 * (1.0 / bias_two)) + adam_eps)
        if g == groups - 1:
            limit = BLOCK + EXTRA - 2 * MODEL_WIDTH
            place = (at + lax.broadcasted_iota(jnp.int32, (count, LANES), 0)) * LANES + lane
            decay = jnp.where(place < limit, decay_rate, 0.0)
        else:
            decay = decay_rate
        return grads, p - learn_rate * (step_size + decay * p), m1, m2

    outs = (grads_out, params_out, one_out, two_out)
    stores = (grad_b, par_b, one_b, two_b)
    ends = (grad_t, par_t, one_t, two_t)

    def out_copy(i, j):
        at = pl.multiple_of(i * ADAM_ROWS, 8)
        return pltpu.make_async_copy(
            stores[j].at[pl.ds(at, ADAM_ROWS)].reshape(ADAM_ROWS * LANES),
            outs[j].at[pl.ds(pl.multiple_of(at * LANES, 1024), ADAM_ROWS * LANES)],
            out_sem.at[i, j],
        )

    def tail_copy(j):
        return pltpu.make_async_copy(
            ends[j], outs[j].at[pl.ds(BLOCK, EXTRA)], tout_sem.at[j]
        )

    first.wait()
    for copy in end_loads:
        copy.wait()
    for g in range(groups):

        @pl.when(group == g)
        def _():
            def body(i, _):
                at = pl.multiple_of(i * ADAM_ROWS, 8)
                flat_load(i).wait()
                for j in range(3):
                    bank_load(i, j).wait()
                for store, value in zip(stores, update(g, at, ADAM_ROWS)):
                    store[pl.ds(at, ADAM_ROWS), :] = value
                for j in range(4):
                    out_copy(i, j).start()
                return 0

            lax.fori_loop(0, ADAM_CHUNKS, body, 0)
            for end, value in zip(ends, update(g, BLOCK_ROWS, 8, EXTRA)):
                end[...] = value.reshape(8 * LANES)[:EXTRA]

    for j in range(4):
        tail_copy(j).start()
    for i in range(ADAM_CHUNKS):
        for j in range(4):
            out_copy(i, j).wait()
    for j in range(4):
        tail_copy(j).wait()
    for copy in copies[3:]:
        copy.wait()


def adam(settled, states, outputs, d_inputs, groups):
    dma = pltpu.SemaphoreType.DMA
    f32 = jnp.float32
    anywhere = pl.BlockSpec(memory_space=pl.ANY)
    bank = pltpu.VMEM((BLOCK_ROWS, LANES), f32)
    end = pltpu.VMEM((EXTRA,), f32)
    return pl.pallas_call(
        functools.partial(adam_kernel, groups),
        out_shape=(jax.ShapeDtypeStruct(states[0].shape, f32),) * 4
        + tuple(jax.ShapeDtypeStruct(a.shape, a.dtype) for a in (outputs, d_inputs)),
        in_specs=[anywhere] + vmem_specs(1) + [anywhere] * 5,
        out_specs=(anywhere,) * 6,
        scratch_shapes=[pltpu.VMEM((BLOCK_ROWS + 24, LANES), f32)]
        + [bank] * 4
        + [end] * 4
        + [dma((ADAM_CHUNKS + 1,)), dma((ADAM_CHUNKS, 3)), dma((3,))]
        + [dma((ADAM_CHUNKS, 4)), dma((4,)), dma((2,))],
        compiler_params=pltpu.CompilerParams(vmem_limit_bytes=ADAM_VMEM),
        name="adam",
    )(*settled, *states, outputs, d_inputs)


def on_device(inputs, segments, cotangent, params, moment_one, moment_two):
    groups = lax.axis_size("group")
    wides = lax.axis_size("wide")
    group = lax.axis_index("group")
    count = wides.bit_length() - 1
    share_len = params.shape[0]
    gain_len = 2 * MODEL_WIDTH
    extra = gain_len // groups
    block_len = share_len - extra
    if groups == 4 and wides == 2 * CHIPS and block_len == BLOCK and inputs.shape[0] == 1:
        outputs, d_inputs, *settled = row_step(
            inputs[0], segments[0], cotangent[0], params, groups
        )
        *updated, outputs, d_inputs = adam(
            settled, (params, moment_one, moment_two), outputs, d_inputs, groups
        )
        return (outputs.T[None], d_inputs.T[None], *updated)
    block_rows = block_len // LANES
    piece_rows = -(-block_rows // wides)
    chunks = 6 if piece_rows % 96 == 0 else 2
    piece_rows = -(-piece_rows // (16 * chunks)) * 16 * chunks
    padding = piece_rows * wides - block_rows
    lead = (2,) * count

    def to_pieces(rows):
        rows = rows.reshape(-1, block_rows, LANES)
        if padding:
            rows = jnp.pad(rows, ((0, 0), (0, padding), (0, 0)))
        return rows.reshape((-1,) + lead + (piece_rows, LANES))

    def from_pieces(pieces):
        rows = pieces.reshape(-1, piece_rows * wides, LANES)[:, :block_rows]
        return rows.reshape(-1, LANES)

    rounded = params.astype(jnp.bfloat16)
    tail = jnp.pad(rounded[share_len - gain_len :], (0, 16 * LANES - gain_len)).reshape(16, LANES)
    tails = gather_tails(tail, groups, 0).reshape(groups, -1)[:, :gain_len]
    before = lax.dynamic_index_in_dim(tails, (group + groups - 1) % groups, keepdims=False)
    joined = jnp.concatenate([before, rounded])
    block = lax.dynamic_slice(joined, (gain_len - extra * group,), (block_len,))
    flat_gains = tails[groups - 1]
    gathered = gather_blocks(to_pieces(block)[0], groups, count, chunks)
    weights = unpack(from_pieces(gathered), flat_gains)
    outputs, d_inputs, main, gains = layer_row(inputs[0], segments[0], cotangent[0], weights)
    gains = gains.astype(jnp.bfloat16).astype(jnp.float32)
    gains = jnp.pad(gains, (0, 16 * LANES - gain_len)).reshape(16, LANES)
    summed_block, head, gains, square = sum_blocks(to_pieces(main), gains, groups, count, chunks)
    gains = gains.reshape(-1)[:gain_len].astype(jnp.bfloat16)
    flat_block = from_pieces(summed_block).reshape(-1)
    head = head.reshape(-1)[:gain_len]
    head = jnp.where(group == groups - 1, gains, head)
    joined = jnp.concatenate([flat_block, head])
    summed = lax.dynamic_slice(joined, (extra * group,), (share_len,)).astype(jnp.float32)
    clip_factor = square[0, 0]
    flat_index = group * share_len + jnp.arange(share_len, dtype=jnp.int32)
    decay_mask = flat_index < share_len * groups - gain_len
    new_params, new_moment_one, new_moment_two = adam_update(
        summed, clip_factor, params, moment_one, moment_two, decay_mask
    )
    return (outputs[None], d_inputs[None], summed, new_params, new_moment_one, new_moment_two)


def solution(mesh):
    return jax.shard_map(
        on_device,
        mesh=mesh,
        in_specs=(
            P(("wide", "group"), None, None),
            P(("wide", "group"), None),
            P(("wide", "group"), None, None),
            P("group"),
            P("group"),
            P("group"),
        ),
        out_specs=(
            P(("wide", "group"), None, None),
            P(("wide", "group"), None, None),
            P("group"),
            P("group"),
            P("group"),
            P("group"),
        ),
        check_vma=False,
    )
```

```python
import functools
import math

import jax
import jax.numpy as jnp
from jax import lax
from jax.experimental import pallas as pl
from jax.experimental.pallas import tpu as pltpu
from jax.sharding import PartitionSpec as P

MESH = pl.DeviceIdType.MESH
LANES = 128

MODEL_WIDTH = 576
QUERY_HEADS = 9
KEY_VALUE_HEADS = 3
HEAD_SIZE = 64
FF = 1536


norm_eps = 1e-05
theta_base = 10000.0
masked_value = -1e30
beta_one = 0.9
beta_two = 0.95
bias_one = 0.19
bias_two = 0.0975
learn_rate = 0.03
decay_rate = 0.1
adam_eps = 1e-08
max_norm = 1.0


def contract(pattern, left_op, right_op):
    return jnp.einsum(pattern, left_op, right_op, preferred_element_type=jnp.float32)


def inner_rows(left_op, right_op):
    return lax.dot_general(
        left_op, right_op, (((0,), (0,)), ((), ())), preferred_element_type=jnp.float32
    )


def outer_column_count(left_op, right_op):
    return lax.dot_general(
        left_op, right_op, (((1,), (1,)), ((), ())), preferred_element_type=jnp.float32
    )


def unpack(main, gains):
    query_key_value_width = (QUERY_HEADS + 2 * KEY_VALUE_HEADS) * HEAD_SIZE
    shapes = [
        (MODEL_WIDTH, query_key_value_width),
        (QUERY_HEADS * HEAD_SIZE, MODEL_WIDTH),
        (MODEL_WIDTH, 2 * FF),
        (FF, MODEL_WIDTH),
    ]
    pieces = []
    offset = 0
    for piece_shape in shapes:
        extent = math.prod(piece_shape) // LANES
        pieces.append(main[offset : offset + extent].reshape(piece_shape))
        offset += extent
    return pieces + [gains[:MODEL_WIDTH], gains[MODEL_WIDTH:]]


def positions_of(segment_row):
    index_row = jnp.arange(segment_row.shape[0], dtype=jnp.int32)
    same = segment_row[:, None] == segment_row[None, :]
    before = index_row[:, None] > index_row[None, :]
    return jnp.sum((same & before).astype(jnp.int32), axis=1)


def rope_tables(positions):
    half_size = HEAD_SIZE // 2
    freqs = theta_base ** (-2.0 * jnp.arange(half_size, dtype=jnp.float32) / HEAD_SIZE)
    angles = positions.astype(jnp.float32)[:, None] * freqs[None, :]
    return (jnp.cos(angles)[:, None, :], jnp.sin(angles)[:, None, :])


def apply_rotation(vectors, cosine_lookup, sine_lookup):
    half_size = HEAD_SIZE // 2
    first_half = vectors[..., :half_size]
    second_half = vectors[..., half_size:]
    return jnp.concatenate(
        [
            first_half * cosine_lookup - second_half * sine_lookup,
            second_half * cosine_lookup + first_half * sine_lookup,
        ],
        axis=-1,
    )


def unrotate(vectors, cosine_lookup, sine_lookup):
    half_size = HEAD_SIZE // 2
    first_half = vectors[..., :half_size]
    second_half = vectors[..., half_size:]
    return jnp.concatenate(
        [
            first_half * cosine_lookup + second_half * sine_lookup,
            second_half * cosine_lookup - first_half * sine_lookup,
        ],
        axis=-1,
    )


def norm_back(d_hidden, normed, inverse, gain):
    d_normed = d_hidden * gain
    return inverse * (d_normed - normed * jnp.mean(d_normed * normed, axis=-1, keepdims=True))


def layer_row(inputs, segment_row, cotangent, weights):
    query_key_value_weight, output_weight, w_gateup, w_down, gain_attn, gain_ffn = weights
    sequence_length = inputs.shape[0]
    repeat_count = QUERY_HEADS // KEY_VALUE_HEADS
    scale_factor = HEAD_SIZE ** (-0.5)
    gain_one = gain_attn.astype(jnp.float32)
    gain_two = gain_ffn.astype(jnp.float32)
    resid_in = inputs.astype(jnp.float32)
    inv_attn = lax.rsqrt(jnp.mean(resid_in * resid_in, axis=-1, keepdims=True) + norm_eps)
    normed_attn = resid_in * inv_attn
    hidden_attn = (normed_attn * gain_one).astype(jnp.bfloat16)
    projected_output = jnp.dot(
        hidden_attn, query_key_value_weight, preferred_element_type=jnp.float32
    )
    cosine_lookup, sine_lookup = rope_tables(positions_of(segment_row))
    query_rows = projected_output[:, : QUERY_HEADS * HEAD_SIZE].reshape(
        sequence_length, QUERY_HEADS, HEAD_SIZE
    )
    key_matrix = projected_output[
        :, QUERY_HEADS * HEAD_SIZE : (QUERY_HEADS + KEY_VALUE_HEADS) * HEAD_SIZE
    ].reshape(sequence_length, KEY_VALUE_HEADS, HEAD_SIZE)
    query_rows_rotated = (
        apply_rotation(query_rows, cosine_lookup, sine_lookup)
        .astype(jnp.bfloat16)
        .reshape(sequence_length, KEY_VALUE_HEADS, repeat_count, HEAD_SIZE)
    )
    keys_rot = apply_rotation(key_matrix, cosine_lookup, sine_lookup).astype(jnp.bfloat16)
    value_rows = (
        projected_output[:, (QUERY_HEADS + KEY_VALUE_HEADS) * HEAD_SIZE :]
        .reshape(sequence_length, KEY_VALUE_HEADS, HEAD_SIZE)
        .astype(jnp.bfloat16)
    )
    index_row = jnp.arange(sequence_length)
    allowed = (segment_row[:, None] == segment_row[None, :]) & (
        index_row[:, None] >= index_row[None, :]
    )
    scores = contract("qgrd,kgd->grqk", query_rows_rotated, keys_rot) * scale_factor
    scores = jnp.where(allowed, scores, masked_value)
    peak = jnp.max(scores, axis=-1, keepdims=True)
    log_total = peak + jnp.log(jnp.sum(jnp.exp(scores - peak), axis=-1, keepdims=True))
    probs_b = jnp.exp(scores - log_total).astype(jnp.bfloat16)
    attended = (
        contract("grqk,kgd->qgrd", probs_b, value_rows)
        .astype(jnp.bfloat16)
        .reshape(sequence_length, QUERY_HEADS * HEAD_SIZE)
    )
    mid = resid_in + jnp.dot(attended, output_weight, preferred_element_type=jnp.float32)
    inv_ffn = lax.rsqrt(jnp.mean(mid * mid, axis=-1, keepdims=True) + norm_eps)
    normed_ffn = mid * inv_ffn
    hidden_ffn = (normed_ffn * gain_two).astype(jnp.bfloat16)
    gate_up = jnp.dot(hidden_ffn, w_gateup, preferred_element_type=jnp.float32)
    gate_pre = gate_up[:, :FF]
    upper = gate_up[:, FF:]
    sigmoid_gate = jax.nn.sigmoid(gate_pre)
    activation = (gate_pre * sigmoid_gate * upper).astype(jnp.bfloat16)
    outputs = (mid + jnp.dot(activation, w_down, preferred_element_type=jnp.float32)).astype(
        jnp.bfloat16
    )
    grad_down = inner_rows(activation, cotangent)
    d_act = outer_column_count(cotangent, w_down)
    d_gate = d_act * upper * sigmoid_gate * (1.0 + gate_pre * (1.0 - sigmoid_gate))
    d_upper = d_act * gate_pre * sigmoid_gate
    d_gate_up = jnp.concatenate([d_gate, d_upper], axis=-1).astype(jnp.bfloat16)
    grad_gateup = inner_rows(hidden_ffn, d_gate_up)
    d_hidden_ffn = outer_column_count(d_gate_up, w_gateup)
    grad_gain_ffn = jnp.sum(d_hidden_ffn * normed_ffn, axis=0)
    d_mid = cotangent.astype(jnp.float32) + norm_back(d_hidden_ffn, normed_ffn, inv_ffn, gain_two)
    grad_middle_batch = d_mid.astype(jnp.bfloat16)
    grad_out = inner_rows(attended, grad_middle_batch)
    grad_attended_rows = (
        outer_column_count(grad_middle_batch, output_weight)
        .astype(jnp.bfloat16)
        .reshape(sequence_length, KEY_VALUE_HEADS, repeat_count, HEAD_SIZE)
    )
    recomputed = contract("qgrd,kgd->grqk", query_rows_rotated, keys_rot) * scale_factor
    probs = jnp.exp(jnp.where(allowed, recomputed, masked_value) - log_total)
    d_probs = contract("qgrd,kgd->grqk", grad_attended_rows, value_rows)
    row_total = jnp.sum(probs * d_probs, axis=-1, keepdims=True)
    d_scores = (probs * (d_probs - row_total) * scale_factor).astype(jnp.bfloat16)
    grad_query_rows = contract("grqk,kgd->qgrd", d_scores, keys_rot).reshape(
        sequence_length, QUERY_HEADS, HEAD_SIZE
    )
    grad_key_rows = contract("grqk,qgrd->kgd", d_scores, query_rows_rotated)
    grad_value_rows = contract("grqk,qgrd->kgd", probs_b, grad_attended_rows)
    grad_query_rows = unrotate(grad_query_rows, cosine_lookup, sine_lookup)
    grad_key_rows = unrotate(grad_key_rows, cosine_lookup, sine_lookup)
    grad_projected_rows = jnp.concatenate(
        [
            grad_query_rows.reshape(sequence_length, QUERY_HEADS * HEAD_SIZE),
            grad_key_rows.reshape(sequence_length, KEY_VALUE_HEADS * HEAD_SIZE),
            grad_value_rows.reshape(sequence_length, KEY_VALUE_HEADS * HEAD_SIZE),
        ],
        axis=-1,
    ).astype(jnp.bfloat16)
    grad_qkv = inner_rows(hidden_attn, grad_projected_rows)
    d_hidden_attn = outer_column_count(grad_projected_rows, query_key_value_weight)
    grad_gain_attn = jnp.sum(d_hidden_attn * normed_attn, axis=0)
    d_inputs = (d_mid + norm_back(d_hidden_attn, normed_attn, inv_attn, gain_one)).astype(
        jnp.bfloat16
    )
    matrices = [grad_qkv, grad_out, grad_gateup, grad_down]
    main = jnp.concatenate([m.astype(jnp.bfloat16).reshape(-1, LANES) for m in matrices])
    gains = jnp.concatenate([grad_gain_attn, grad_gain_ffn])
    return (outputs, d_inputs, main, gains)


def adam_update(grads, clip_factor, params, moment_one, moment_two, decay_mask):
    clipped = grads * clip_factor
    new_moment_one = beta_one * moment_one + (1.0 - beta_one) * clipped
    new_moment_two = beta_two * moment_two + (1.0 - beta_two) * clipped * clipped
    step_size = new_moment_one / bias_one / (jnp.sqrt(new_moment_two / bias_two) + adam_eps)
    decay_term = jnp.where(decay_mask, decay_rate * params, jnp.zeros_like(params))
    new_params = params - learn_rate * (step_size + decay_term)
    return (new_params, new_moment_one, new_moment_two)


def my_bits(wide, count):
    return [(wide // 2**b) % 2 for b in range(count)]


def flipped(wide, bit, b):
    return wide + (1 - 2 * bit) * 2**b


def greet(wide, group, bits, groups):
    barrier = pltpu.get_barrier_semaphore()
    peers = [(flipped(wide, bit, b), group) for b, bit in enumerate(bits)]
    peers += [(wide, (group + d) % groups) for d in range(1, groups)]
    for peer in peers:
        pl.semaphore_signal(barrier, inc=1, device_id=peer, device_id_type=MESH)
    pl.semaphore_wait(barrier, len(peers))


def send(src, dst, send_sem, recv_sem, peer):
    copy = pltpu.make_async_remote_copy(
        src_ref=src,
        dst_ref=dst,
        send_sem=send_sem,
        recv_sem=recv_sem,
        device_id=peer,
        device_id_type=MESH,
    )
    copy.start()
    return copy


def bit_order(chunk, count):
    rest = list(range(1, count))
    return [0] + (rest if chunk % 2 == 0 else rest[::-1])


def tails_kernel(groups, bits_count, tail_ref, out_ref, send_sem, recv_sem):
    wide, group = lax.axis_index("wide"), lax.axis_index("group")
    greet(wide, group, [], groups)
    out_ref[pl.ds(group, 1)] = tail_ref[...][None]
    copies = []
    for d in range(1, groups):
        copies.append(
            send(
                tail_ref,
                out_ref.at[group],
                send_sem.at[d - 1],
                recv_sem.at[d - 1],
                (wide, (group + d) % groups),
            )
        )
    for copy in copies[3:]:
        copy.wait()


def gather_kernel(groups, count, chunks, block_ref, out_ref, own_sem, zs, zr, ws, wr):
    wide, group = lax.axis_index("wide"), lax.axis_index("group")
    bits = my_bits(wide, count)
    step = block_ref.shape[-2] // chunks
    greet(wide, group, bits, groups)

    def place(ref, lead, open_bits, chunk):
        index = [slice(None) if b in open_bits else bits[b] for b in reversed(range(count))]
        return ref.at[tuple(lead + index + [pl.ds(chunk * step, step)])]

    def copy(src, dst, send_sem, recv_sem, peer):
        return pltpu.make_async_remote_copy(
            src_ref=src,
            dst_ref=dst,
            send_sem=send_sem,
            recv_sem=recv_sem,
            device_id=peer,
            device_id_type=MESH,
        )

    def along(way, d, c):
        source = (group - way * (d - 1) + groups) % groups
        unit = (0 if way > 0 else groups - 1) + d - 1
        src = place(block_ref, [], [], c) if d == 1 else place(out_ref, [source], [], c)
        return copy(
            src,
            place(out_ref, [source], [], c),
            zs.at[unit, c],
            zr.at[unit, c],
            (wide, (group + way + groups) % groups),
        )

    def passes(way, d):
        ahead = group + way
        behind = group - way * (d - 1)
        return (ahead >= 0) & (ahead < groups) & (behind >= 0) & (behind < groups)

    def comes(way, d):
        behind = group - way * d
        return (behind >= 0) & (behind < groups)

    def across(way, d, c, stage):
        order = bit_order(c, count)[::-1]
        b = order[stage]
        source = (group - way * d + groups) % groups
        unit = (0 if way > 0 else groups - 1) + d - 1
        here = place(out_ref, [source], order[:stage], c)
        return copy(
            here,
            here,
            ws.at[unit, c, stage],
            wr.at[unit, c, stage],
            (flipped(wide, bits[b], b), group),
        )

    units = [(d, c) for d in range(1, groups) for c in range(chunks)]
    for c in range(chunks):
        for way in (1, -1):

            @pl.when(passes(way, 1))
            def _():
                along(way, 1, c).start()

    own = pltpu.make_async_copy(block_ref, out_ref.at[group], own_sem)
    own.start()
    for tick in range(len(units) // 2 + count + 1):
        for u, (d, c) in reversed(list(enumerate(units))):
            stage = tick - u // 2
            if not 0 <= stage <= count:
                continue
            for way in (1, -1):

                @pl.when(comes(way, d))
                def _():
                    if stage == 0:
                        along(way, d, c).wait_recv()
                    else:
                        across(way, d, c, stage - 1).wait_recv()
                    if stage < count:
                        across(way, d, c, stage).start()

                if stage == 0 and d + 1 < groups:

                    @pl.when(passes(way, d + 1))
                    def _():
                        along(way, d + 1, c).start()

    for way in (1, -1):
        for d, c in units:

            @pl.when(passes(way, d))
            def _():
                along(way, d, c).wait_send()

            @pl.when(comes(way, d))
            def _():
                for stage in range(count):
                    across(way, d, c, stage).wait_send()

    own.wait()


def sum_kernel(groups, count, chunks, x_ref, gain_ref, out_ref, head_ref, gsum_ref, sq_ref, *scratch):
    recvs, accs = scratch[:count], scratch[count : 2 * count]
    recv_z, gain_w, gain_z, sq_z, piece_head = scratch[2 * count : 2 * count + 5]
    ss, sr, zs, zr, gs, gr, xs, xr, gzs, gzr, qs, qr, hs, hr = scratch[2 * count + 5 :]
    wide, group = lax.axis_index("wide"), lax.axis_index("group")
    bits = my_bits(wide, count)
    step = x_ref.shape[-2] // chunks
    greet(wide, group, bits, groups)
    copies = {}
    f32 = jnp.float32

    def partner(b):
        return (flipped(wide, bits[b], b), group)

    def part(c, stage, value):
        order = bit_order(c, count)
        left = sorted(order[stage:], reverse=True)
        return [value if b == order[stage] else slice(None) for b in left]

    def held(c, stage):
        return x_ref if stage == 0 else accs[stage - 1].at[c]

    def view(c, stage, flip):
        b = bit_order(c, count)[stage]
        index = [slice(None)] + part(c, stage, 1 - bits[b] if flip else bits[b])
        if stage == 0:
            index += [slice(None)] * (count + 2 - len(index) - 1)
            return x_ref.at[tuple(index + [pl.ds(c * step, step)])]
        return accs[stage - 1].at[tuple([c] + index)]

    def start_scatter(c, stage):
        b = bit_order(c, count)[stage]
        copies["s", c, stage] = send(
            view(c, stage, True), recvs[stage].at[c], ss.at[c, stage], sr.at[c, stage], partner(b)
        )

    def add_scatter(c, stage):
        copies["s", c, stage].wait_recv()
        mine, other, total = view(c, stage, False), recvs[stage].at[c], accs[stage].at[c]

        def body(i, _):
            total[i] = (mine[i].astype(f32) + other[i].astype(f32)).astype(jnp.bfloat16)
            return 0

        lax.fori_loop(0, groups, body, 0)

    def start_groups(c):
        for d in range(1, groups):
            to = (group + d) % groups
            copies["z", c, d] = send(
                accs[-1].at[c, to],
                recv_z.at[c, d - 1],
                zs.at[c, d - 1],
                zr.at[c, d - 1],
                (wide, to),
            )

    def place(open_bits, c):
        index = [slice(None) if b in open_bits else bits[b] for b in reversed(range(count))]
        return out_ref.at[tuple(index + [pl.ds(c * step, step)])]

    def add_groups(c):
        total = accs[-1][c, group].astype(f32)
        for d in range(1, groups):
            copies["z", c, d].wait_recv()
            total = total + recv_z[c, d - 1].astype(f32)
        place([], c)[...] = total.astype(jnp.bfloat16)

    def start_gather(c, stage):
        order = bit_order(c, count)[::-1]
        here = place(order[:stage], c)
        copies["g", c, stage] = send(
            here, here, gs.at[c, stage], gr.at[c, stage], partner(order[stage])
        )

    for c in range(chunks):
        start_scatter(c, 0)
    gain_w[0] = gain_ref[...]
    copies["x", 0] = send(gain_w.at[0], gain_w.at[count + 1], xs.at[0], xr.at[0], partner(0))

    for tick in range(chunks // 2 + 2 * count + 1):
        for c in reversed(range(chunks)):
            s = tick - c // 2
            if 0 <= s < count:
                add_scatter(c, s)
                if s + 1 < count:
                    start_scatter(c, s + 1)
                else:
                    start_groups(c)
            elif s == count:
                add_groups(c)
                start_gather(c, 0)
            elif count < s <= 2 * count:
                copies["g", c, s - count - 1].wait_recv()
                if s < 2 * count:
                    start_gather(c, s - count)
        if tick < count:
            copies["x", tick].wait_recv()
            gain_w[tick + 1] = gain_w[tick] + gain_w[count + 1 + tick]
            if tick + 1 < count:
                copies["x", tick + 1] = send(
                    gain_w.at[tick + 1],
                    gain_w.at[count + 2 + tick],
                    xs.at[tick + 1],
                    xr.at[tick + 1],
                    partner(tick + 1),
                )
            else:
                gain_z[pl.ds(group, 1)] = gain_w[pl.ds(count, 1)]
                for d in range(1, groups):
                    copies["gz", d] = send(
                        gain_w.at[count],
                        gain_z.at[group],
                        gzs.at[d - 1],
                        gzr.at[d - 1],
                        (wide, (group + d) % groups),
                    )

    first = tuple([0] * count + [pl.ds(0, 16)])
    copies["h"] = send(out_ref.at[first], head_ref, hs, hr, (wide, (group + groups - 1) % groups))
    flat_lead = out_ref.shape[:-2]

    def squares(i, total):
        index = tuple((i // 2**b) % 2 for b in reversed(range(len(flat_lead))))
        value = out_ref[index].astype(f32)
        value = value * value
        return total + jnp.sum(value.reshape(-1, 8, LANES), axis=0)

    square = lax.fori_loop(0, math.prod(flat_lead), squares, jnp.zeros((8, LANES), f32))
    piece_head[...] = square
    sq_z[pl.ds(group, 1)] = square[None]
    for d in range(1, groups):
        copies["q", d] = send(
            piece_head, sq_z.at[group], qs.at[d - 1], qr.at[d - 1], (wide, (group + d) % groups)
        )
    for d in range(1, groups):
        copies["gz", d].wait_recv()
    gains = gain_z[0]
    for d in range(1, groups):
        gains = gains + gain_z[d]
    gains = gains.astype(jnp.bfloat16).astype(f32)
    gsum_ref[...] = gains
    for d in range(1, groups):
        copies["q", d].wait_recv()
    square = sq_z[0]
    for d in range(1, groups):
        square = square + sq_z[d]
    square = square + jnp.sum((gains * gains).reshape(-1, 8, LANES), axis=0)
    total = jnp.sum(jnp.sum(square, axis=-1, keepdims=True), axis=0, keepdims=True)
    clip = jnp.minimum(jnp.float32(1.0), max_norm * lax.rsqrt(total))
    sq_ref[...] = jnp.broadcast_to(clip, sq_ref.shape)
    copies["h"].wait_recv()
    for copy in copies.values():
        copy.wait_send()


def params_of(identity):
    return pltpu.CompilerParams(
        collective_id=identity, has_side_effects=True, vmem_limit_bytes=60 * 2**20
    )


def vmem_specs(n):
    return [pl.BlockSpec(memory_space=pltpu.VMEM)] * n


def gather_tails(tail, groups, identity):
    dma = pltpu.SemaphoreType.DMA
    return pl.pallas_call(
        functools.partial(tails_kernel, groups, 0),
        out_shape=jax.ShapeDtypeStruct((groups,) + tail.shape, tail.dtype),
        in_specs=vmem_specs(1),
        out_specs=vmem_specs(1)[0],
        scratch_shapes=[dma((groups - 1,)), dma((groups - 1,))],
        compiler_params=params_of(identity),
        name="tails",
    )(tail)


def gather_blocks(block, groups, count, chunks):
    dma = pltpu.SemaphoreType.DMA
    units = 2 * (groups - 1)
    return pl.pallas_call(
        functools.partial(gather_kernel, groups, count, chunks),
        out_shape=jax.ShapeDtypeStruct((groups,) + block.shape, block.dtype),
        in_specs=vmem_specs(1),
        out_specs=vmem_specs(1)[0],
        scratch_shapes=[
            dma,
            dma((units, chunks)),
            dma((units, chunks)),
            dma((units, chunks, count)),
            dma((units, chunks, count)),
        ],
        compiler_params=params_of(1),
        name="gather_weights",
    )(block)


def sum_blocks(main, gains, groups, count, chunks):
    dma = pltpu.SemaphoreType.DMA
    rows = main.shape[-2]
    step = rows // chunks
    bf16, f32 = jnp.bfloat16, jnp.float32
    stages = [
        pltpu.VMEM((chunks, groups) + (2,) * (count - 1 - k) + (step, LANES), bf16)
        for k in range(count)
    ]
    return pl.pallas_call(
        functools.partial(sum_kernel, groups, count, chunks),
        out_shape=(
            jax.ShapeDtypeStruct((2,) * count + (rows, LANES), bf16),
            jax.ShapeDtypeStruct((16, LANES), bf16),
            jax.ShapeDtypeStruct(gains.shape, f32),
            jax.ShapeDtypeStruct((8, LANES), f32),
        ),
        in_specs=vmem_specs(2),
        out_specs=tuple(vmem_specs(4)),
        scratch_shapes=stages
        + stages
        + [
            pltpu.VMEM((chunks, groups - 1, step, LANES), bf16),
            pltpu.VMEM((2 * count + 1,) + gains.shape, f32),
            pltpu.VMEM((groups,) + gains.shape, f32),
            pltpu.VMEM((groups, 8, LANES), f32),
            pltpu.VMEM((8, LANES), f32),
        ]
        + [dma((chunks, count))] * 2
        + [dma((chunks, groups - 1))] * 2
        + [dma((chunks, count))] * 2
        + [dma((count,))] * 2
        + [dma((groups - 1,))] * 4
        + [dma, dma],
        compiler_params=params_of(2),
        name="sum_grads",
    )(main, gains)


def dot(left_op, right_op, left_dim, right_dim):
    return lax.dot_general(
        left_op,
        right_op,
        (((left_dim,), (right_dim,)), ((), ())),
        preferred_element_type=jnp.float32,
    )


def cores_of(wide):
    core, x_bit, y_bit = wide % 2, (wide // 2) % 2, (wide // 4) % 2
    over_x, over_y = wide + (1 - 2 * x_bit) * 2, wide + (1 - 2 * y_bit) * 4
    one = over_x * (1 - core) + over_y * core
    two = over_y * (1 - core) + over_x * core
    far = over_x + over_y - wide
    twin = wide + 1 - 2 * core
    return core, over_x, over_y, far, one, two, twin


def greet_all(peers):
    barrier = pltpu.get_barrier_semaphore()
    for peer in peers:
        pl.semaphore_signal(barrier, inc=1, device_id=peer, device_id_type=MESH)
    pl.semaphore_wait(barrier, len(peers))


def remote(src, dst, send_sem, recv_sem, peer):
    return pltpu.make_async_remote_copy(
        src_ref=src,
        dst_ref=dst,
        send_sem=send_sem,
        recv_sem=recv_sem,
        device_id=peer,
        device_id_type=MESH,
    )


QKV = (QUERY_HEADS + 2 * KEY_VALUE_HEADS) * HEAD_SIZE
INNER = QUERY_HEADS * HEAD_SIZE
JOINT = QKV + INNER
HALF_JOINT = JOINT // 2
CHIPS = 4
CHIP_ROWS = MODEL_WIDTH // CHIPS
UNITS = FF // CHIPS
HALF_WIDTH = MODEL_WIDTH // 2
SPLIT = 3
SUB = CHIP_ROWS // SPLIT
BLOCK = MODEL_WIDTH * FF
BLOCK_ROWS = BLOCK // LANES
EXTRA = 2 * MODEL_WIDTH // 4
HEAD_ROWS = 8


def lanes_of(rows):
    return lax.broadcasted_iota(jnp.int32, (rows, LANES), 1)


def rows_at(ref, at, count, kept=0):
    if kept:
        value = ref[pl.ds(at * LANES, kept)]
        value = jnp.concatenate([value, jnp.zeros((count * LANES - kept,), value.dtype)])
    else:
        value = ref[pl.ds(pl.multiple_of(at * LANES, 1024), count * LANES)]
    return value.reshape(count, LANES)


ADAM_CHUNKS = 8
ADAM_ROWS = BLOCK_ROWS // ADAM_CHUNKS
PIECE_ROWS = BLOCK_ROWS // 8
PART_ROWS = PIECE_ROWS // SPLIT
ROW_VMEM = 60 * 2**20
ADAM_VMEM = 60 * 2**20


def row_kernel(
    groups, x_ref, seg_ref, cot_ref, params_ref,
    out_ref, din_ref, flat, clip_ref,
    joint_ref, gu_ref, down_ref, gain_w, raw, lin, lin_t, tail_s, gain_s, pan_w,
    proj_s, att_s, mid_s, dmid_s, dproj_s, cots, hids, act_s, gate_s, up_s, part_s, part_r,
    gj_ref, ggu_ref, gdn_ref, core_j, core_g, core_d, acc_j, acc_g, acc_d,
    rs_one, rs_two, z_j, z_g, z_d, ag, note, note_z, pan,
    raw_sem, ts, tr, gns, gnr, wzs, wzr, as_, ar, es, er,
    cs, cr, hs, hr, ps, pr,
    sws, swr, r1s, r1r, r2s, r2r, zs, zr, zjs, zjr, ags, agr, ns, nr, nzs, nzr, hds, hdr,
):
    f32, bf16 = jnp.float32, jnp.bfloat16
    wide, group = lax.axis_index("wide"), lax.axis_index("group")
    core, over_x, over_y, far, one, two, twin = cores_of(wide)
    chip = wide // 2
    whole = pltpu.make_async_copy(params_ref, lin, raw_sem.at[0])

    def part_load(i, at, count):
        here = pl.ds(pl.multiple_of(at * LANES, 1024), count * LANES)
        return pltpu.make_async_copy(params_ref.at[here], lin.at[here], raw_sem.at[i])

    qkv_rows, out_rows = BLOCK_ROWS * QKV // JOINT // CHIPS, BLOCK_ROWS * INNER // JOINT // CHIPS
    qkv_from, out_from_row = qkv_rows * chip, CHIPS * qkv_rows + out_rows * chip
    load_qkv, load_out = part_load(1, qkv_from, qkv_rows), part_load(2, out_from_row, out_rows)

    load_end = pltpu.make_async_copy(
        params_ref.at[pl.ds(BLOCK - 8 * LANES, 8 * LANES + EXTRA)], lin_t, raw_sem.at[3]
    )

    @pl.when(group == 0)
    def _():
        load_qkv.start()
        load_out.start()
        load_end.start()

    @pl.when(group > 0)
    def _():
        whole.start()

    peers = [(p, group) for p in (over_x, over_y, far, twin)]
    peers += [(wide, (group + d) % groups) for d in range(1, groups)]
    near = peers[:3]
    greet_all(peers)
    width, length, half = MODEL_WIDTH, x_ref.shape[1], HEAD_SIZE // 2
    turn_rate = -2.0 * math.log(theta_base) / HEAD_SIZE
    heads, kv = QUERY_HEADS, KEY_VALUE_HEADS
    repeat = heads // kv
    scale = HEAD_SIZE**-0.5
    def block(ref, j):
        return ref.at[pl.ds(j * length, length)]

    cots[0:length, :] = cot_ref[...].astype(f32).T.astype(bf16)
    cot_copies = [
        remote(block(cots, 0), block(cots, j + 1), cs.at[j], cr.at[j], near[j]) for j in range(3)
    ]
    for copy in cot_copies:
        copy.start()


    copy_rows = 216

    def unroll(start, count):
        def step(i, _):
            at = start + i * copy_rows
            raw[pl.ds(pl.multiple_of(HEAD_ROWS + at, 8), copy_rows), :] = rows_at(lin, at, copy_rows)
            return 0

        lax.fori_loop(0, count // copy_rows, step, 0)

    @pl.when(group == 0)
    def _():
        load_qkv.wait()
        unroll(qkv_from, qkv_rows)
        load_out.wait()
        unroll(out_from_row, out_rows)
        load_end.wait()
        at = HEAD_ROWS + BLOCK_ROWS
        raw[at - 8 : at, :] = rows_at(lin_t, 0, 8)
        raw[at : at + 8, :] = rows_at(lin_t, 8, 8, EXTRA)

    @pl.when(group > 0)
    def _():
        whole.wait()
        unroll(0, BLOCK_ROWS)
        raw[pl.ds(HEAD_ROWS + BLOCK_ROWS, 8), :] = rows_at(lin, BLOCK_ROWS, 8, EXTRA)

    def joined(first, second, shift, cut):
        lane = lanes_of(first.shape[0])
        return jnp.where(lane < cut, pltpu.roll(first, shift, 1), pltpu.roll(second, shift, 1))

    tail = remote(tail_s, raw.at[pl.ds(0, HEAD_ROWS)], ts, tr, (wide, (group + 1) % groups))
    top = HEAD_ROWS + BLOCK_ROWS + 2

    @pl.when(group < groups - 1)
    def _():
        at = top - HEAD_ROWS
        tail_s[...] = joined(raw[at : at + 8, :], raw[at + 1 : at + 9, :], 96, 96)
        tail.start()

    def gain_copy(g):
        return remote(gain_s, gain_s, gns.at[g], gnr, (wide, g))

    @pl.when(group == groups - 1)
    def _():
        at = top - 9
        gain_s[...] = joined(raw[at : at + 16, :], raw[at + 1 : at + 17, :], 96, 96)
        for g in range(groups - 1):
            gain_copy(g).start()

    @pl.when(group > 0)
    def _():
        tail.wait_recv()

    def take(start, count, stride):
        return raw[pl.ds(start, count, stride), :]

    pairs = CHIP_ROWS // 2

    def put_joint(p, even, odd):
        pan_w[pl.ds(p % 6 * CHIP_ROWS, pairs, 2), :] = even
        pan_w[pl.ds(p % 6 * CHIP_ROWS + 1, pairs, 2), :] = odd
        joint_ref[pl.ds(pl.multiple_of(CHIP_ROWS * chip, 16), CHIP_ROWS), p * LANES : (p + 1) * LANES] = pan_w[
            p % 6 * CHIP_ROWS : (p % 6 + 1) * CHIP_ROWS, :
        ].astype(bf16)

    qkv_at = HEAD_ROWS + 1080 * chip
    out_at = HEAD_ROWS + 4320 + 648 * chip

    def qkv(k):
        return take(qkv_at + k, pairs, 15)

    def out(k):
        return take(out_at + k, pairs, 9)

    @pl.when((group == 0) & (core == 0))
    def _():
        for p in range(6):
            put_joint(p, qkv(p), joined(qkv(7 + p), qkv(8 + p), 64, 64))

    @pl.when((group == 0) & (core == 1))
    def _():
        put_joint(6, qkv(6), joined(qkv(13), qkv(14), 64, 64))
        lane = lanes_of(pairs)
        put_joint(
            7,
            jnp.where(lane < 64, qkv(7), pltpu.roll(out(0), 64, 1)),
            jnp.where(lane < 64, pltpu.roll(qkv(14), 64, 1), out(4)),
        )
        for k in range(4):
            put_joint(8 + k, joined(out(k), out(k + 1), 64, 64), out(5 + k))

    for g, back, shift in ((1, 3, 32), (2, 5, 64)):

        @pl.when(group == g)
        def _():
            for j in range(3):
                at = HEAD_ROWS - back + 12 * core + 3 * chip + j
                value = joined(take(at, HALF_WIDTH, 24), take(at + 1, HALF_WIDTH, 24), shift, shift)
                gu_ref[core, (g - 1) * HALF_WIDTH : g * HALF_WIDTH, j * LANES : (j + 1) * LANES] = value.astype(bf16)

    half_units = UNITS // 2

    @pl.when(group == 3)
    def _():
        rows = pl.ds(pl.multiple_of(half_units * core, 16), half_units)
        count = half_units // 2
        for p in range(5):
            at = HEAD_ROWS + 864 * wide + p
            even = joined(take(at - 7, count, 9), take(at - 6, count, 9), 96, 96)
            odd = joined(take(at - 3, count, 9), take(at - 2, count, 9), 32, 32)
            pan_w[pl.ds(p * half_units, count, 2), :] = even
            pan_w[pl.ds(p * half_units + 1, count, 2), :] = odd
            value = pan_w[p * half_units : (p + 1) * half_units, :].astype(bf16)
            if p < 4:
                down_ref[rows, p * LANES : (p + 1) * LANES] = value
            else:
                down_ref[rows, p * LANES : MODEL_WIDTH] = value[:, : MODEL_WIDTH - p * LANES]

    def attn_at(q, c, k):
        return joint_ref.at[
            pl.ds(pl.multiple_of(CHIP_ROWS * q + SUB * k, 16), SUB),
            pl.ds(pl.multiple_of(HALF_JOINT * c, LANES), HALF_JOINT),
        ]

    def piece(s, k):
        if s == 0:
            return attn_at(chip, core, k)
        if s < 3:
            step = HALF_WIDTH // SPLIT
            return gu_ref.at[core, pl.ds((s - 1) * HALF_WIDTH + k * step, step)]
        step = half_units // SPLIT
        return down_ref.at[pl.ds(pl.multiple_of(half_units * core + k * step, 16), step)]

    def pass_on(s, k, way):
        to = (wide, (group + way + groups) % groups)
        return remote(piece(s, k), piece(s, k), wzs.at[(way + 1) // 2, s, k], wzr.at[s, k], to)

    def sends(s):
        right = (group >= s) & (group < groups - 1)
        left = (group <= s) & (group > 0)
        return right, left

    def forward(s, k):
        right, left = sends(s)

        @pl.when(right)
        def _():
            pass_on(s, k, 1).start()

        @pl.when(left)
        def _():
            pass_on(s, k, -1).start()

    def give(s, k):
        return remote(piece(s, k), piece(s, k), es.at[s, k], er.at[s, k], (twin, group))

    for s in range(groups):

        @pl.when(group == s)
        def _():
            for k in range(SPLIT):
                if s == 0:
                    pass_on(s, k, 1).start()
                else:
                    pass_on(s, k, -1).start()
                    give(s, k).start()
                    if s == 2 and k < 2:
                        pass_on(s, k, 1).start()

    q_one, q_two = one // 2, two // 2
    q_far = 3 - chip

    def stage(n, k, q):
        peer = (one, two, two, twin, twin, twin, twin)[n]
        return remote(attn_at(q, core, k), attn_at(q, core, k), as_.at[n, k], ar.at[n, k], (peer, group))

    for k in range(SPLIT):

        @pl.when(group > 0)
        def _():
            pass_on(0, k, 1).wait_recv()
            forward(0, k)

        stage(0, k, chip).start()
        stage(1, k, chip).start()
        stage(3, k, chip).start()

    for s in range(1, groups - 1):

        @pl.when(group == s)
        def _():
            for k in range(2 if s == 2 else 0, SPLIT):
                pass_on(s, k, 1).start()

    def relay(s, g):
        @pl.when(group == g)
        def _():
            for k in range(SPLIT):
                pass_on(s, k, 1).wait_recv()
                forward(s, k)
                give(s, k).start()

    for s in (1, 2, 3):
        relay(s, s - 1)
    @pl.when(group < groups - 1)
    def _():
        gain_copy(0).wait_recv()

    gains = gain_s[...].astype(bf16).astype(f32)
    for k in range(4):
        gain_w[0:1, k * LANES : (k + 1) * LANES] = gains[k : k + 1]
    gain_w[0:1, 4 * LANES : MODEL_WIDTH] = gains[4:5, : MODEL_WIDTH - 4 * LANES]
    turned = pltpu.roll(gains, 64, 1)
    lane = lanes_of(1)
    for k in range(4):
        gain_w[1:2, k * LANES : (k + 1) * LANES] = jnp.where(lane < 64, turned[4 + k : 5 + k], turned[5 + k : 6 + k])
    gain_w[1:2, 4 * LANES : MODEL_WIDTH] = turned[8:9, : MODEL_WIDTH - 4 * LANES]

    gain_one, gain_two = gain_w[0:1, :], gain_w[1:2, :]
    x = x_ref[...].astype(f32).T
    inv_attn = lax.rsqrt(jnp.mean(x * x, axis=-1, keepdims=True) + norm_eps)
    normed_attn = x * inv_attn
    hidden_attn = (normed_attn * gain_one).astype(bf16)

    seg_row = jnp.broadcast_to(seg_ref[...].astype(f32), (length, length))
    rows = lax.broadcasted_iota(jnp.int32, (length, length), 0)
    columns = lax.broadcasted_iota(jnp.int32, (length, length), 1)
    allowed = (seg_row == seg_row.T) & (rows >= columns)
    positions = jnp.sum(jnp.where(allowed, 1.0, 0.0), axis=-1, keepdims=True) - 1.0
    angles = positions * jnp.exp(turn_rate * (lanes_of(1) % half).astype(f32))
    lane = lax.broadcasted_iota(jnp.int32, (length, LANES), 1)
    first = lane % HEAD_SIZE < half
    cosine, sine = jnp.cos(angles), jnp.sin(angles)
    sine = jnp.where(first, -sine, sine)

    def swap(u):
        return jnp.where(first, pltpu.roll(u, LANES - half, 1), pltpu.roll(u, half, 1))

    for k in range(SPLIT):
        stage(0, k, q_one).wait_recv()
        stage(2, k, q_one).start()
        stage(4, k, q_one).start()
        stage(1, k, q_two).wait_recv()
        stage(5, k, q_two).start()
    for s in (2, 3):
        relay(s, s - 2)
    for k in range(SPLIT):
        stage(2, k, q_far).wait_recv()
        stage(6, k, q_far).start()
    for s in (1, 2):
        relay(s, s + 1)
    for k in range(SPLIT):
        for n in range(3, 7):
            stage(n, k, chip).wait_recv()

    panels = 8
    turned_panels = (heads + kv) * HEAD_SIZE // LANES
    wide_qkv = panels * LANES
    for p in range(0, panels, 2):
        both = dot(hidden_attn, joint_ref[:, p * LANES : (p + 2) * LANES], 1, 0)
        for q in (p, p + 1):
            u = both[:, (q - p) * LANES : (q - p + 1) * LANES]
            if q < turned_panels:
                u = u * cosine + swap(u) * sine
            proj_s[:, q * LANES : (q + 1) * LANES] = u.astype(bf16)

    def slot(s):
        return proj_s[:, s * HEAD_SIZE : (s + 1) * HEAD_SIZE]

    mask = jnp.concatenate([allowed] * repeat, axis=0)
    saved = []
    for j in range(kv):
        queries = jnp.concatenate([slot(repeat * j + r) for r in range(repeat)], axis=0)
        keys, values = slot(heads + j), slot(heads + kv + j)
        scores = jnp.where(mask, dot(queries, keys, 1, 1) * scale, masked_value)
        peak = jnp.max(scores, axis=-1, keepdims=True)
        raised = jnp.exp(scores - peak)
        probs = raised * (1.0 / jnp.sum(raised, axis=-1, keepdims=True))
        probs_b = probs.astype(bf16)
        attended = dot(probs_b, values, 1, 0)
        for r in range(repeat):
            at = (repeat * j + r) * HEAD_SIZE
            att_s[:, at : at + HEAD_SIZE] = attended[r * length : (r + 1) * length].astype(bf16)
        saved.append((queries, keys, values, probs, probs_b))

    out_from = QKV // LANES * LANES
    shift = QKV - out_from
    w_out = joint_ref.at[:, out_from:JOINT]
    mid = x + dot(att_s[...], w_out[...], 1, 0)[:, shift:]
    inv_ffn = lax.rsqrt(jnp.mean(mid * mid, axis=-1, keepdims=True) + norm_eps)
    normed_ffn = mid * inv_ffn
    hids[0:length, :] = (normed_ffn * gain_two).astype(bf16)
    hid_copies = [
        remote(block(hids, 0), block(hids, j + 1), hs.at[j], hr.at[j], near[j]) for j in range(3)
    ]
    for copy in hid_copies:
        copy.start()
    mid_s[...] = mid

    relay(3, 0)
    relay(1, 3)
    for k in range(SPLIT):
        for s in range(1, groups):
            give(s, k).wait_recv()

    def feed(j):
        at = slice(j * length, (j + 1) * length)
        hidden, cotangent = hids[at, :], cots[at, :]
        gate, upper = dot(hidden, gu_ref[0], 1, 0), dot(hidden, gu_ref[1], 1, 0)
        d_act = dot(cotangent, down_ref[...], 1, 1)
        sigmoid = jax.nn.sigmoid(gate)
        activation = (gate * sigmoid * upper).astype(bf16)
        d_gate = (d_act * upper * sigmoid * (1.0 + gate * (1.0 - sigmoid))).astype(bf16)
        d_upper = (d_act * gate * sigmoid).astype(bf16)
        act_s[at, :], gate_s[at, :], up_s[at, :] = activation, d_gate, d_upper
        d_hidden = dot(d_gate, gu_ref[0], 1, 1) + dot(d_upper, gu_ref[1], 1, 1)
        return d_hidden, dot(activation, down_ref[...], 1, 0)

    def part_copy(n, j):
        return remote(part_s.at[n, j], part_r.at[n, j], ps.at[n, j], pr.at[n, j], near[j])

    d_hidden, out_own = feed(0)
    for j in range(3):
        cot_copies[j].wait_recv()
        hid_copies[j].wait_recv()
        d_part, out_part = feed(j + 1)
        part_s[0, j] = d_part.astype(bf16)
        part_copy(0, j).start()
        part_s[1, j] = out_part.astype(bf16)

    ggu_ref[0] = dot(hids[...], gate_s[...], 0, 0).astype(bf16)
    ggu_ref[1] = dot(hids[...], up_s[...], 0, 0).astype(bf16)
    gdn_ref[...] = dot(act_s[...], cots[...], 0, 0).astype(bf16)

    half_units = UNITS // 2
    other = 1 - core

    def half_cols(c):
        return pl.ds(pl.multiple_of(HALF_JOINT * c, LANES), HALF_JOINT)

    def half_rows(c):
        return pl.ds(pl.multiple_of(half_units * c, 16), half_units)

    def chip_rows(q):
        return pl.ds(pl.multiple_of(CHIP_ROWS * q, 16), CHIP_ROWS)

    trades = [
        remote(ggu_ref.at[other], core_g, sws.at[0], swr.at[0], (twin, group)),
        remote(gdn_ref.at[half_rows(other)], core_d, sws.at[1], swr.at[1], (twin, group)),
        remote(gj_ref.at[:, half_cols(other)], core_j, sws.at[2], swr.at[2], (twin, group)),
    ]
    for trade in trades[:2]:
        trade.start()
    def add_rows(count, step, total, mine, theirs):
        def body(i, _):
            at = pl.ds(pl.multiple_of(i * step, 16), step)
            total(at, mine(at).astype(f32) + theirs(at).astype(f32))
            return 0

        lax.fori_loop(0, count // step, body, 0)

    def into(ref):
        def put(at, value):
            ref[at, :] = value.astype(bf16)

        return put

    def z_source(g):
        if g == 0:
            return acc_j.at[chip_rows(chip)], z_j
        if g < 3:
            return acc_g.at[pl.ds((g - 1) * HALF_WIDTH, HALF_WIDTH)], z_g
        return acc_d, z_d

    def z_copy(g):
        source, target = z_source(g)
        place = (group - g + groups) % groups
        at = (place + groups - 1) % groups
        return remote(source, target.at[at], zs.at[g], zr.at[at], (wide, g))

    def z_send(g):
        @pl.when(group != g)
        def _():
            z_copy(g).start()

    def sub_rows(q, k):
        return pl.ds(pl.multiple_of(CHIP_ROWS * q + SUB * k, 16), SUB)

    def z_part(k, at):
        return remote(
            acc_j.at[sub_rows(chip, k)],
            z_j.at[at, pl.ds(SUB * k, SUB)],
            zjs.at[k],
            zjr.at[at, k],
            (wide, 0),
        )

    trades[0].wait_recv()
    add_rows(MODEL_WIDTH, 192, into(acc_g), lambda at: ggu_ref[core, at, :], lambda at: core_g[at, :])
    z_send(1)
    z_send(2)
    trades[1].wait_recv()
    half_from = half_units * core

    def down_mine(at):
        return gdn_ref[pl.ds(pl.multiple_of(half_from + at.start, 16), at.size), :]

    add_rows(half_units, 96, into(acc_d), down_mine, lambda at: core_d[at, :])
    z_send(3)
    for j in range(3):
        part_copy(0, j).wait_recv()
    for j in range(3):
        part_copy(1, j).start()
    for j in range(3):
        d_hidden = d_hidden + part_r[0, j].astype(f32)
    mid = mid_s[...]
    normed_ffn = mid * inv_ffn
    gain_ffn = jnp.sum(d_hidden * normed_ffn, axis=0, keepdims=True)
    d_mid = cots[0:length, :].astype(f32) + norm_back(d_hidden, normed_ffn, inv_ffn, gain_two)
    dmid_s[...] = jnp.zeros_like(dmid_s)
    dmid_s[:, shift:] = d_mid.astype(bf16)
    d_attended = dot(dmid_s[...], w_out[...], 1, 1)
    grad_out = dot(att_s[...], dmid_s[...], 0, 0)
    gj_ref[:, out_from + LANES : JOINT] = grad_out[:, LANES:].astype(bf16)
    edge = grad_out[:, :LANES]
    att_s[...] = d_attended.astype(bf16)

    dproj_s[...] = jnp.zeros_like(dproj_s)
    for j in range(kv):
        queries, keys, values, probs, probs_b = saved[j]
        d_att = jnp.concatenate(
            [
                att_s[:, (repeat * j + r) * HEAD_SIZE : (repeat * j + r + 1) * HEAD_SIZE]
                for r in range(repeat)
            ],
            axis=0,
        )
        d_probs = dot(d_att, values, 1, 1)
        row_total = jnp.sum(probs * d_probs, axis=-1, keepdims=True)
        d_scores = (probs * (d_probs - row_total) * scale).astype(bf16)
        d_queries = dot(d_scores, keys, 1, 0)
        for r in range(repeat):
            at = (repeat * j + r) * HEAD_SIZE
            dproj_s[:, at : at + HEAD_SIZE] = d_queries[r * length : (r + 1) * length]
        at = (heads + j) * HEAD_SIZE
        dproj_s[:, at : at + HEAD_SIZE] = dot(d_scores, queries, 0, 0)
        at = (heads + kv + j) * HEAD_SIZE
        dproj_s[:, at : at + HEAD_SIZE] = dot(probs_b, d_att, 0, 0)

    for p in range(panels):
        raw = dproj_s[:, p * LANES : (p + 1) * LANES]
        if p < turned_panels:
            raw = raw * cosine - swap(raw) * sine
        proj_s[:, p * LANES : (p + 1) * LANES] = raw.astype(bf16)
    d_hidden = dot(proj_s[...], joint_ref[:, :wide_qkv], 1, 1)
    grad_qkv = dot(hidden_attn, proj_s[...], 0, 0)
    gj_ref[:, :out_from] = grad_qkv[:, :out_from].astype(bf16)
    gj_ref[:, out_from:wide_qkv] = (grad_qkv[:, out_from:] + edge).astype(bf16)
    gain_attn = jnp.sum(d_hidden * normed_attn, axis=0, keepdims=True)
    din_ref[...] = (d_mid + norm_back(d_hidden, normed_attn, inv_attn, gain_one)).T.astype(bf16)
    both = jnp.concatenate([gain_attn, gain_ffn], axis=1)
    note[0, 0:16, :] = jnp.zeros((16, LANES), f32)
    for k in range(2 * width // LANES):
        note[0, k : k + 1, :] = both[:, k * LANES : (k + 1) * LANES].astype(bf16).astype(f32)

    trades[2].start()
    trades[2].wait_recv()

    add_rows(MODEL_WIDTH, 96, into(acc_j), lambda at: gj_ref[at, half_cols(core)], lambda at: core_j[at, :])

    def rs_copy(i, k):
        q = (q_one, q_far)[i]
        return remote(
            acc_j.at[sub_rows(q, k)],
            rs_one.at[i, pl.ds(SUB * k, SUB)],
            r1s.at[i, k],
            r1r.at[i, k],
            (one, group),
        )

    def rs_last(k):
        return remote(
            acc_j.at[sub_rows(q_two, k)], rs_two.at[pl.ds(SUB * k, SUB)], r2s.at[k], r2r.at[k], (two, group)
        )

    for i in (1, 0):
        for k in range(SPLIT):
            rs_copy(i, k).start()
    outputs = mid + out_own
    for j in range(3):
        part_copy(1, j).wait_recv()
        outputs = outputs + part_r[1, j].astype(f32)
    out_ref[...] = outputs.T.astype(bf16)

    def add_piece(q, k, theirs):
        at = sub_rows(q, k)
        acc_j[at, :] = (acc_j[at, :].astype(f32) + theirs[SUB * k : SUB * (k + 1), :].astype(f32)).astype(bf16)

    for k in range(SPLIT):
        rs_copy(1, k).wait_recv()
        add_piece(q_two, k, rs_one.at[1])
        rs_last(k).start()
    for k in range(SPLIT):
        rs_copy(0, k).wait_recv()
        add_piece(chip, k, rs_one.at[0])
        rs_last(k).wait_recv()
        add_piece(chip, k, rs_two)

        @pl.when(group > 0)
        def _():
            z_part(k, group - 1).start()

    def squares(value):
        return jnp.sum((value * value).reshape(-1, 8, LANES), axis=0)

    def z_add(g, i, step, rows, widths):
        source, target = z_source(g)
        at = pl.ds(i * step, step)
        value = source[at, :].astype(f32)
        for d in range(groups - 1):
            value = value + target[d, at, :].astype(f32)
        value = value.astype(bf16)
        total = jnp.zeros((8, LANES), f32)
        for p in range(widths // LANES):
            part = value[:, p * LANES : (p + 1) * LANES]
            place = i * PART_ROWS + p * step if g == 0 else p * rows + i * step
            ag[wide, place : place + step, :] = part
            total = total + squares(part.astype(f32))
        if widths % LANES:
            part = value[:, widths // LANES * LANES :]
            core_d[at, 0 : LANES // 2] = part
            part = part.astype(f32)
            part = jnp.sum((part * part).reshape(-1, 8, LANES // 2), axis=0)
            total = total + jnp.concatenate([part, jnp.zeros_like(part)], axis=1)
        return total

    def z_total(g, rows, widths):
        source, target = z_source(g)
        for at in range(groups - 1):
            remote(source, target.at[at], zs.at[g], zr.at[at], (wide, g)).wait_recv()
        step = 48
        total = jnp.zeros((8, LANES), f32)
        for i in range(rows // step):
            total = total + z_add(g, i, step, rows, widths)
        note[0, 16:24, :] = total
        if widths % LANES:
            n, last = rows // 2, widths // LANES * rows
            both = [core_d[0:n, 0 : LANES // 2], core_d[n:rows, 0 : LANES // 2]]
            ag[wide, last : last + n, :] = jnp.concatenate(both, axis=1)

    def note_copy(n):
        if n < 3:
            return remote(note.at[0], note.at[n + 4], ns.at[n], nr.at[n], near[n])
        return remote(note.at[1], note.at[2], ns.at[3], nr.at[3], (twin, group))

    def ag_copy(n, k):
        peer = (one, two, two, twin, twin, twin, twin)[n]
        q = (chip, chip, q_one, chip, q_one, q_two, q_far)[n]
        here = ag.at[2 * q + core, pl.ds(PART_ROWS * k, PART_ROWS)]
        return remote(here, here, ags.at[n, k], agr.at[n, k], (peer, group))

    for tick in range(SPLIT + 2):
        k = tick
        if k < SPLIT:

            @pl.when(group == 0)
            def _():
                for at in range(groups - 1):
                    z_part(k, at).wait_recv()
                total = z_add(0, k, SUB, CHIP_ROWS, HALF_JOINT)
                note[0, 16:24, :] = total if k == 0 else note[0, 16:24, :] + total

            if k == 0:
                for g, rows, widths in ((1, HALF_WIDTH, UNITS), (2, HALF_WIDTH, UNITS), (3, half_units, MODEL_WIDTH)):

                    @pl.when(group == g)
                    def _():
                        z_total(g, rows, widths)

            for n in (0, 1, 3):
                ag_copy(n, k).start()
            if k == SPLIT - 1:
                for n in range(3):
                    note_copy(n).start()
        k = tick - 1
        if 0 <= k < SPLIT:
            ag_copy(0, k).wait_recv()
            ag_copy(2, k).start()
            ag_copy(4, k).start()
            ag_copy(1, k).wait_recv()
            ag_copy(5, k).start()
        k = tick - 2
        if 0 <= k < SPLIT:
            if k == SPLIT - 1:
                for n in range(3):
                    note_copy(n).wait_recv()
                note[1] = (note[0] + note[4]) + (note[5] + note[6])
                note_copy(3).start()
            ag_copy(2, k).wait_recv()
            ag_copy(6, k).start()
    note_copy(3).wait_recv()
    note[3] = note[1] + note[2]
    note_z[pl.ds(group, 1)] = note[3:4]

    def note_far(d):
        return remote(
            note.at[3], note_z.at[group], nzs.at[d - 1], nzr.at[d - 1], (wide, (group + d) % groups)
        )

    for d in range(1, groups):
        note_far(d).start()

    pairs = CHIP_ROWS // 2
    lane_pairs = lanes_of(pairs)

    def halves(first, second):
        lane = lanes_of(first.shape[0])
        return jnp.where(lane < 64, pltpu.roll(first, 64, 1), pltpu.roll(second, 64, 1))

    def lay_joint(q):
        for p in range(12):
            for k in range(SPLIT):
                at, to = k * PART_ROWS + p % 6 * SUB, p * CHIP_ROWS + k * SUB
                pan[to : to + SUB, :] = ag[2 * q + p // 6, at : at + SUB, :].astype(f32)

        def even(p):
            return pan[pl.ds(p * CHIP_ROWS, pairs, 2), :]

        def odd(p):
            return pan[pl.ds(p * CHIP_ROWS + 1, pairs, 2), :]

        def put_qkv(k, value):
            flat[pl.ds(1080 * q + k, pairs, 15), :] = value

        def put_out(k, value):
            flat[pl.ds(4320 + 648 * q + k, pairs, 9), :] = value

        for p in range(7):
            put_qkv(p, even(p))
            put_qkv(8 + p, halves(odd(p), odd(p + 1)))
        put_qkv(7, jnp.where(lane_pairs < 64, even(7), pltpu.roll(odd(0), 64, 1)))
        for k in range(4):
            put_out(k, halves(even(7 + k), even(8 + k)))
            put_out(5 + k, odd(8 + k))
        put_out(4, jnp.where(lane_pairs < 64, pltpu.roll(even(11), 64, 1), odd(7)))

    def lay_gateup(q):
        for c in range(2):
            for j in range(3):
                value = ag[2 * q + c, j * HALF_WIDTH : (j + 1) * HALF_WIDTH, :].astype(f32)
                flat[pl.ds(12 * c + 3 * q + j, HALF_WIDTH, 24), :] = value

    def lay_down(q):
        n = half_units
        for c in range(2):
            w = 2 * q + c
            pan[0 : 4 * n, :] = ag[w, 0 : 4 * n, :].astype(f32)
            packed = ag[w, 4 * n : 4 * n + n // 2, :].astype(f32)
            pan[4 * n : 4 * n + n // 2, :] = packed
            pan[4 * n + n // 2 : 5 * n, :] = pltpu.roll(packed, 64, 1)

            def even(p):
                return pan[pl.ds(p * n, n // 2, 2), :]

            def odd(p):
                return pan[pl.ds(p * n + 1, n // 2, 2), :]

            def put(k, value):
                flat[pl.ds(864 * w + k, n // 2, 9), :] = value

            for p in range(4):
                put(p, even(p))
                put(5 + p, halves(odd(p), odd(p + 1)))
            put(4, jnp.where(lanes_of(n // 2) < 64, even(4), pltpu.roll(odd(0), 64, 1)))

    def lay(q):
        @pl.when(group == 0)
        def _():
            lay_joint(q)

        @pl.when((group == 1) | (group == 2))
        def _():
            lay_gateup(q)

        @pl.when(group == 3)
        def _():
            lay_down(q)

    for q, ends in ((chip, (3,)), (q_two, (4,)), (q_one, (5,)), (q_far, (6,))):
        for n in ends:
            for k in range(SPLIT):
                ag_copy(n, k).wait_recv()
        lay(q)

    head = remote(
        flat.at[pl.ds(0, HEAD_ROWS)],
        flat.at[pl.ds(BLOCK_ROWS, HEAD_ROWS)],
        hds,
        hdr,
        (wide, (group + groups - 1) % groups),
    )

    @pl.when(group > 0)
    def _():
        head.start()

    for d in range(1, groups):
        note_far(d).wait_recv()
    total = note_z[0]
    for d in range(1, groups):
        total = total + note_z[d]
    gains = total[:16]
    square = total[16:24] + squares(gains)
    square = jnp.sum(jnp.sum(square, axis=-1, keepdims=True), axis=0, keepdims=True)
    clip = jnp.minimum(jnp.float32(1.0), max_norm * lax.rsqrt(square))

    @pl.when(group == groups - 1)
    def _():
        flat[pl.ds(BLOCK_ROWS, 16), :] = gains

    clip_ref[...] = jnp.broadcast_to(clip, clip_ref.shape)

    @pl.when(group < groups - 1)
    def _():
        head.wait_recv()

    for k in range(SPLIT):
        for s in range(1, groups):
            give(s, k).wait_send()
        for n in range(7):
            stage(n, k, chip).wait_send()
    for s in range(groups):
        right, left = sends(s)
        for k in range(SPLIT):

            @pl.when(right)
            def _():
                pass_on(s, k, 1).wait_send()

            @pl.when(left)
            def _():
                pass_on(s, k, -1).wait_send()

    @pl.when(group < groups - 1)
    def _():
        tail.wait_send()

    @pl.when(group == groups - 1)
    def _():
        for g in range(groups - 1):
            gain_copy(g).wait_send()

    for j in range(3):
        cot_copies[j].wait_send()
        hid_copies[j].wait_send()
        part_copy(0, j).wait_send()
        part_copy(1, j).wait_send()
    for trade in trades:
        trade.wait_send()
    for k in range(SPLIT):
        for i in range(2):
            rs_copy(i, k).wait_send()
        rs_last(k).wait_send()
        for n in range(7):
            ag_copy(n, k).wait_send()

        @pl.when(group > 0)
        def _():
            z_part(k, group - 1).wait_send()

    for g in range(1, groups):

        @pl.when(group != g)
        def _():
            z_copy(g).wait_send()

    for n in range(4):
        note_copy(n).wait_send()
    for d in range(1, groups):
        note_far(d).wait_send()

    @pl.when(group > 0)
    def _():
        head.wait_send()


def row_step(inputs, segment_row, cotangent, params, groups):
    length = inputs.shape[0]
    dma = pltpu.SemaphoreType.DMA
    f32, bf16 = jnp.float32, jnp.bfloat16
    full = (length, MODEL_WIDTH)
    panel_lanes = 8 * LANES
    four = (CHIPS * length, MODEL_WIDTH)
    units = (CHIPS * length, UNITS)
    half_units = UNITS // 2
    z = groups - 1
    flipped_row = jax.ShapeDtypeStruct(full[::-1], bf16)
    joint = pltpu.VMEM((MODEL_WIDTH, JOINT), bf16)
    gateup = pltpu.VMEM((2, MODEL_WIDTH, UNITS), bf16)
    down = pltpu.VMEM((UNITS, MODEL_WIDTH), bf16)
    cut_joint = pltpu.VMEM((MODEL_WIDTH, HALF_JOINT), bf16)
    cut_gateup = pltpu.VMEM((MODEL_WIDTH, UNITS), bf16)
    cut_down = pltpu.VMEM((half_units, MODEL_WIDTH), bf16)
    return pl.pallas_call(
        functools.partial(row_kernel, groups),
        out_shape=(
            flipped_row,
            flipped_row,
            jax.ShapeDtypeStruct((BLOCK_ROWS + 24, LANES), f32),
            jax.ShapeDtypeStruct((8, LANES), f32),
        ),
        in_specs=vmem_specs(3) + [pl.BlockSpec(memory_space=pl.ANY)],
        out_specs=tuple(vmem_specs(4)),
        scratch_shapes=[
            joint, gateup, down,
            pltpu.VMEM((2, MODEL_WIDTH), f32),
            pltpu.VMEM((HEAD_ROWS + BLOCK_ROWS + 24, LANES), f32),
            pltpu.VMEM(params.shape, f32),
            pltpu.VMEM((8 * LANES + EXTRA,), f32),
            pltpu.VMEM((8, LANES), f32),
            pltpu.VMEM((16, LANES), f32),
            pltpu.VMEM((5 * half_units, LANES), f32),
            pltpu.VMEM((length, panel_lanes), bf16),
            pltpu.VMEM(full, bf16),
            pltpu.VMEM(full, f32),
            pltpu.VMEM((length, JOINT - QKV // LANES * LANES), bf16),
            pltpu.VMEM((length, panel_lanes), f32),
            pltpu.VMEM(four, bf16),
            pltpu.VMEM(four, bf16),
            pltpu.VMEM(units, bf16),
            pltpu.VMEM(units, bf16),
            pltpu.VMEM(units, bf16),
            pltpu.VMEM((2, 3) + full, bf16),
            pltpu.VMEM((2, 3) + full, bf16),
            joint, gateup, down,
            cut_joint, cut_gateup, cut_down,
            cut_joint, cut_gateup, cut_down,
            pltpu.VMEM((2, CHIP_ROWS, HALF_JOINT), bf16),
            pltpu.VMEM((CHIP_ROWS, HALF_JOINT), bf16),
            pltpu.VMEM((z, CHIP_ROWS, HALF_JOINT), bf16),
            pltpu.VMEM((z, HALF_WIDTH, UNITS), bf16),
            pltpu.VMEM((z, half_units, MODEL_WIDTH), bf16),
            pltpu.VMEM((8, PIECE_ROWS, LANES), bf16),
            pltpu.VMEM((7, 24, LANES), f32),
            pltpu.VMEM((groups, 24, LANES), f32),
            pltpu.VMEM((12 * CHIP_ROWS, LANES), f32),
            dma((4,)), dma, dma, dma((z,)), dma,
            dma((2, groups, SPLIT)), dma((groups, SPLIT)),
            dma((7, SPLIT)), dma((7, SPLIT)),
            dma((groups, SPLIT)), dma((groups, SPLIT)),
            dma((3,)), dma((3,)), dma((3,)), dma((3,)), dma((2, 3)), dma((2, 3)),
            dma((3,)), dma((3,)), dma((2, SPLIT)), dma((2, SPLIT)), dma((SPLIT,)), dma((SPLIT,)),
            dma((groups,)), dma((z,)), dma((SPLIT,)), dma((z, SPLIT)), dma((7, SPLIT)), dma((7, SPLIT)), dma((4,)), dma((4,)), dma((z,)), dma((z,)),
            dma, dma,
        ],
        compiler_params=pltpu.CompilerParams(
            collective_id=4, has_side_effects=True, vmem_limit_bytes=ROW_VMEM
        ),
        name="row_step",
    )(inputs.T, segment_row[None], cotangent.T, params)


def adam_kernel(
    groups, flat_in, clip_ref, par_in, one_in, two_in, layer_out, layer_din,
    grads_out, params_out, one_out, two_out, out_ref, din_ref,
    flat, grad_b, par_b, one_b, two_b, grad_t, par_t, one_t, two_t,
    flat_sem, load_sem, end_sem, out_sem, tout_sem, layer_sem,
):
    group = lax.axis_index("group")
    sources = (par_in, one_in, two_in)
    banks = (par_b, one_b, two_b)
    ahead = 24

    def flat_load(i):
        rows = pl.ds(pl.multiple_of(i * ADAM_ROWS + ahead, 8), ADAM_ROWS)
        return pltpu.make_async_copy(flat_in.at[rows], flat.at[rows], flat_sem.at[i])

    def bank_load(i, j):
        at = pl.multiple_of(i * ADAM_ROWS, 8)
        return pltpu.make_async_copy(
            sources[j].at[pl.ds(pl.multiple_of(at * LANES, 1024), ADAM_ROWS * LANES)],
            banks[j].at[pl.ds(at, ADAM_ROWS)].reshape(ADAM_ROWS * LANES),
            load_sem.at[i, j],
        )

    first = pltpu.make_async_copy(
        flat_in.at[pl.ds(0, ahead)], flat.at[pl.ds(0, ahead)], flat_sem.at[ADAM_CHUNKS]
    )
    first.start()
    for i in range(ADAM_CHUNKS):
        flat_load(i).start()
        for j in range(3):
            bank_load(i, j).start()
    end_loads = [
        pltpu.make_async_copy(source.at[pl.ds(BLOCK, EXTRA)], end, end_sem.at[j])
        for j, (source, end) in enumerate(zip(sources, (par_t, one_t, two_t)))
    ]
    copies = end_loads + [
        pltpu.make_async_copy(layer_out, out_ref, layer_sem.at[0]),
        pltpu.make_async_copy(layer_din, din_ref, layer_sem.at[1]),
    ]
    for copy in copies:
        copy.start()

    def update(g, at, count, kept=0):
        lane = lanes_of(count)
        back, cut = 9 * g // 4, LANES - 32 * g
        grads = flat[pl.ds(at + back, count), :]
        if g:
            second = flat[pl.ds(at + back + 1, count), :]
            grads = jnp.where(lane < cut, pltpu.roll(grads, cut, 1), pltpu.roll(second, cut, 1))
        if kept:
            p, m1, m2 = [rows_at(ref, 0, count, kept) for ref in (par_t, one_t, two_t)]
        else:
            p, m1, m2 = [ref[pl.ds(at, count), :] for ref in banks]
        clipped = grads * clip_ref[0:1, :]
        m1 = beta_one * m1 + (1.0 - beta_one) * clipped
        m2 = beta_two * m2 + (1.0 - beta_two) * clipped * clipped
        step_size = m1 * (1.0 / bias_one) / (jnp.sqrt(m2 * (1.0 / bias_two)) + adam_eps)
        if g == groups - 1:
            limit = BLOCK + EXTRA - 2 * MODEL_WIDTH
            place = (at + lax.broadcasted_iota(jnp.int32, (count, LANES), 0)) * LANES + lane
            decay = jnp.where(place < limit, decay_rate, 0.0)
        else:
            decay = decay_rate
        return grads, p - learn_rate * (step_size + decay * p), m1, m2

    outs = (grads_out, params_out, one_out, two_out)
    stores = (grad_b, par_b, one_b, two_b)
    ends = (grad_t, par_t, one_t, two_t)

    def out_copy(i, j):
        at = pl.multiple_of(i * ADAM_ROWS, 8)
        return pltpu.make_async_copy(
            stores[j].at[pl.ds(at, ADAM_ROWS)].reshape(ADAM_ROWS * LANES),
            outs[j].at[pl.ds(pl.multiple_of(at * LANES, 1024), ADAM_ROWS * LANES)],
            out_sem.at[i, j],
        )

    def tail_copy(j):
        return pltpu.make_async_copy(
            ends[j], outs[j].at[pl.ds(BLOCK, EXTRA)], tout_sem.at[j]
        )

    first.wait()
    for copy in end_loads:
        copy.wait()
    for g in range(groups):

        @pl.when(group == g)
        def _():
            def body(i, _):
                at = pl.multiple_of(i * ADAM_ROWS, 8)
                flat_load(i).wait()
                for j in range(3):
                    bank_load(i, j).wait()
                for store, value in zip(stores, update(g, at, ADAM_ROWS)):
                    store[pl.ds(at, ADAM_ROWS), :] = value
                for j in range(4):
                    out_copy(i, j).start()
                return 0

            lax.fori_loop(0, ADAM_CHUNKS, body, 0)
            for end, value in zip(ends, update(g, BLOCK_ROWS, 8, EXTRA)):
                end[...] = value.reshape(8 * LANES)[:EXTRA]

    for j in range(4):
        tail_copy(j).start()
    for i in range(ADAM_CHUNKS):
        for j in range(4):
            out_copy(i, j).wait()
    for j in range(4):
        tail_copy(j).wait()
    for copy in copies[3:]:
        copy.wait()


def adam(settled, states, outputs, d_inputs, groups):
    dma = pltpu.SemaphoreType.DMA
    f32 = jnp.float32
    anywhere = pl.BlockSpec(memory_space=pl.ANY)
    bank = pltpu.VMEM((BLOCK_ROWS, LANES), f32)
    end = pltpu.VMEM((EXTRA,), f32)
    return pl.pallas_call(
        functools.partial(adam_kernel, groups),
        out_shape=(jax.ShapeDtypeStruct(states[0].shape, f32),) * 4
        + tuple(jax.ShapeDtypeStruct(a.shape, a.dtype) for a in (outputs, d_inputs)),
        in_specs=[anywhere] + vmem_specs(1) + [anywhere] * 5,
        out_specs=(anywhere,) * 6,
        scratch_shapes=[pltpu.VMEM((BLOCK_ROWS + 24, LANES), f32)]
        + [bank] * 4
        + [end] * 4
        + [dma((ADAM_CHUNKS + 1,)), dma((ADAM_CHUNKS, 3)), dma((3,))]
        + [dma((ADAM_CHUNKS, 4)), dma((4,)), dma((2,))],
        compiler_params=pltpu.CompilerParams(vmem_limit_bytes=ADAM_VMEM),
        name="adam",
    )(*settled, *states, outputs, d_inputs)


def on_device(inputs, segments, cotangent, params, moment_one, moment_two):
    groups = lax.axis_size("group")
    wides = lax.axis_size("wide")
    group = lax.axis_index("group")
    count = wides.bit_length() - 1
    share_len = params.shape[0]
    gain_len = 2 * MODEL_WIDTH
    extra = gain_len // groups
    block_len = share_len - extra
    if groups == 4 and wides == 2 * CHIPS and block_len == BLOCK and inputs.shape[0] == 1:
        outputs, d_inputs, *settled = row_step(
            inputs[0], segments[0], cotangent[0], params, groups
        )
        *updated, outputs, d_inputs = adam(
            settled, (params, moment_one, moment_two), outputs, d_inputs, groups
        )
        return (outputs.T[None], d_inputs.T[None], *updated)
    block_rows = block_len // LANES
    piece_rows = -(-block_rows // wides)
    chunks = 6 if piece_rows % 96 == 0 else 2
    piece_rows = -(-piece_rows // (16 * chunks)) * 16 * chunks
    padding = piece_rows * wides - block_rows
    lead = (2,) * count

    def to_pieces(rows):
        rows = rows.reshape(-1, block_rows, LANES)
        if padding:
            rows = jnp.pad(rows, ((0, 0), (0, padding), (0, 0)))
        return rows.reshape((-1,) + lead + (piece_rows, LANES))

    def from_pieces(pieces):
        rows = pieces.reshape(-1, piece_rows * wides, LANES)[:, :block_rows]
        return rows.reshape(-1, LANES)

    rounded = params.astype(jnp.bfloat16)
    tail = jnp.pad(rounded[share_len - gain_len :], (0, 16 * LANES - gain_len)).reshape(16, LANES)
    tails = gather_tails(tail, groups, 0).reshape(groups, -1)[:, :gain_len]
    before = lax.dynamic_index_in_dim(tails, (group + groups - 1) % groups, keepdims=False)
    joined = jnp.concatenate([before, rounded])
    block = lax.dynamic_slice(joined, (gain_len - extra * group,), (block_len,))
    flat_gains = tails[groups - 1]
    gathered = gather_blocks(to_pieces(block)[0], groups, count, chunks)
    weights = unpack(from_pieces(gathered), flat_gains)
    outputs, d_inputs, main, gains = layer_row(inputs[0], segments[0], cotangent[0], weights)
    gains = gains.astype(jnp.bfloat16).astype(jnp.float32)
    gains = jnp.pad(gains, (0, 16 * LANES - gain_len)).reshape(16, LANES)
    summed_block, head, gains, square = sum_blocks(to_pieces(main), gains, groups, count, chunks)
    gains = gains.reshape(-1)[:gain_len].astype(jnp.bfloat16)
    flat_block = from_pieces(summed_block).reshape(-1)
    head = head.reshape(-1)[:gain_len]
    head = jnp.where(group == groups - 1, gains, head)
    joined = jnp.concatenate([flat_block, head])
    summed = lax.dynamic_slice(joined, (extra * group,), (share_len,)).astype(jnp.float32)
    clip_factor = square[0, 0]
    flat_index = group * share_len + jnp.arange(share_len, dtype=jnp.int32)
    decay_mask = flat_index < share_len * groups - gain_len
    new_params, new_moment_one, new_moment_two = adam_update(
        summed, clip_factor, params, moment_one, moment_two, decay_mask
    )
    return (outputs[None], d_inputs[None], summed, new_params, new_moment_one, new_moment_two)


def solution(mesh):
    return jax.shard_map(
        on_device,
        mesh=mesh,
        in_specs=(
            P(("wide", "group"), None, None),
            P(("wide", "group"), None),
            P(("wide", "group"), None, None),
            P("group"),
            P("group"),
            P("group"),
        ),
        out_specs=(
            P(("wide", "group"), None, None),
            P(("wide", "group"), None, None),
            P("group"),
            P("group"),
            P("group"),
            P("group"),
        ),
        check_vma=False,
    )
```
